128 devices in a mesh: px: 16 (over y, x), py: 8 (over z, core).
Axes of the slice: x: 4, y: 4, z: 4, core: 2. Of those that a mesh axis runs over, the one named last changes fastest.
Arguments:
- node_latents: bfloat16 [256, 160, 512], P('px', 'py'), may hold values from -6 to 6
- fine_edges: bfloat16 [256, 160, 6, 512], P('px', 'py'), may hold values from -6 to 6
- long_edges: bfloat16 [20480, 512], P(('px', 'py')), may hold values from -6 to 6
- neighbours: int32 [256, 160, 6], P('px', 'py'), may hold values from 0 to 7, as said below
- coarse_slots: int32 [2560], P(('px', 'py')), may hold values from 0 to 319, as said below
- long_senders: int32 [20480], P(('px', 'py')), may hold values from 0 to 2559
- long_receivers: int32 [20480], P(('px', 'py')), may hold values from 0 to 2559, as said below
- edge_inner: bfloat16 [2, 1536, 512], replicated, may hold values from -0.15625 to 0.15625
- edge_outer: bfloat16 [2, 512, 512], replicated, may hold values from -0.25 to 0.25
- edge_gain: float32 [2, 512], replicated, may hold values from 0.5 to 1.5
- node_inner: bfloat16 [2, 1024, 512], replicated, may hold values from -0.1875 to 0.1875
- node_outer: bfloat16 [2, 512, 512], replicated, may hold values from -0.25 to 0.25
- node_gain: float32 [2, 512], replicated, may hold values from 0.5 to 1.5
Outputs:
- new_nodes: bfloat16 [256, 160, 512], P('px', 'py')
- new_fine: bfloat16 [256, 160, 6, 512], P('px', 'py')
- new_long: bfloat16 [20480, 512], P(('px', 'py'))
The draws below stay inside these ranges and needn't reach their ends.
Inputs may be any that keep to these rules, and one draw needn't show every extreme that they name: `neighbours`: the 6 codes of one node are different. `coarse_slots`: the 20 entries of one device's block are different. `long_receivers`: among the 160 long edges of one device, at most 3 have receivers c with the same c // 20, and on every device some such group has exactly 3.
All inputs are finite; a program needn't handle non-finite values.
Results may differ from the reference program's by a relative error of at most 0.0095.
Values may be sent and summed in bfloat16 or wider, within the bound.
No kernel may reach another device: no remote copies, remote signals or barrier semaphores. Data moves between devices by JAX's collectives and lax.ppermute only.
A program may use at most 128 MiB of HBM per device.

```python
import jax
import jax.numpy as jnp
from jax import lax

D = 512
HID = 512
K = 6
LAYERS = 2
PR = 16
PC = 20
CO_DEV = 20
LE_DEV = 160
GR = 256
GC = 160
COARSE = 2560
LONG = 20480
CAP = 3
N_PY = 8


def draw_neighbours(key, part):
    scores = jax.random.randint(key, (GR, GC, 8), 0, 1 << 20) * 8 + jnp.arange(8, dtype=jnp.int32)
    ranking = jnp.argsort(scores, axis=-1, stable=True)
    return ranking[..., :K].astype(jnp.int32)


def draw_coarse_slots(key, part):
    patch_cells = PR * PC
    blocks = COARSE // CO_DEV
    scores = jax.random.randint(key, (blocks, patch_cells), 0, (1 << 30) // patch_cells) * patch_cells + jnp.arange(patch_cells, dtype=jnp.int32)
    ranking = jnp.argsort(scores, axis=-1, stable=True)
    return ranking[:, :CO_DEV].reshape(COARSE).astype(jnp.int32)


def draw_long_receivers(key, part):
    blocks = LONG // LE_DEV
    slot_count = blocks * CAP
    first_key, second_key, third_key, fourth_key = jax.random.split(key, 4)
    favoured = jax.random.randint(first_key, (blocks, 1), 0, blocks)
    positions = jnp.arange(slot_count, dtype=jnp.int32)
    owner_of = positions // CAP
    noise = jax.random.randint(second_key, (blocks, slot_count), 0, (1 << 30) // slot_count)
    scores = jnp.where(owner_of[None, :] == favoured, positions[None, :], (noise + 1) * slot_count + positions[None, :])
    chosen = jnp.argsort(scores, axis=-1, stable=True)[:, :LE_DEV].astype(jnp.int32)
    owners = chosen // CAP
    within = jax.random.randint(third_key, (blocks, LE_DEV), 0, CO_DEV)
    mixing = jax.random.randint(fourth_key, (blocks, LE_DEV), 0, 1 << 20) * LE_DEV + jnp.arange(LE_DEV, dtype=jnp.int32)
    shuffle = jnp.argsort(mixing, axis=-1, stable=True)
    receivers = jnp.take_along_axis(owners * CO_DEV + within, shuffle, axis=1)
    return receivers.reshape(LONG).astype(jnp.int32)


def place_ends(drawn, key, least, top_value):
    longest = drawn.shape.index(max(drawn.shape))
    spots = []
    for shift in (0, 1):
        where = [jax.random.randint(jax.random.fold_in(key, axis), (), 0, length) for axis, length in enumerate(drawn.shape)]
        where[longest] = (where[longest] + shift) % drawn.shape[longest]
        spots.append(tuple(where))
    return drawn.at[spots[0]].set(least).at[spots[1]].set(top_value)


def shard_levels(stream_key, dims, pieces, smallest, largest):
    def one(dim, blocks):
        draws = jax.random.uniform(jax.random.fold_in(jax.random.fold_in(stream_key, 6), dim), (blocks,), jnp.float32, smallest / len(pieces), largest / len(pieces))
        return jnp.repeat(jnp.exp(draws), dims[dim] // blocks).reshape((-1,) + (1,) * (len(dims) - dim - 1))

    loudness = one(*pieces[0])
    for cut in pieces[1:]:
        loudness = loudness * one(*cut)
    return loudness


def normal_values(key, shape, scale, bound, cuts=(), held_as=jnp.bfloat16):
    entries = jax.random.normal(key, shape, jnp.float32) * scale
    if len(cuts) > 0:
        entries = shard_levels(key, shape, cuts, -0.22, 0.18) * entries
    return jnp.clip(entries, min=-bound, max=bound).astype(held_as)


def setup_inputs(seed: int = 0) -> dict:
    streams_of = jax.random.split(jax.random.key(seed), 14)
    return {
        "node_latents": normal_values(streams_of[0], (GR, GC, D), 1.0, 6.0, ((0, 16), (1, 8))),
        "fine_edges": normal_values(streams_of[1], (GR, GC, K, D), 1.0, 6.0, ((0, 16), (1, 8))),
        "long_edges": normal_values(streams_of[2], (LONG, D), 1.0, 6.0, ((0, 128),)),
        "neighbours": draw_neighbours(jax.random.fold_in(streams_of[13], 71), 0),
        "coarse_slots": draw_coarse_slots(jax.random.fold_in(streams_of[13], 71), 0),
        "long_senders": place_ends(jax.random.randint(streams_of[5], (LONG,), 0, COARSE), jax.random.fold_in(streams_of[5], 1), 0, COARSE - 1).astype(jnp.int32),
        "long_receivers": draw_long_receivers(jax.random.fold_in(streams_of[13], 71), 0),
        "edge_inner": normal_values(streams_of[7], (LAYERS, 3 * D, HID), (3 * D) ** -0.5, 0.15625),
        "edge_outer": normal_values(streams_of[8], (LAYERS, HID, D), HID ** -0.5, 0.25),
        "edge_gain": jnp.clip(1.0 + 0.1 * jax.random.normal(streams_of[9], (LAYERS, D), jnp.float32), 0.5, 1.5),
        "node_inner": normal_values(streams_of[10], (LAYERS, 2 * D, HID), (2 * D) ** -0.5, 0.1875),
        "node_outer": normal_values(streams_of[11], (LAYERS, HID, D), HID ** -0.5, 0.25),
        "node_gain": jnp.clip(1.0 + 0.1 * jax.random.normal(streams_of[12], (LAYERS, D), jnp.float32), 0.5, 1.5),
    }


EPSILON = 1e-05

def layer_norm(values, gains):
    center = values - lax.optimization_barrier(jnp.mean(values, axis=-1, keepdims=True))
    spread = lax.optimization_barrier(jnp.mean(center * center, axis=-1, keepdims=True))
    return center * lax.rsqrt(spread + EPSILON) * gains

def apply_mlp(inputs, before, inner, outer, gains):
    hidden = jax.nn.silu(jnp.dot(inputs, inner, preferred_element_type=jnp.float32)).astype(jnp.bfloat16)
    output = jnp.dot(hidden, outer, preferred_element_type=jnp.float32)
    return (before.astype(jnp.float32) + layer_norm(output, gains)).astype(jnp.bfloat16)

def reference(node_latents, fine_edges, long_edges, neighbours, coarse_slots, long_senders, long_receivers, edge_inner, edge_outer, edge_gain, node_inner, node_outer, node_gain):
    grid_rows, grid_columns, features = node_latents.shape
    shifted_code = neighbours + (neighbours >= 4).astype(jnp.int32)
    rows_here = lax.broadcasted_iota(jnp.int32, neighbours.shape, 0)
    cols_here = lax.broadcasted_iota(jnp.int32, neighbours.shape, 1)
    sender_rows = (rows_here + shifted_code // 3 - 1) % grid_rows
    sender_cols = (cols_here + shifted_code % 3 - 1) % grid_columns
    sender_flat = (sender_rows * grid_columns + sender_cols).reshape(-1).astype(jnp.int32)
    owner_device = lax.iota(jnp.int32, COARSE) // CO_DEV
    coarse_row = owner_device // N_PY * PR + coarse_slots // PC
    coarse_col = owner_device % N_PY * PC + coarse_slots % PC
    coarse_flat = (coarse_row * grid_columns + coarse_col).astype(jnp.int32)
    grid_cells = grid_rows * grid_columns
    latents = node_latents.reshape(grid_cells, features)
    fine_rows = fine_edges.reshape(grid_cells * K, features)
    long_rows = long_edges
    for layer_index in range(LAYERS):
        receivers_here = jnp.repeat(latents, K, axis=0)
        inputs = jnp.concatenate([fine_rows, jnp.take(latents, sender_flat, axis=0), receivers_here], axis=1)
        fine_rows = apply_mlp(inputs, fine_rows, edge_inner[layer_index], edge_outer[layer_index], edge_gain[layer_index])
        coarse = jnp.take(latents, coarse_flat, axis=0)
        long_inputs = jnp.concatenate([long_rows, jnp.take(coarse, long_senders, axis=0), jnp.take(coarse, long_receivers, axis=0)], axis=1)
        long_rows = apply_mlp(long_inputs, long_rows, edge_inner[layer_index], edge_outer[layer_index], edge_gain[layer_index])
        incoming = lax.optimization_barrier(jnp.sum(fine_rows.reshape(grid_cells, K, features).astype(jnp.float32), axis=1))
        long_totals = jax.ops.segment_sum(long_rows.astype(jnp.float32), long_receivers, num_segments=COARSE)
        incoming = incoming.at[coarse_flat].add(long_totals).astype(jnp.bfloat16)
        node_inputs = jnp.concatenate([latents, incoming], axis=1)
        latents = apply_mlp(node_inputs, latents, node_inner[layer_index], node_outer[layer_index], node_gain[layer_index])
    return (latents.reshape(node_latents.shape), fine_rows.reshape(fine_edges.shape), long_rows)
```

```python
import jax
import jax.numpy as jnp
from jax import lax
from jax.experimental import pallas as pl
from jax.experimental.pallas import tpu as pltpu
from jax.sharding import PartitionSpec as P

EPSILON = 1e-05
AXES = ("px", "py")
DIGITS = ((32, 4), (8, 4), (2, 4), (1, 2))
CORE = DIGITS[3]
SLOT = 32
BAND = 2
BUCKET = 4
VMEM = 48 * 1024 * 1024


def shift(values, digit, step):
    stride, size = digit
    pairs = []
    for i in range(128):
        here = i // stride % size
        pairs.append((i, i + ((here + step) % size - here) * stride))
    return lax.ppermute(values, AXES, pairs)


def spread(rows):
    pieces = [rows]
    for digit in DIGITS[:3]:
        joined = jnp.concatenate(pieces, axis=0) if len(pieces) > 1 else pieces[0]
        pieces = [joined] + [shift(joined, digit, s) for s in range(1, digit[1])]
    return pieces + [shift(piece, CORE, 1) for piece in pieces]


def table_index(device, row, coarse_count):
    me = lax.axis_index(AXES)

    def back(digit):
        stride, size = digit
        return (me // stride - device // stride) % size

    ky, kx, kz, kc = (back(digit) for digit in DIGITS)
    return (((kc * 4 + kz) * 4 + kx) * 4 + ky) * coarse_count + row


def along(values, axis, step):
    count = lax.axis_size(axis)
    return lax.ppermute(values, axis, [(i, (i + step) % count) for i in range(count)])


def extended(latents):
    rows, columns, features = latents.shape
    above = along(latents[-1:], "px", 1)
    below = along(latents[:1], "px", -1)
    tall = jnp.concatenate([above, latents, below], axis=0)
    left = along(tall[:, -1:], "py", 1)
    right = along(tall[:, :1], "py", -1)
    rest = jnp.zeros((rows + 2, SLOT - columns - 2, features), latents.dtype)
    return jnp.concatenate([tall, left, right, rest], axis=1).reshape(-1, features)


def selection(neighbours):
    rows, columns, degree = neighbours.shape
    q = neighbours + (neighbours >= 4).astype(jnp.int32)
    band_row = lax.broadcasted_iota(jnp.int32, neighbours.shape, 0) % BAND
    column = lax.broadcasted_iota(jnp.int32, neighbours.shape, 1)
    sent = column + q % 3 - 1
    sent = jnp.where(sent < 0, columns, jnp.where(sent >= columns, columns + 1, sent))
    sender = ((band_row + q // 3) * SLOT + sent).reshape(-1, 1)
    receiver = (128 + band_row * SLOT + column).reshape(-1, 1)
    lanes = lax.broadcasted_iota(jnp.int32, (rows * columns * degree, 256), 1)
    return ((lanes == sender) | (lanes == receiver)).astype(jnp.bfloat16)


def dot(a, b):
    return jnp.dot(a, b, preferred_element_type=jnp.float32)


def finish(before, inner_sum, outer, gains):
    hidden = jax.nn.silu(inner_sum).astype(jnp.bfloat16)
    output = dot(hidden, outer)
    center = output - jnp.mean(output, axis=-1, keepdims=True)
    spread_of = jnp.mean(center * center, axis=-1, keepdims=True)
    scaled = center * lax.rsqrt(spread_of + EPSILON) * gains
    return (before.astype(jnp.float32) + scaled).astype(jnp.bfloat16)


def fine_layer(layer, fine, picks, ext, inner, outer, gain, nodes):
    edges, features = fine.shape
    hidden = inner.shape[2]
    bands = 8
    block = edges // bands
    per_band = nodes // bands
    degree = block // per_band
    near = (BAND + 2) * SLOT

    def body(fine_ref, picks_ref, ext_ref, inner_ref, outer_ref, gain_ref, next_ref, sum_ref, send_ref, recv_ref):
        step = pl.program_id(0)

        @pl.when(step == 0)
        def _():
            send_ref[...] = dot(ext_ref[...], inner_ref[0, features : 2 * features]).astype(jnp.bfloat16)
            recv_ref[...] = dot(ext_ref[...], inner_ref[0, 2 * features :]).astype(jnp.bfloat16)

        start = pl.multiple_of(step * BAND * SLOT, BAND * SLOT)
        mine = pl.multiple_of(step * BAND * SLOT + SLOT, SLOT)
        before = fine_ref[...]
        total = dot(before, inner_ref[0, :features])
        total += dot(picks_ref[:, :near], send_ref[pl.ds(start, near), :])
        total += dot(picks_ref[:, near : near + BAND * SLOT], recv_ref[pl.ds(mine, BAND * SLOT), :])
        after = finish(before, total, outer_ref[0], gain_ref[layer : layer + 1, :])
        next_ref[...] = after
        node = lax.broadcasted_iota(jnp.int32, (per_band, block), 0) * degree
        edge = lax.broadcasted_iota(jnp.int32, (per_band, block), 1)
        pool = ((edge >= node) & (edge < node + degree)).astype(jnp.bfloat16)
        sum_ref[...] = dot(pool, after)

    whole = lambda shape: pl.BlockSpec(shape, lambda i: (layer,) + (0,) * (len(shape) - 1))
    fixed = lambda shape: pl.BlockSpec(shape, lambda i: (0,) * len(shape))
    return pl.pallas_call(
        body,
        name=f"fine{layer}",
        out_shape=(
            jax.ShapeDtypeStruct(fine.shape, jnp.bfloat16),
            jax.ShapeDtypeStruct((nodes, features), jnp.float32),
        ),
        grid=(bands,),
        in_specs=[
            pl.BlockSpec((block, features), lambda i: (i, 0)),
            pl.BlockSpec((block, 256), lambda i: (i, 0)),
            fixed(ext.shape),
            whole((1,) + inner.shape[1:]),
            whole((1,) + outer.shape[1:]),
            fixed(gain.shape),
        ],
        out_specs=(
            pl.BlockSpec((block, features), lambda i: (i, 0)),
            pl.BlockSpec((per_band, features), lambda i: (i, 0)),
        ),
        scratch_shapes=[
            pltpu.VMEM((ext.shape[0], hidden), jnp.bfloat16),
            pltpu.VMEM((ext.shape[0], hidden), jnp.bfloat16),
        ],
        compiler_params=pltpu.CompilerParams(
            dimension_semantics=("arbitrary",), vmem_limit_bytes=VMEM
        ),
    )(fine, picks, ext, inner, outer, gain)


def long_layer(layer, held, sender, receiver, pieces, inner, outer, gain):
    slots, features = held.shape
    count = len(pieces)
    each = pieces[0].shape[0]
    tile = 128

    def body(held_ref, sender_ref, receiver_ref, inner_ref, outer_ref, gain_ref, *rest):
        piece_refs, next_ref, table, arrived = rest[:count], rest[count], rest[count + 1], rest[count + 2]
        copies = [
            pltpu.make_async_copy(piece_refs[p], table.at[pl.ds(p * each, each), :], arrived.at[p])
            for p in range(count)
        ]
        for copy in copies:
            copy.start()
        for copy in copies:
            copy.wait()
        for m in range(slots // tile):
            rows = slice(m * tile, (m + 1) * tile)
            lanes = lax.broadcasted_iota(jnp.int32, (tile, count * each), 1)
            sent = dot((lanes == sender_ref[rows, :]).astype(jnp.bfloat16), table[...]).astype(jnp.bfloat16)
            lanes = lax.broadcasted_iota(jnp.int32, (tile, 32), 1)
            got = dot((lanes == receiver_ref[rows, :]).astype(jnp.bfloat16), table[:32, :]).astype(jnp.bfloat16)
            before = held_ref[rows, :]
            total = dot(before, inner_ref[0, :features])
            total += dot(sent, inner_ref[0, features : 2 * features])
            total += dot(got, inner_ref[0, 2 * features :])
            next_ref[rows, :] = finish(before, total, outer_ref[0], gain_ref[layer : layer + 1, :])

    whole = lambda shape: pl.BlockSpec(shape, lambda i: (layer,) + (0,) * (len(shape) - 1))
    fixed = lambda shape: pl.BlockSpec(shape, lambda i: (0,) * len(shape))
    return pl.pallas_call(
        body,
        name=f"long{layer}",
        out_shape=jax.ShapeDtypeStruct(held.shape, jnp.bfloat16),
        grid=(1,),
        in_specs=[
            fixed(held.shape),
            fixed(sender.shape),
            fixed(receiver.shape),
            whole((1,) + inner.shape[1:]),
            whole((1,) + outer.shape[1:]),
            fixed(gain.shape),
        ]
        + [pl.BlockSpec(memory_space=pl.ANY)] * count,
        out_specs=fixed(held.shape),
        scratch_shapes=[
            pltpu.VMEM((count * each, features), jnp.bfloat16),
            pltpu.SemaphoreType.DMA((count,)),
        ],
        compiler_params=pltpu.CompilerParams(vmem_limit_bytes=VMEM),
    )(held, sender, receiver, inner, outer, gain, *pieces)


def node_layer(layer, latents, fine_sum, held, target, coarse_column, inner, outer, gain, coarse_count):
    nodes, features = latents.shape
    slots = held.shape[0]

    def body(latents_ref, sum_ref, held_ref, target_ref, coarse_ref, inner_ref, outer_ref, gain_ref, next_ref, own_ref):
        node = lax.broadcasted_iota(jnp.int32, (nodes, slots), 0)
        adds = (node == target_ref[...]).astype(jnp.bfloat16)
        incoming = (sum_ref[...] + dot(adds, held_ref[...])).astype(jnp.bfloat16)
        before = latents_ref[...]
        total = dot(before, inner_ref[0, :features]) + dot(incoming, inner_ref[0, features:])
        after = finish(before, total, outer_ref[0], gain_ref[layer : layer + 1, :])
        next_ref[...] = after
        lanes = lax.broadcasted_iota(jnp.int32, (coarse_ref.shape[0], nodes), 1)
        own = dot((lanes == coarse_ref[...]).astype(jnp.bfloat16), after)
        own_ref[...] = own[:coarse_count].astype(jnp.bfloat16)

    whole = lambda shape: pl.BlockSpec(shape, lambda i: (layer,) + (0,) * (len(shape) - 1))
    fixed = lambda shape: pl.BlockSpec(shape, lambda i: (0,) * len(shape))
    return pl.pallas_call(
        body,
        name=f"node{layer}",
        out_shape=(
            jax.ShapeDtypeStruct(latents.shape, jnp.bfloat16),
            jax.ShapeDtypeStruct((coarse_count, features), jnp.bfloat16),
        ),
        grid=(1,),
        in_specs=[
            fixed(latents.shape),
            fixed(fine_sum.shape),
            fixed(held.shape),
            fixed(target.shape),
            fixed(coarse_column.shape),
            whole((1,) + inner.shape[1:]),
            whole((1,) + outer.shape[1:]),
            fixed(gain.shape),
        ],
        out_specs=(fixed(latents.shape), fixed((coarse_count, features))),
        compiler_params=pltpu.CompilerParams(vmem_limit_bytes=VMEM),
    )(latents, fine_sum, held, target, coarse_column, inner, outer, gain)


def bucketed(long_edges, senders, receivers, coarse_count, devices):
    count, features = long_edges.shape
    owner = receivers // coarse_count
    same = owner[:, None] == owner[None, :]
    index = lax.iota(jnp.int32, count)
    rank = jnp.sum((same & (index[None, :] < index[:, None])).astype(jnp.int32), axis=1)
    place = owner * BUCKET + rank
    spots = lax.broadcasted_iota(jnp.int32, (devices * BUCKET, count), 0)
    to_edge = (spots == place[None, :]).astype(jnp.bfloat16)
    to_tags = (spots == owner[None, :] * BUCKET + BUCKET - 1).astype(jnp.bfloat16)
    lane = lax.broadcasted_iota(jnp.int32, (count, features), 1)
    field = lane % 4
    tag = jnp.where(
        field == 0,
        (senders // coarse_count)[:, None],
        jnp.where(
            field == 1,
            (senders % coarse_count)[:, None],
            jnp.where(field == 2, (receivers % coarse_count)[:, None], 1),
        ),
    )
    tag = jnp.where(lane // 4 == rank[:, None], tag, 0).astype(jnp.bfloat16)
    filled = dot(to_edge, long_edges) + dot(to_tags, tag)
    return filled.astype(jnp.bfloat16).reshape(devices, BUCKET, features), owner * 3 + rank


def exchange(rows):
    return lax.all_to_all(rows, AXES, split_axis=0, concat_axis=0, tiled=True)


def shards(
    node_latents,
    fine_edges,
    long_edges,
    neighbours,
    coarse_slots,
    long_senders,
    long_receivers,
    edge_inner,
    edge_outer,
    edge_gain,
    node_inner,
    node_outer,
    node_gain,
):
    patch_rows, patch_columns, features = node_latents.shape
    nodes = patch_rows * patch_columns
    coarse_count = coarse_slots.shape[0]
    layers = edge_inner.shape[0]
    devices = lax.axis_size("px") * lax.axis_size("py")

    latents = node_latents.reshape(nodes, features)
    own = jnp.take(latents, coarse_slots, axis=0, mode="clip")
    payload, back = bucketed(long_edges, long_senders, long_receivers, coarse_count, devices)
    arrived = exchange(payload)
    held = arrived.reshape(devices * BUCKET, features)
    tags = arrived[:, BUCKET - 1, : 4 * (BUCKET - 1)].astype(jnp.int32)
    tags = jnp.pad(tags, ((0, 0), (0, 4))).reshape(devices * BUCKET, 4)
    valid = tags[:, 3:] > 0
    sender = jnp.where(valid, table_index(tags[:, :1], tags[:, 1:2], coarse_count), -1)
    receiver = jnp.where(valid, tags[:, 2:3], -1)
    match = receiver == lax.iota(jnp.int32, coarse_count)[None, :]
    target = jnp.sum(jnp.where(match, coarse_slots[None, :] + 1, 0), axis=1)[None, :] - 1
    coarse_column = jnp.pad(coarse_slots, (0, 32 - coarse_count), constant_values=-1)[:, None]
    picks = selection(neighbours)
    fine = fine_edges.reshape(-1, features)
    for layer in range(layers):
        pieces = spread(own)
        ext = extended(latents.reshape(node_latents.shape))
        fine, fine_sum = fine_layer(layer, fine, picks, ext, edge_inner, edge_outer, edge_gain, nodes)
        held = long_layer(layer, held, sender, receiver, pieces, edge_inner, edge_outer, edge_gain)
        latents, own = node_layer(
            layer, latents, fine_sum, held, target, coarse_column, node_inner, node_outer, node_gain, coarse_count
        )
    home = exchange(held.reshape(devices, BUCKET, features)[:, : BUCKET - 1])
    picked = back[:, None] == lax.iota(jnp.int32, devices * (BUCKET - 1))[None, :]
    new_long = dot(picked.astype(jnp.bfloat16), home.reshape(-1, features)).astype(jnp.bfloat16)
    return latents.reshape(node_latents.shape), fine.reshape(fine_edges.shape), new_long


def solution(mesh):
    in_specs = (
        P("px", "py", None),
        P("px", "py", None, None),
        P(AXES, None),
        P("px", "py", None),
        P(AXES),
        P(AXES),
        P(AXES),
        P(),
        P(),
        P(),
        P(),
        P(),
        P(),
    )
    out_specs = (P("px", "py", None), P("px", "py", None, None), P(AXES, None))
    return jax.shard_map(shards, mesh=mesh, in_specs=in_specs, out_specs=out_specs, check_vma=False)
```

```python
import jax
import jax.numpy as jnp
from jax import lax
from jax.experimental import pallas as pl
from jax.experimental.pallas import tpu as pltpu
from jax.sharding import PartitionSpec as P

EPSILON = 1e-05
AXES = ("px", "py")
DIGITS = ((32, 4), (8, 4), (2, 4), (1, 2))
CORE = DIGITS[3]
BAND = 4
TAGS = 128
LOW = 64
CAP = 3
VMEM = 24 * 1024 * 1024


def shift(values, digit, step):
    stride, size = digit
    pairs = []
    for i in range(128):
        here = i // stride % size
        pairs.append((i, i + ((here + step) % size - here) * stride))
    return lax.ppermute(values, AXES, pairs)


def tie(*values):
    return lax.optimization_barrier(values)


def stage(rows, digit):
    return [rows] + [shift(rows, digit, s) for s in range(1, digit[1])]


def table_row(device, coarse, coarse_count):
    home, row = coarse // coarse_count, coarse % coarse_count
    ky, kx, kz, kc = ((device // stride - home // stride) % size for stride, size in DIGITS)
    return (((kc * 4 + kz) * 4 + kx) * 4 + ky) * coarse_count + row


def along(values, axis, step):
    count = lax.axis_size(axis)
    return lax.ppermute(values, axis, [(i, (i + step) % count) for i in range(count)])


def selection(neighbours):
    rows, columns, degree = neighbours.shape
    codes = neighbours.transpose(1, 2, 0)
    q = codes + (codes >= 4).astype(jnp.int32)
    column = lax.broadcasted_iota(jnp.int32, codes.shape, 0)
    row = lax.broadcasted_iota(jnp.int32, codes.shape, 2)
    from_row = row + q // 3 - 1
    step = q % 3
    near = (column % BAND + step) * rows + from_row
    sender = jnp.where(from_row < 0, 160 + column + step, jnp.where(from_row >= rows, 192 + column + step, near))
    receiver = 96 + column % BAND * rows + row
    lanes = lax.broadcasted_iota(jnp.int32, codes.shape + (256,), 3)
    picks = (lanes == sender[..., None]) | (lanes == receiver[..., None])
    return picks.astype(jnp.bfloat16).reshape(-1, 256)


def dot(a, b):
    return jnp.dot(a, b, preferred_element_type=jnp.float32)


def finish(before, inner_sum, outer, gains):
    hidden = jax.nn.silu(inner_sum).astype(jnp.bfloat16)
    output = dot(hidden, outer)
    center = output - jnp.mean(output, axis=-1, keepdims=True)
    spread_of = jnp.mean(center * center, axis=-1, keepdims=True)
    scaled = center * lax.rsqrt(spread_of + EPSILON) * gains
    return (before.astype(jnp.float32) + scaled).astype(jnp.bfloat16)


def fine_layer(layer, fine, picks, latents, left, right, above, below, inner, outer, gain, rows):
    edges, features = fine.shape
    nodes = latents.shape[0]
    hidden = inner.shape[2]
    near = (BAND + 2) * rows
    own = BAND * rows
    steps = nodes // own
    block = edges // steps
    degree = edges // nodes
    columns = above.shape[0]

    def body(fine_ref, picks_ref, latents_ref, left_ref, right_ref, above_ref, below_ref, inner_ref, outer_ref, gain_ref,
             next_ref, sum_ref, send_ref, recv_ref, table_ref):
        step = pl.program_id(0)

        @pl.when(step == 0)
        def _():
            send = inner_ref[layer, features : 2 * features, :]
            project = lambda ref: dot(ref[...], send).astype(jnp.bfloat16)
            send_ref[:rows, :] = project(left_ref)
            send_ref[rows : rows + nodes, :] = project(latents_ref)
            send_ref[rows + nodes :, :] = project(right_ref)
            recv_ref[...] = dot(latents_ref[...], inner_ref[layer, 2 * features :, :]).astype(jnp.bfloat16)
            table_ref[...] = jnp.zeros(table_ref.shape, jnp.bfloat16)
            table_ref[160 : 160 + columns, :] = project(above_ref)
            table_ref[192 : 192 + columns, :] = project(below_ref)

        start = pl.multiple_of(step * own, own)
        table_ref[:near, :] = send_ref[pl.ds(start, near), :]
        table_ref[near : near + own, :] = recv_ref[pl.ds(start, own), :]
        before = fine_ref[...]
        total = dot(before, inner_ref[layer, :features, :]) + dot(picks_ref[...], table_ref[...])
        after = finish(before, total, outer_ref[layer], gain_ref[layer : layer + 1, :])
        next_ref[...] = after
        split = after.astype(jnp.float32).reshape(BAND, degree, rows, features)
        sum_ref[...] = jnp.sum(split, axis=1).reshape(own, features)

    held = pl.BlockSpec(memory_space=pltpu.VMEM)
    return pl.pallas_call(
        body,
        name=f"fine{layer}",
        out_shape=(
            jax.ShapeDtypeStruct(fine.shape, jnp.bfloat16),
            jax.ShapeDtypeStruct((nodes, features), jnp.float32),
        ),
        grid=(steps,),
        in_specs=[
            pl.BlockSpec((block, features), lambda i: (i, 0)),
            pl.BlockSpec((block, 256), lambda i: (i, 0)),
        ]
        + [held] * 8,
        out_specs=(
            pl.BlockSpec((block, features), lambda i: (i, 0)),
            pl.BlockSpec((own, features), lambda i: (i, 0)),
        ),
        scratch_shapes=[
            pltpu.VMEM((nodes + 2 * rows, hidden), jnp.bfloat16),
            pltpu.VMEM((nodes, hidden), jnp.bfloat16),
            pltpu.VMEM((256, hidden), jnp.bfloat16),
        ],
        compiler_params=pltpu.CompilerParams(dimension_semantics=("arbitrary",), vmem_limit_bytes=VMEM),
    )(fine, picks, latents, left, right, above, below, inner, outer, gain)


def coarse_layer(layer, long_rows, tagged, pieces, latents, fine_sum, coarse_row, coarse_column,
                 edge_inner, edge_outer, edge_gain, node_inner, node_outer, node_gain, slots, coarse_count):
    edges = tagged.shape[0]
    nodes, features = latents.shape
    count = len(pieces)
    each = pieces[0].shape[0]
    table_rows = count * each
    pad = coarse_row.shape[1]

    def body(long_ref, tag_ref, latents_ref, sum_ref, row_ref, column_ref, ei_ref, eo_ref, eg_ref, ni_ref, no_ref, ng_ref, *rest):
        piece_refs = rest[:count]
        long_next_ref, next_ref, own_ref, table = rest[count:]
        for p in range(count):
            table[p * each : (p + 1) * each, :] = piece_refs[p][...]
        tags = tag_ref[:, features : features + TAGS].astype(jnp.float32).astype(jnp.int32)
        valid = tags[:, 4:5] > 0
        sender = jnp.where(valid, tags[:, 0:1] * LOW + tags[:, 1:2], -1)
        receiver = jnp.where(valid, tags[:, 2:3] * LOW + tags[:, 3:4], -1)

        def pick(index, width):
            lanes = lax.broadcasted_iota(jnp.int32, (index.shape[0], width), 1)
            return (lanes == index).astype(jnp.bfloat16)

        sent = dot(pick(sender, table_rows), table[...]).astype(jnp.bfloat16)
        here = pick(receiver[:slots], pad)
        got_here = dot(here, table[:pad, :]).astype(jnp.bfloat16)
        got_away = dot(pick(receiver[slots:], table_rows), table[...]).astype(jnp.bfloat16)
        got = jnp.concatenate([got_here, got_away], axis=0)
        before = long_ref[:, :features]
        total = dot(before, ei_ref[layer, :features, :])
        total += dot(sent, ei_ref[layer, features : 2 * features, :])
        total += dot(got, ei_ref[layer, 2 * features :, :])
        after = finish(before, total, eo_ref[layer], eg_ref[layer : layer + 1, :])
        long_next_ref[...] = after

        node = lax.broadcasted_iota(jnp.int32, (nodes, pad), 0)
        place = (node == row_ref[...]).astype(jnp.bfloat16)
        adds = lax.dot_general(place, here, (((1,), (1,)), ((), ())), preferred_element_type=jnp.float32)
        incoming = (sum_ref[...] + dot(adds.astype(jnp.bfloat16), after[:slots])).astype(jnp.bfloat16)
        old = latents_ref[...]
        total = dot(old, ni_ref[layer, :features, :]) + dot(incoming, ni_ref[layer, features:, :])
        new = finish(old, total, no_ref[layer], ng_ref[layer : layer + 1, :])
        next_ref[...] = new
        own_ref[...] = dot(pick(column_ref[...], nodes), new)[:coarse_count].astype(jnp.bfloat16)

    held = pl.BlockSpec(memory_space=pltpu.VMEM)
    return pl.pallas_call(
        body,
        name=f"coarse{layer}",
        out_shape=(
            jax.ShapeDtypeStruct((edges, features), jnp.bfloat16),
            jax.ShapeDtypeStruct(latents.shape, jnp.bfloat16),
            jax.ShapeDtypeStruct((coarse_count, features), jnp.bfloat16),
        ),
        in_specs=[held] * (12 + count),
        out_specs=(held, held, held),
        scratch_shapes=[pltpu.VMEM((table_rows, features), jnp.bfloat16)],
        compiler_params=pltpu.CompilerParams(vmem_limit_bytes=VMEM),
    )(long_rows, tagged, latents, fine_sum, coarse_row, coarse_column,
      edge_inner, edge_outer, edge_gain, node_inner, node_outer, node_gain, *pieces)


def tag_lanes(device, senders, receivers, coarse_count):
    sender = table_row(device, senders, coarse_count)
    receiver = table_row(device, receivers, coarse_count)
    fields = (sender // LOW, sender % LOW, receiver // LOW, receiver % LOW)
    lane = lax.broadcasted_iota(jnp.int32, (senders.shape[0], TAGS), 1)
    tags = jnp.where(lane == len(fields), 1, 0)
    for at, field in enumerate(fields):
        tags = jnp.where(lane == at, field[:, None], tags)
    return tags.astype(jnp.bfloat16)


def bucketed(long_edges, senders, receivers, coarse_count, devices):
    count = receivers.shape[0]
    owner = receivers // coarse_count
    same = owner[:, None] == owner[None, :]
    index = lax.iota(jnp.int32, count)
    rank = jnp.sum((same & (index[None, :] < index[:, None])).astype(jnp.int32), axis=1)
    place = owner * CAP + rank
    spots = lax.broadcasted_iota(jnp.int32, (devices * CAP, count), 0)
    to_edge = (spots == place[None, :]).astype(jnp.bfloat16)
    tagged = jnp.concatenate([long_edges, tag_lanes(owner, senders, receivers, coarse_count)], axis=1)
    return dot(to_edge, tagged).astype(jnp.bfloat16)


def shards(
    node_latents,
    fine_edges,
    long_edges,
    neighbours,
    coarse_slots,
    long_senders,
    long_receivers,
    edge_inner,
    edge_outer,
    edge_gain,
    node_inner,
    node_outer,
    node_gain,
):
    rows, columns, features = node_latents.shape
    degree = fine_edges.shape[2]
    nodes = rows * columns
    coarse_count = coarse_slots.shape[0]
    layers = edge_inner.shape[0]
    devices = lax.axis_size("px") * lax.axis_size("py")
    slots = devices * CAP

    latents = node_latents.transpose(1, 0, 2).reshape(nodes, features)
    fine = fine_edges.transpose(1, 2, 0, 3).reshape(nodes * degree, features)
    coarse_at = coarse_slots % columns * rows + coarse_slots // columns
    own = jnp.take(latents, coarse_at, axis=0, mode="clip")
    padded = jnp.pad(coarse_at, (0, 32 - coarse_count), constant_values=-1)
    coarse_row, coarse_column = padded[None, :], padded[:, None]
    me = lax.axis_index(AXES)
    mine = jnp.concatenate([long_edges, tag_lanes(me, long_senders, long_receivers, coarse_count)], axis=1)
    payload = bucketed(long_edges, long_senders, long_receivers, coarse_count, devices)
    picks = selection(neighbours)
    tagged = None
    for layer in range(layers):
        joined = jnp.concatenate(stage(own, DIGITS[0]), axis=0)
        joined, grid = tie(joined, latents.reshape(columns, rows, features))
        left = along(grid[-1], "py", 1)
        right = along(grid[0], "py", -1)
        joined = jnp.concatenate(stage(joined, DIGITS[1]), axis=0)
        joined, left, right, payload = tie(joined, left, right, payload)
        pieces = stage(joined, DIGITS[2])
        high = jnp.concatenate([left[-1:], grid[:, -1], right[-1:]], axis=0)
        low = jnp.concatenate([left[:1], grid[:, 0], right[:1]], axis=0)
        above = along(high, "px", 1)
        below = along(low, "px", -1)
        if tagged is None:
            sent = payload.reshape(devices, CAP, features + TAGS)
            arrived = lax.all_to_all(sent, AXES, split_axis=0, concat_axis=0, tiled=True)
            tagged = jnp.concatenate([arrived.reshape(slots, features + TAGS), mine], axis=0)
            long_rows = tagged
        fine, fine_sum = fine_layer(
            layer, fine, picks, latents, left, right, above, below, edge_inner, edge_outer, edge_gain, rows
        )
        pieces = pieces + [shift(piece, CORE, 1) for piece in pieces]
        long_rows, latents, own = coarse_layer(
            layer, long_rows, tagged, pieces, latents, fine_sum, coarse_row, coarse_column,
            edge_inner, edge_outer, edge_gain, node_inner, node_outer, node_gain, slots, coarse_count,
        )
    return (
        latents.reshape(columns, rows, features).transpose(1, 0, 2),
        fine.reshape(columns, degree, rows, features).transpose(2, 0, 1, 3),
        long_rows[slots:],
    )


def solution(mesh):
    in_specs = (
        P("px", "py", None),
        P("px", "py", None, None),
        P(AXES, None),
        P("px", "py", None),
        P(AXES),
        P(AXES),
        P(AXES),
        P(),
        P(),
        P(),
        P(),
        P(),
        P(),
    )
    out_specs = (P("px", "py", None), P("px", "py", None, None), P(AXES, None))
    return jax.shard_map(shards, mesh=mesh, in_specs=in_specs, out_specs=out_specs, check_vma=False)
```

```python
import jax
import jax.numpy as jnp
from jax import lax
from jax.experimental import pallas as pl
from jax.experimental.pallas import tpu as pltpu
from jax.sharding import PartitionSpec as P

EPSILON = 1e-05
AXES = ("px", "py")
DIGITS = ((32, 4), (8, 4), (2, 4), (1, 2))
CORE = DIGITS[3]
BAND = 4
TAGS = 128
LOW = 64
CAP = 3
MIB = 1024 * 1024


def shift(values, digit, step):
    stride, size = digit
    pairs = []
    for i in range(128):
        here = i // stride % size
        pairs.append((i, i + ((here + step) % size - here) * stride))
    return lax.ppermute(values, AXES, pairs)


def tie(*values):
    return lax.optimization_barrier(values)


def stage(rows, digit):
    return [rows] + [shift(rows, digit, s) for s in range(1, digit[1])]


def table_row(digits, coarse, coarse_count):
    home = jnp.floor((coarse.astype(jnp.float32) + 0.5) * (1.0 / coarse_count)).astype(jnp.int32)
    row = coarse - home * coarse_count
    ky, kx, kz, kc = (
        (mine - lax.shift_right_logical(home, stride.bit_length() - 1)) & (size - 1)
        for mine, (stride, size) in zip(digits, DIGITS, strict=True)
    )
    return (((kc * 4 + kz) * 4 + kx) * 4 + ky) * coarse_count + row, home, row


def along(values, axis, step):
    count = lax.axis_size(axis)
    return lax.ppermute(values, axis, [(i, (i + step) % count) for i in range(count)])


def selection(neighbours):
    rows, columns, degree = neighbours.shape
    codes = neighbours.transpose(1, 2, 0)
    q = codes + (codes >= 4).astype(jnp.int32)
    column = lax.broadcasted_iota(jnp.int32, codes.shape, 0)
    row = lax.broadcasted_iota(jnp.int32, codes.shape, 2)
    from_row = row + q // 3 - 1
    step = q % 3
    near = (column % BAND + step) * rows + from_row
    sender = jnp.where(from_row < 0, 160 + column + step, jnp.where(from_row >= rows, 192 + column + step, near))
    receiver = 96 + column % BAND * rows + row
    lanes = lax.broadcasted_iota(jnp.int32, codes.shape + (256,), 3)
    picks = (lanes == sender[..., None]) | (lanes == receiver[..., None])
    return picks.astype(jnp.bfloat16).reshape(-1, 256)


def dot(a, b):
    return jnp.dot(a, b, preferred_element_type=jnp.float32)


def finish(before, inner_sum, outer, gains):
    hidden = jax.nn.silu(inner_sum).astype(jnp.bfloat16)
    output = dot(hidden, outer)
    center = output - jnp.mean(output, axis=-1, keepdims=True)
    spread_of = jnp.mean(center * center, axis=-1, keepdims=True)
    scaled = center * lax.rsqrt(spread_of + EPSILON) * gains
    return (before.astype(jnp.float32) + scaled).astype(jnp.bfloat16)


def fine_layer(layer, fine, picks, latents, left, right, above, below, inner, outer, gain, rows):
    edges, features = fine.shape
    nodes = latents.shape[0]
    hidden = inner.shape[2]
    near = (BAND + 2) * rows
    own = BAND * rows
    steps = nodes // own
    block = edges // steps
    degree = edges // nodes
    columns = above.shape[0]

    def body(fine_ref, picks_ref, latents_ref, left_ref, right_ref, above_ref, below_ref, inner_ref, outer_ref, gain_ref,
             next_ref, sum_ref, send_ref, recv_ref, table_ref):
        step = pl.program_id(0)

        @pl.when(step == 0)
        def _():
            send = inner_ref[layer, features : 2 * features, :]
            project = lambda ref: dot(ref[...], send).astype(jnp.bfloat16)
            send_ref[:rows, :] = project(left_ref)
            send_ref[rows : rows + nodes, :] = project(latents_ref)
            send_ref[rows + nodes :, :] = project(right_ref)
            recv_ref[...] = dot(latents_ref[...], inner_ref[layer, 2 * features :, :]).astype(jnp.bfloat16)
            table_ref[...] = jnp.zeros(table_ref.shape, jnp.bfloat16)
            table_ref[160 : 160 + columns, :] = project(above_ref)
            table_ref[192 : 192 + columns, :] = project(below_ref)

        start = pl.multiple_of(step * own, own)
        table_ref[:near, :] = send_ref[pl.ds(start, near), :]
        table_ref[near : near + own, :] = recv_ref[pl.ds(start, own), :]
        before = fine_ref[...]
        total = dot(before, inner_ref[layer, :features, :]) + dot(picks_ref[...], table_ref[...])
        after = finish(before, total, outer_ref[layer], gain_ref[layer : layer + 1, :])
        next_ref[...] = after
        split = after.astype(jnp.float32).reshape(BAND, degree, rows, features)
        sum_ref[...] = jnp.sum(split, axis=1).reshape(own, features)

    held = pl.BlockSpec(memory_space=pltpu.VMEM)
    return pl.pallas_call(
        body,
        name=f"fine{layer}",
        out_shape=(
            jax.ShapeDtypeStruct(fine.shape, jnp.bfloat16),
            jax.ShapeDtypeStruct((nodes, features), jnp.float32),
        ),
        grid=(steps,),
        in_specs=[
            pl.BlockSpec((block, features), lambda i: (i, 0)),
            pl.BlockSpec((block, 256), lambda i: (i, 0)),
        ]
        + [held] * 8,
        out_specs=(
            pl.BlockSpec((block, features), lambda i: (i, 0)),
            pl.BlockSpec((own, features), lambda i: (i, 0)),
        ),
        scratch_shapes=[
            pltpu.VMEM((nodes + 2 * rows, hidden), jnp.bfloat16),
            pltpu.VMEM((nodes, hidden), jnp.bfloat16),
            pltpu.VMEM((256, hidden), jnp.bfloat16),
        ],
        compiler_params=pltpu.CompilerParams(dimension_semantics=("arbitrary",), vmem_limit_bytes=14 * MIB),
    )(fine, picks, latents, left, right, above, below, inner, outer, gain)


def pick(index, width):
    lanes = lax.broadcasted_iota(jnp.int32, (index.shape[0], width), 1)
    return (lanes == index).astype(jnp.bfloat16)


def rows_to_columns(left, right):
    return lax.dot_general(left, right, (((1,), (1,)), ((), ())), preferred_element_type=jnp.float32)


def decode(tags, at):
    numbers = tags.astype(jnp.int32)
    return jnp.where(numbers[:, 4:5] > 0, numbers[:, at : at + 1] * LOW + numbers[:, at + 1 : at + 2], -1)


def coarse_start(coarse_slots, latents, rows, columns):
    count = coarse_slots.shape[1]
    nodes, features = latents.shape

    def body(slots_ref, latents_ref, own_ref, choose_ref):
        slot = slots_ref[...]
        row = jnp.floor((slot.astype(jnp.float32) + 0.5) * (1.0 / columns)).astype(jnp.int32)
        at = (slot - row * columns) * rows + row
        place = (lax.broadcasted_iota(jnp.int32, (nodes, count), 0) == at).astype(jnp.bfloat16)
        same = lax.broadcasted_iota(jnp.int32, (32, count), 0) == lax.broadcasted_iota(jnp.int32, (32, count), 1)
        choose = rows_to_columns(same.astype(jnp.bfloat16), place).astype(jnp.bfloat16)
        choose_ref[...] = choose
        own_ref[...] = dot(choose, latents_ref[...])[:count].astype(jnp.bfloat16)

    held = pl.BlockSpec(memory_space=pltpu.VMEM)
    return pl.pallas_call(
        body,
        name="coarse_start",
        out_shape=(
            jax.ShapeDtypeStruct((count, features), jnp.bfloat16),
            jax.ShapeDtypeStruct((32, nodes), jnp.bfloat16),
        ),
        in_specs=[held] * 2,
        out_specs=(held, held),
        compiler_params=pltpu.CompilerParams(vmem_limit_bytes=4 * MIB),
    )(coarse_slots, latents)


def pack_edges(long_edges, senders, receivers, me, coarse_count, devices):
    count, features = long_edges.shape
    blocks = features // TAGS
    slots = devices * CAP

    def body(me_ref, long_ref, send_ref, recv_ref, sent_ref, mine_ref, wide):
        send, recv = send_ref[...], recv_ref[...]
        here = [
            lax.shift_right_logical(me_ref[0], stride.bit_length() - 1) & (size - 1) for stride, size in DIGITS
        ]
        _, owner, row = table_row(here, recv, coarse_count)
        there = [
            lax.shift_right_logical(owner, stride.bit_length() - 1) & (size - 1) for stride, size in DIGITS
        ]
        field = lax.broadcasted_iota(jnp.int32, (TAGS, count), 0)

        def fields(digits):
            sender = table_row(digits, send, coarse_count)[0]
            receiver = table_row(digits, recv, coarse_count)[0]
            both = jnp.where(field < 2, sender, receiver)
            high = lax.shift_right_logical(both, LOW.bit_length() - 1)
            value = jnp.where(field % 2 == 0, high, both & (LOW - 1))
            value = jnp.where(field == 4, 1, jnp.where(field == 5, owner, value))
            return jnp.where(field < 6, value, 0).astype(jnp.float32).astype(jnp.bfloat16)

        down = lax.broadcasted_iota(jnp.int32, (count, count), 0)
        across = lax.broadcasted_iota(jnp.int32, (count, count), 1)
        mine = rows_to_columns((down == across).astype(jnp.bfloat16), fields(here))
        mine_ref[...] = mine.astype(jnp.bfloat16)
        same = (mine[:, 5:6].astype(jnp.int32) == owner) & (down < across)
        rank = jnp.sum(same.astype(jnp.float32), axis=0, keepdims=True).astype(jnp.int32)
        spot = rank * devices + owner
        place = (lax.broadcasted_iota(jnp.int32, (slots, count), 0) == spot).astype(jnp.bfloat16)
        edges = dot(place, long_ref[...])
        tags = rows_to_columns(place, fields(there))
        for j in range(CAP):
            part = slice(j * devices, (j + 1) * devices)
            for b in range(blocks):
                wide[pl.ds(j * blocks + b, devices, stride=16), :] = edges[part, b * TAGS : (b + 1) * TAGS]
            wide[pl.ds(CAP * blocks + j, devices, stride=16), :] = tags[part]
        wide[pl.ds(15, devices, stride=16), :] = jnp.zeros((devices, TAGS), jnp.float32)
        sent_ref[...] = wide[...].astype(jnp.bfloat16)

    held = pl.BlockSpec(memory_space=pltpu.VMEM)
    return pl.pallas_call(
        body,
        name="pack_edges",
        out_shape=(
            jax.ShapeDtypeStruct((devices * 16, TAGS), jnp.bfloat16),
            jax.ShapeDtypeStruct((count, TAGS), jnp.bfloat16),
        ),
        in_specs=[pl.BlockSpec(memory_space=pltpu.SMEM)] + [held] * 3,
        out_specs=(held, held),
        scratch_shapes=[pltpu.VMEM((devices * 16, TAGS), jnp.float32)],
        compiler_params=pltpu.CompilerParams(vmem_limit_bytes=8 * MIB),
    )(me, long_edges, senders, receivers)


def unpack_edges(arrived, choose, features, table_rows):
    devices = arrived.shape[0] // 16
    blocks = features // TAGS
    slots = devices * CAP
    pad, nodes = choose.shape

    def body(arrived_ref, choose_ref, rows_ref, send_ref, recv_ref, adds_ref, wide):
        wide[...] = arrived_ref[...].astype(jnp.float32)
        for j in range(CAP):
            part = slice(j * devices, (j + 1) * devices)
            for b in range(blocks):
                lanes = slice(b * TAGS, (b + 1) * TAGS)
                rows_ref[part, lanes] = wide[pl.ds(j * blocks + b, devices, stride=16), :].astype(jnp.bfloat16)
            tags = wide[pl.ds(CAP * blocks + j, devices, stride=16), :]
            send_ref[part, :] = pick(decode(tags, 0), table_rows)
            recv_ref[part, :] = pick(decode(tags, 2), TAGS)
        here = recv_ref[:, :pad]
        place = lax.dot_general(choose_ref[...], here, (((0,), (1,)), ((), ())), preferred_element_type=jnp.float32)
        adds_ref[...] = place.astype(jnp.bfloat16)

    held = pl.BlockSpec(memory_space=pltpu.VMEM)
    return pl.pallas_call(
        body,
        name="unpack_edges",
        out_shape=(
            jax.ShapeDtypeStruct((slots, features), jnp.bfloat16),
            jax.ShapeDtypeStruct((slots, table_rows), jnp.bfloat16),
            jax.ShapeDtypeStruct((slots, TAGS), jnp.bfloat16),
            jax.ShapeDtypeStruct((nodes, slots), jnp.bfloat16),
        ),
        in_specs=[held] * 2,
        out_specs=(held,) * 4,
        scratch_shapes=[pltpu.VMEM(arrived.shape, jnp.float32)],
        compiler_params=pltpu.CompilerParams(vmem_limit_bytes=8 * MIB),
    )(arrived, choose)


def long_step(before, sent, got, inner_ref, outer_ref, gain_ref, layer):
    features = before.shape[1]
    total = dot(before, inner_ref[layer, :features, :])
    total += dot(sent, inner_ref[layer, features : 2 * features, :])
    total += dot(got, inner_ref[layer, 2 * features :, :])
    return finish(before, total, outer_ref[layer], gain_ref[layer : layer + 1, :])


def coarse_layer(layer, long_rows, sends, recvs, adds, choose, pieces, latents, fine_sum,
                 edge_inner, edge_outer, edge_gain, node_inner, node_outer, node_gain, coarse_count):
    slots = long_rows.shape[0]
    nodes, features = latents.shape
    count = len(pieces)
    each = pieces[0].shape[0]
    table_rows = count * each

    def body(long_ref, sends_ref, recvs_ref, adds_ref, choose_ref, latents_ref, sum_ref,
             ei_ref, eo_ref, eg_ref, ni_ref, no_ref, ng_ref, *rest):
        piece_refs = rest[:count]
        long_next_ref, next_ref, own_ref, table, ni, no, sems = rest[count:]
        weights = [
            pltpu.make_async_copy(ni_ref.at[layer], ni, sems.at[0]),
            pltpu.make_async_copy(no_ref.at[layer], no, sems.at[1]),
        ]
        for copy in weights:
            copy.start()
        for p in range(count):
            table[p * each : (p + 1) * each, :] = piece_refs[p][...]
        sent = dot(sends_ref[...], table[...]).astype(jnp.bfloat16)
        got = dot(recvs_ref[...], table[:TAGS, :]).astype(jnp.bfloat16)
        after = long_step(long_ref[...], sent, got, ei_ref, eo_ref, eg_ref, layer)
        long_next_ref[...] = after
        incoming = (sum_ref[...] + dot(adds_ref[...], after)).astype(jnp.bfloat16)
        old = latents_ref[...]
        for copy in weights:
            copy.wait()
        total = dot(old, ni[:features, :]) + dot(incoming, ni[features:, :])
        new = finish(old, total, no[...], ng_ref[layer : layer + 1, :])
        next_ref[...] = new
        own_ref[...] = dot(choose_ref[...], new)[:coarse_count].astype(jnp.bfloat16)

    held = pl.BlockSpec(memory_space=pltpu.VMEM)
    away = pl.BlockSpec(memory_space=pl.ANY)
    return pl.pallas_call(
        body,
        name=f"coarse{layer}",
        out_shape=(
            jax.ShapeDtypeStruct((slots, features), jnp.bfloat16),
            jax.ShapeDtypeStruct(latents.shape, jnp.bfloat16),
            jax.ShapeDtypeStruct((coarse_count, features), jnp.bfloat16),
            jax.ShapeDtypeStruct((table_rows, features), jnp.bfloat16),
        ),
        in_specs=[held] * 10 + [away] * 2 + [held] * (1 + count),
        out_specs=(held,) * 4,
        scratch_shapes=[
            pltpu.VMEM(node_inner.shape[1:], jnp.bfloat16),
            pltpu.VMEM(node_outer.shape[1:], jnp.bfloat16),
            pltpu.SemaphoreType.DMA((2,)),
        ],
        compiler_params=pltpu.CompilerParams(vmem_limit_bytes=14 * MIB),
    )(long_rows, sends, recvs, adds, choose, latents, fine_sum,
      edge_inner, edge_outer, edge_gain, node_inner, node_outer, node_gain, *pieces)


def own_layer(layer, long_rows, tags, table, edge_inner, edge_outer, edge_gain):
    def body(long_ref, tag_ref, table_ref, ei_ref, eo_ref, eg_ref, next_ref):
        rows = table_ref.shape[0]
        numbers = tag_ref[...].astype(jnp.float32)
        sent = dot(pick(decode(numbers, 0), rows), table_ref[...]).astype(jnp.bfloat16)
        got = dot(pick(decode(numbers, 2), rows), table_ref[...]).astype(jnp.bfloat16)
        next_ref[...] = long_step(long_ref[...], sent, got, ei_ref, eo_ref, eg_ref, layer)

    held = pl.BlockSpec(memory_space=pltpu.VMEM)
    return pl.pallas_call(
        body,
        name=f"own{layer}",
        out_shape=jax.ShapeDtypeStruct(long_rows.shape, jnp.bfloat16),
        in_specs=[held] * 6,
        out_specs=held,
        compiler_params=pltpu.CompilerParams(vmem_limit_bytes=10 * MIB),
    )(long_rows, tags, table, edge_inner, edge_outer, edge_gain)


def shards(
    node_latents,
    fine_edges,
    long_edges,
    neighbours,
    coarse_slots,
    long_senders,
    long_receivers,
    edge_inner,
    edge_outer,
    edge_gain,
    node_inner,
    node_outer,
    node_gain,
):
    rows, columns, features = node_latents.shape
    degree = fine_edges.shape[2]
    nodes = rows * columns
    coarse_count = coarse_slots.shape[0]
    layers = edge_inner.shape[0]
    devices = lax.axis_size("px") * lax.axis_size("py")

    latents = node_latents.transpose(1, 0, 2).reshape(nodes, features)
    fine = fine_edges.transpose(1, 2, 0, 3).reshape(nodes * degree, features)
    own, choose = coarse_start(coarse_slots[None, :], latents, rows, columns)
    own_rows = long_edges
    me = lax.axis_index(AXES).reshape(1)
    payload, own_tags = pack_edges(long_edges, long_senders[None, :], long_receivers[None, :], me, coarse_count, devices)
    for layer in range(layers):
        grid = latents.reshape(columns, rows, features)
        joined = jnp.concatenate(stage(own, DIGITS[0]), axis=0)
        left = along(grid[-1], "py", 1)
        right = along(grid[0], "py", -1)
        if layer == 0:
            packed = payload.reshape(devices, 16, TAGS)
            arrived = lax.all_to_all(packed, AXES, split_axis=0, concat_axis=0, tiled=True).reshape(payload.shape)
        joined, left, right, payload = tie(joined, left, right, payload)
        high = jnp.concatenate([left[-1:], grid[:, -1], right[-1:]], axis=0)
        low = jnp.concatenate([left[:1], grid[:, 0], right[:1]], axis=0)
        joined = jnp.concatenate(stage(joined, DIGITS[1]), axis=0)
        above = along(high, "px", 1)
        below = along(low, "px", -1)
        joined, above, below, arrived, own_rows, neighbours = tie(joined, above, below, arrived, own_rows, neighbours)
        pieces = stage(joined, DIGITS[2])
        if layer == 0:
            long_rows, sends, recvs, adds = unpack_edges(arrived, choose, features, 2 * len(pieces) * joined.shape[0])
            picks = selection(neighbours)
        else:
            own_rows = own_layer(layer - 1, own_rows, own_tags, table, edge_inner, edge_outer, edge_gain)
        fine, fine_sum = fine_layer(
            layer, fine, picks, latents, left, right, above, below, edge_inner, edge_outer, edge_gain, rows
        )
        first, *others, fine_sum, own_rows, long_rows = tie(*pieces, fine_sum, own_rows, long_rows)
        pieces = [first] + others
        pieces = pieces + [shift(piece, CORE, 1) for piece in pieces]
        long_rows, latents, own, table = coarse_layer(
            layer, long_rows, sends, recvs, adds, choose, pieces, latents, fine_sum,
            edge_inner, edge_outer, edge_gain, node_inner, node_outer, node_gain, coarse_count,
        )
    own_rows = own_layer(layers - 1, own_rows, own_tags, table, edge_inner, edge_outer, edge_gain)
    return (
        latents.reshape(columns, rows, features).transpose(1, 0, 2),
        fine.reshape(columns, degree, rows, features).transpose(2, 0, 1, 3),
        own_rows,
    )


def solution(mesh):
    in_specs = (
        P("px", "py", None),
        P("px", "py", None, None),
        P(AXES, None),
        P("px", "py", None),
        P(AXES),
        P(AXES),
        P(AXES),
        P(),
        P(),
        P(),
        P(),
        P(),
        P(),
    )
    out_specs = (P("px", "py", None), P("px", "py", None, None), P(AXES, None))
    return jax.shard_map(shards, mesh=mesh, in_specs=in_specs, out_specs=out_specs, check_vma=False)
```

```python
import jax
import jax.numpy as jnp
from jax import lax
from jax.experimental import pallas as pl
from jax.experimental.pallas import tpu as pltpu
from jax.sharding import PartitionSpec as P

EPSILON = 1e-05
AXES = ("px", "py")
RING = 16
Z, CORE = (2, 4), (1, 2)
BAND = 4
TAGS = 128
LOW = 64
CAP = 3
ABOVE, BELOW = 160, 192
MIB = 1024 * 1024


def shift(values, digit, step):
    stride, size = digit
    pairs = []
    for i in range(8):
        here = i // stride % size
        pairs.append((i, i + ((here + step) % size - here) * stride))
    return lax.ppermute(values, "py", pairs)


def tie(*values):
    return lax.optimization_barrier(values)


def table_row(px, py, coarse, coarse_count):
    home = jnp.floor((coarse.astype(jnp.float32) + 0.5) * (1.0 / coarse_count)).astype(jnp.int32)
    row = coarse - home * coarse_count
    away = (px - lax.shift_right_logical(home, 3)) & (RING - 1)
    near, far = away & 3, lax.shift_right_logical(away + 1, 2) & 3
    home_z, home_core = lax.shift_right_logical(home, 1) & 3, home & 1
    kz = (lax.shift_right_logical(py, 1) - home_z) & 3
    kc = (py - home_core) & 1
    return (((kc * 4 + kz) * 4 + far) * 4 + near) * coarse_count + row, home


def along(values, axis, step):
    count = lax.axis_size(axis)
    return lax.ppermute(values, axis, [(i, (i + step) % count) for i in range(count)])


def selection(neighbours):
    rows, columns, degree = neighbours.shape

    def body(codes_ref, picks_ref):
        codes = codes_ref[...]
        q = codes + (codes >= 4).astype(jnp.int32)
        down = (q >= 3).astype(jnp.int32) + (q >= 6).astype(jnp.int32)
        step = q - 3 * down
        from_row = lax.broadcasted_iota(jnp.int32, codes.shape, 1) + down - 1
        column = lax.broadcasted_iota(jnp.int32, codes.shape, 2)
        from_column = column + step - 1
        near = ((column & (BAND - 1)) + step) * rows + from_row
        outer = jnp.where(from_column < 0, columns, jnp.where(from_column >= columns, columns + 1, from_column))
        sender = jnp.where(from_row < 0, ABOVE + outer, jnp.where(from_row >= rows, BELOW + outer, near))
        lanes = lax.broadcasted_iota(jnp.int32, (rows, 256), 1)
        row = lax.broadcasted_iota(jnp.int32, (rows, 256), 0)
        for c in range(columns):
            receiver = lanes == (BAND + 2 + c % BAND) * rows + row
            for k in range(degree):
                picks = (lanes == sender[k, :, c : c + 1]) | receiver
                picks_ref[(c * degree + k) * rows : (c * degree + k + 1) * rows, :] = picks.astype(jnp.bfloat16)

    held = pl.BlockSpec(memory_space=pltpu.VMEM)
    return pl.pallas_call(
        body,
        name="selection",
        out_shape=jax.ShapeDtypeStruct((rows * columns * degree, 256), jnp.bfloat16),
        in_specs=[held],
        out_specs=held,
        compiler_params=pltpu.CompilerParams(vmem_limit_bytes=4 * MIB),
    )(neighbours.transpose(2, 0, 1))


def dot(a, b):
    return jnp.dot(a, b, preferred_element_type=jnp.float32)


def finish(before, inner_sum, outer, gains):
    hidden = jax.nn.silu(inner_sum).astype(jnp.bfloat16)
    output = dot(hidden, outer)
    center = output - jnp.mean(output, axis=-1, keepdims=True)
    spread_of = jnp.mean(center * center, axis=-1, keepdims=True)
    scaled = center * lax.rsqrt(spread_of + EPSILON) * gains
    return (before.astype(jnp.float32) + scaled).astype(jnp.bfloat16)


def fine_layer(layer, fine, picks, latents, left, right, sides, inner, outer, gain, rows, columns):
    edges, features = fine.shape
    nodes = latents.shape[0]
    hidden = inner.shape[2]
    near = (BAND + 2) * rows
    own = BAND * rows
    steps = nodes // own
    block = edges // steps
    degree = edges // nodes

    def body(fine_ref, picks_ref, latents_ref, left_ref, right_ref, sides_ref, inner_ref, outer_ref, gain_ref,
             next_ref, sum_ref, send_ref, recv_ref, table_ref):
        step = pl.program_id(0)

        @pl.when(step == 0)
        def _():
            send = inner_ref[layer, features : 2 * features, :]
            project = lambda ref: dot(ref[...], send).astype(jnp.bfloat16)
            table_ref[ABOVE : ABOVE + sides.shape[0], :] = project(sides_ref)
            table_ref[ABOVE + sides.shape[0] :, :] = jnp.zeros((256 - ABOVE - sides.shape[0], hidden), jnp.bfloat16)
            send_ref[rows : rows + nodes, :] = project(latents_ref)
            recv_ref[...] = dot(latents_ref[...], inner_ref[layer, 2 * features :, :]).astype(jnp.bfloat16)
            side = project(left_ref)
            send_ref[:rows, :] = side[:rows]
            table_ref[ABOVE + columns : ABOVE + columns + 1, :] = side[rows : rows + 1]
            table_ref[BELOW + columns : BELOW + columns + 1, :] = side[rows + 1 : rows + 2]
            side = project(right_ref)
            send_ref[rows + nodes :, :] = side[:rows]
            table_ref[ABOVE + columns + 1 : ABOVE + columns + 2, :] = side[rows : rows + 1]
            table_ref[BELOW + columns + 1 : BELOW + columns + 2, :] = side[rows + 1 : rows + 2]

        start = pl.multiple_of(step * own, own)
        table_ref[:near, :] = send_ref[pl.ds(start, near), :]
        table_ref[near : near + own, :] = recv_ref[pl.ds(start, own), :]
        before = fine_ref[...]
        total = dot(before, inner_ref[layer, :features, :]) + dot(picks_ref[...], table_ref[...])
        after = finish(before, total, outer_ref[layer], gain_ref[layer : layer + 1, :])
        next_ref[...] = after
        split = after.astype(jnp.float32).reshape(BAND, degree, rows, features)
        sum_ref[...] = jnp.sum(split, axis=1).reshape(own, features)

    held = pl.BlockSpec(memory_space=pltpu.VMEM)
    return pl.pallas_call(
        body,
        name=f"fine{layer}",
        out_shape=(
            jax.ShapeDtypeStruct(fine.shape, jnp.bfloat16),
            jax.ShapeDtypeStruct((nodes, features), jnp.float32),
        ),
        grid=(steps,),
        in_specs=[
            pl.BlockSpec((block, features), lambda i: (i, 0)),
            pl.BlockSpec((block, 256), lambda i: (i, 0)),
        ]
        + [held] * 7,
        out_specs=(
            pl.BlockSpec((block, features), lambda i: (i, 0)),
            pl.BlockSpec((own, features), lambda i: (i, 0)),
        ),
        scratch_shapes=[
            pltpu.VMEM((nodes + 2 * rows, hidden), jnp.bfloat16),
            pltpu.VMEM((nodes, hidden), jnp.bfloat16),
            pltpu.VMEM((256, hidden), jnp.bfloat16),
        ],
        compiler_params=pltpu.CompilerParams(dimension_semantics=("arbitrary",), vmem_limit_bytes=14 * MIB),
    )(fine, picks, latents, left, right, sides, inner, outer, gain)


def pick(index, width):
    lanes = lax.broadcasted_iota(jnp.int32, (index.shape[0], width), 1)
    return (lanes == index).astype(jnp.bfloat16)


def rows_to_columns(left, right):
    return lax.dot_general(left, right, (((1,), (1,)), ((), ())), preferred_element_type=jnp.float32)


def decode(tags, at):
    numbers = tags.astype(jnp.int32)
    return jnp.where(numbers[:, 4:5] > 0, numbers[:, at : at + 1] * LOW + numbers[:, at + 1 : at + 2], -1)


def blocks_of(*arrays):
    return [pl.BlockSpec(a.shape, lambda i, n=len(a.shape): (0,) * n) for a in arrays]


def send_rows(both, up_ref, down_ref, own_ref):
    half, count = up_ref.shape[0], own_ref.shape[0]
    rows = both.astype(jnp.bfloat16)
    up_ref[...] = rows[:half]
    down_ref[...] = rows[half:]
    own_ref[...] = rows[:count]


def join(own, up, two, down, latents, rows):
    count, features = own.shape
    columns = up.shape[0] - count

    def body(own_ref, up_ref, two_ref, down_ref, latents_ref, joined_ref, last_ref, first_ref, sides_ref):
        for at, ref in enumerate((own_ref, up_ref, two_ref, down_ref)):
            joined_ref[at * count : (at + 1) * count, :] = ref[:count, :]
        last_ref[:rows, :] = latents_ref[-rows:, :]
        last_ref[rows : rows + 1, :] = up_ref[-1:, :]
        last_ref[rows + 1 :, :] = down_ref[-1:, :]
        first_ref[:rows, :] = latents_ref[:rows, :]
        first_ref[rows : rows + 1, :] = up_ref[count : count + 1, :]
        first_ref[rows + 1 :, :] = down_ref[count : count + 1, :]
        sides_ref[...] = jnp.zeros(sides_ref.shape, jnp.bfloat16)
        sides_ref[:columns, :] = up_ref[count:, :]
        sides_ref[BELOW - ABOVE : BELOW - ABOVE + columns, :] = down_ref[count:, :]

    held = pl.BlockSpec(memory_space=pltpu.VMEM)
    return pl.pallas_call(
        body,
        name="join",
        out_shape=tuple(jax.ShapeDtypeStruct((n, features), jnp.bfloat16) for n in (4 * count, rows + 2, rows + 2, 256 - ABOVE - 32)),
        in_specs=[held] * 5,
        out_specs=(held,) * 4,
        compiler_params=pltpu.CompilerParams(vmem_limit_bytes=2 * MIB),
    )(own, up, two, down, latents)


def coarse_start(coarse_slots, latents, rows, columns):
    count = coarse_slots.shape[1]
    nodes, features = latents.shape
    half = count + columns

    def body(slots_ref, latents_ref, up_ref, down_ref, own_ref, choose_ref):
        slot = slots_ref[...]
        row = jnp.floor((slot.astype(jnp.float32) + 0.5) * (1.0 / columns)).astype(jnp.int32)
        at = (slot - row * columns) * rows + row
        place = (lax.broadcasted_iota(jnp.int32, (nodes, count), 0) == at).astype(jnp.bfloat16)
        out = lax.broadcasted_iota(jnp.int32, (2 * half, count), 0)
        line = lax.broadcasted_iota(jnp.int32, (2 * half, count), 1)
        same = ((out == line) | (out == line + half)).astype(jnp.bfloat16)
        out = lax.broadcasted_iota(jnp.int32, (2 * half, nodes), 0)
        node = lax.broadcasted_iota(jnp.int32, (2 * half, nodes), 1)
        edge = ((out >= count) & (out < half) & (node == (out - count) * rows + rows - 1)) | (
            (out >= half + count) & (node == (out - half - count) * rows)
        )
        choose = (rows_to_columns(same, place) + edge.astype(jnp.float32)).astype(jnp.bfloat16)
        choose_ref[...] = choose
        send_rows(dot(choose, latents_ref[...]), up_ref, down_ref, own_ref)

    shapes = (
        *(jax.ShapeDtypeStruct((n, features), jnp.bfloat16) for n in (half, half, count)),
        jax.ShapeDtypeStruct((2 * half, nodes), jnp.bfloat16),
    )
    return pl.pallas_call(
        body,
        name="coarse_start",
        out_shape=shapes,
        grid=(1,),
        in_specs=blocks_of(coarse_slots, latents),
        out_specs=blocks_of(*shapes),
        compiler_params=pltpu.CompilerParams(vmem_limit_bytes=4 * MIB),
    )(coarse_slots, latents)


def pack_edges(long_edges, senders, receivers, me, coarse_count, devices):
    count, features = long_edges.shape
    blocks = features // TAGS
    slots = devices * CAP

    def body(me_ref, long_ref, send_ref, recv_ref, sent_ref, mine_ref, wide):
        send, recv = send_ref[...], recv_ref[...]
        _, owner = table_row(0, 0, recv, coarse_count)
        here = (lax.shift_right_logical(me_ref[0], 3), me_ref[0] & 7)
        there = (lax.shift_right_logical(owner, 3), owner & 7)
        field = lax.broadcasted_iota(jnp.int32, (TAGS, count), 0)

        def fields(digits):
            sender = table_row(*digits, send, coarse_count)[0]
            receiver = table_row(*digits, recv, coarse_count)[0]
            both = jnp.where(field < 2, sender, receiver)
            high = lax.shift_right_logical(both, LOW.bit_length() - 1)
            value = jnp.where(field % 2 == 0, high, both & (LOW - 1))
            value = jnp.where(field == 4, 1, jnp.where(field == 5, owner, value))
            return jnp.where(field < 6, value, 0).astype(jnp.float32).astype(jnp.bfloat16)

        down = lax.broadcasted_iota(jnp.int32, (count, count), 0)
        across = lax.broadcasted_iota(jnp.int32, (count, count), 1)
        mine = rows_to_columns((down == across).astype(jnp.bfloat16), fields(here))
        mine_ref[...] = mine.astype(jnp.bfloat16)
        same = (mine[:, 5:6].astype(jnp.int32) == owner) & (down < across)
        rank = jnp.sum(same.astype(jnp.float32), axis=0, keepdims=True).astype(jnp.int32)
        spot = rank * devices + owner
        place = (lax.broadcasted_iota(jnp.int32, (slots, count), 0) == spot).astype(jnp.bfloat16)
        edges = dot(place, long_ref[...])
        tags = rows_to_columns(place, fields(there))
        for j in range(CAP):
            part = slice(j * devices, (j + 1) * devices)
            for b in range(blocks):
                wide[pl.ds(j * blocks + b, devices, stride=16), :] = edges[part, b * TAGS : (b + 1) * TAGS]
            wide[pl.ds(CAP * blocks + j, devices, stride=16), :] = tags[part]
        wide[pl.ds(15, devices, stride=16), :] = jnp.zeros((devices, TAGS), jnp.float32)
        sent_ref[...] = wide[...].astype(jnp.bfloat16)

    shapes = (
        jax.ShapeDtypeStruct((devices * 16, TAGS), jnp.bfloat16),
        jax.ShapeDtypeStruct((count, TAGS), jnp.bfloat16),
    )
    return pl.pallas_call(
        body,
        name="pack_edges",
        out_shape=shapes,
        grid=(1,),
        in_specs=[pl.BlockSpec(memory_space=pltpu.SMEM)] + blocks_of(long_edges, senders, receivers),
        out_specs=blocks_of(*shapes),
        scratch_shapes=[pltpu.VMEM((devices * 16, TAGS), jnp.float32)],
        compiler_params=pltpu.CompilerParams(vmem_limit_bytes=8 * MIB),
    )(me, long_edges, senders, receivers)


def unpack_edges(arrived, own_tags, choose, features, table_rows, coarse_count):
    devices = arrived.shape[0] // 16
    blocks = features // TAGS
    slots = devices * CAP
    count = own_tags.shape[0]
    nodes = choose.shape[1]

    def body(arrived_ref, tags_ref, choose_ref, rows_ref, send_ref, recv_ref, adds_ref, wide):
        wide[...] = arrived_ref[...].astype(jnp.float32)
        for j in range(CAP):
            part = slice(j * devices, (j + 1) * devices)
            for b in range(blocks):
                lanes = slice(b * TAGS, (b + 1) * TAGS)
                rows_ref[part, lanes] = wide[pl.ds(j * blocks + b, devices, stride=16), :].astype(jnp.bfloat16)
            tags = wide[pl.ds(CAP * blocks + j, devices, stride=16), :]
            send_ref[part, :] = pick(decode(tags, 0), table_rows)
            recv_ref[part, :] = pick(decode(tags, 2), TAGS)
        mine = tags_ref[...].astype(jnp.float32)
        send_ref[slots : slots + count, :] = pick(decode(mine, 0), table_rows)
        send_ref[slots + count :, :] = pick(decode(mine, 2), table_rows)
        here = recv_ref[:, :coarse_count]
        place = lax.dot_general(
            choose_ref[:coarse_count, :], here, (((0,), (1,)), ((), ())), preferred_element_type=jnp.float32
        )
        adds_ref[...] = place.astype(jnp.bfloat16)

    held = pl.BlockSpec(memory_space=pltpu.VMEM)
    return pl.pallas_call(
        body,
        name="unpack_edges",
        out_shape=(
            jax.ShapeDtypeStruct((slots, features), jnp.bfloat16),
            jax.ShapeDtypeStruct((slots + 2 * count, table_rows), jnp.bfloat16),
            jax.ShapeDtypeStruct((slots, TAGS), jnp.bfloat16),
            jax.ShapeDtypeStruct((nodes, slots), jnp.bfloat16),
        ),
        in_specs=[held] * 3,
        out_specs=(held,) * 4,
        scratch_shapes=[pltpu.VMEM(arrived.shape, jnp.float32)],
        compiler_params=pltpu.CompilerParams(vmem_limit_bytes=8 * MIB),
    )(arrived, own_tags, choose)


def long_step(before, sent, got, inner_ref, outer_ref, gain_ref, layer):
    features = before.shape[1]
    total = dot(before, inner_ref[layer, :features, :])
    total += dot(sent, inner_ref[layer, features : 2 * features, :])
    total += dot(got, inner_ref[layer, 2 * features :, :])
    return finish(before, total, outer_ref[layer], gain_ref[layer : layer + 1, :])


def coarse_layer(layer, long_rows, own_rows, sends, recvs, adds, choose, pieces, latents, fine_sum,
                 edge_inner, edge_outer, edge_gain, node_inner, node_outer, node_gain, coarse_count, last):
    slots = long_rows.shape[0]
    nodes, features = latents.shape
    count = len(pieces)
    each = pieces[0].shape[0]
    table_rows = count * each
    both = slots + own_rows.shape[0]

    def body(long_ref, own_ref, sends_ref, recvs_ref, adds_ref, choose_ref, latents_ref, sum_ref,
             ei_ref, eo_ref, eg_ref, ni_ref, no_ref, ng_ref, *rest):
        piece_refs = rest[:count]
        next_ref, *outs, ni, no, sems = rest[count:]
        table = outs[1] if last else outs[4]
        weights = [
            pltpu.make_async_copy(ni_ref.at[layer], ni, sems.at[0]),
            pltpu.make_async_copy(no_ref.at[layer], no, sems.at[1]),
        ]
        for copy in weights:
            copy.start()
        for p in range(count):
            table[p * each : (p + 1) * each, :] = piece_refs[p][...]
        got = dot(recvs_ref[...], table[:TAGS, :]).astype(jnp.bfloat16)
        if last:
            picked = dot(sends_ref[...], table[...]).astype(jnp.bfloat16)
            before = jnp.concatenate([long_ref[...], own_ref[...]], axis=0)
            got = jnp.concatenate([got, picked[both:]], axis=0)
            after = long_step(before, picked[:both], got, ei_ref, eo_ref, eg_ref, layer)
            outs[0][...] = after[slots:]
            after = after[:slots]
        else:
            sent = dot(sends_ref[:slots, :], table[...]).astype(jnp.bfloat16)
            after = long_step(long_ref[...], sent, got, ei_ref, eo_ref, eg_ref, layer)
            outs[0][...] = after
        incoming = (sum_ref[...] + dot(adds_ref[...], after)).astype(jnp.bfloat16)
        old = latents_ref[...]
        for copy in weights:
            copy.wait()
        total = dot(old, ni[:features, :]) + dot(incoming, ni[features:, :])
        new = finish(old, total, no[...], ng_ref[layer : layer + 1, :])
        next_ref[...] = new
        if not last:
            send_rows(dot(choose_ref[...], new), *outs[1:4])

    held = pl.BlockSpec(memory_space=pltpu.VMEM)
    away = pl.BlockSpec(memory_space=pl.ANY)
    table_shape = (table_rows, features)
    half = choose.shape[0] // 2
    kept = (both - slots,) if last else (slots, half, half, coarse_count, table_rows)
    shapes = [jax.ShapeDtypeStruct((n, features), jnp.bfloat16) for n in (nodes, *kept)]

    return pl.pallas_call(
        body,
        name=f"coarse{layer}",
        out_shape=tuple(shapes),
        in_specs=[held] * 11 + [away] * 2 + [held] * (1 + count),
        out_specs=(held,) * len(shapes),
        scratch_shapes=([pltpu.VMEM(table_shape, jnp.bfloat16)] if last else [])
        + [
            pltpu.VMEM(node_inner.shape[1:], jnp.bfloat16),
            pltpu.VMEM(node_outer.shape[1:], jnp.bfloat16),
            pltpu.SemaphoreType.DMA((2,)),
        ],
        compiler_params=pltpu.CompilerParams(vmem_limit_bytes=(18 if last else 14) * MIB),
    )(long_rows, own_rows, sends, recvs, adds, choose, latents, fine_sum,
      edge_inner, edge_outer, edge_gain, node_inner, node_outer, node_gain, *pieces)


def own_layer(layer, long_rows, sends, table, edge_inner, edge_outer, edge_gain):
    count = long_rows.shape[0]

    def body(long_ref, sends_ref, table_ref, ei_ref, eo_ref, eg_ref, next_ref):
        picked = dot(sends_ref[-2 * count :, :], table_ref[...]).astype(jnp.bfloat16)
        next_ref[...] = long_step(long_ref[...], picked[:count], picked[count:], ei_ref, eo_ref, eg_ref, layer)

    held = pl.BlockSpec(memory_space=pltpu.VMEM)
    return pl.pallas_call(
        body,
        name=f"own{layer}",
        out_shape=jax.ShapeDtypeStruct(long_rows.shape, jnp.bfloat16),
        in_specs=[held] * 6,
        out_specs=held,
        compiler_params=pltpu.CompilerParams(vmem_limit_bytes=8 * MIB),
    )(long_rows, sends, table, edge_inner, edge_outer, edge_gain)


def shards(
    node_latents,
    fine_edges,
    long_edges,
    neighbours,
    coarse_slots,
    long_senders,
    long_receivers,
    edge_inner,
    edge_outer,
    edge_gain,
    node_inner,
    node_outer,
    node_gain,
):
    rows, columns, features = node_latents.shape
    degree = fine_edges.shape[2]
    nodes = rows * columns
    coarse_count = coarse_slots.shape[0]
    layers = edge_inner.shape[0]
    devices = lax.axis_size("px") * lax.axis_size("py")

    latents = node_latents.transpose(1, 0, 2).reshape(nodes, features)
    fine = fine_edges.transpose(1, 2, 0, 3).reshape(nodes * degree, features)
    up, down, own, choose = coarse_start(coarse_slots[None, :], latents, rows, columns)
    long_edges, own = tie(long_edges, own)
    own_rows = long_edges
    me = lax.axis_index(AXES).reshape(1)
    payload, own_tags = pack_edges(long_edges, long_senders[None, :], long_receivers[None, :], me, coarse_count, devices)
    for layer in range(layers):
        last = layer == layers - 1
        up = along(up, "px", 1)
        down = along(down, "px", -1)
        two = along(own, "px", 2)
        if layer == 0:
            two, payload = tie(two, payload)
            packed = payload.reshape(devices, 16, TAGS)
            arrived = lax.all_to_all(packed, AXES, split_axis=0, concat_axis=0, tiled=True).reshape(payload.shape)
        joined, to_right, to_left, sides = join(own, up, two, down, latents, rows)
        joined = jnp.concatenate([joined] + [along(joined, "px", 4 * s) for s in (1, 2, 3)], axis=0)
        joined, to_right, to_left, own_rows = tie(joined, to_right, to_left, own_rows)
        pieces = [joined] + [shift(joined, Z, s) for s in (1, 2, 3)]
        left = along(to_right, "py", 1)
        right = along(to_left, "py", -1)
        if layer == 0:
            table_rows = 2 * len(pieces) * joined.shape[0]
            long_rows, sends, recvs, adds = unpack_edges(arrived, own_tags, choose, features, table_rows, coarse_count)
            left, long_rows, neighbours = tie(left, long_rows, neighbours)
            picks = selection(neighbours)
        else:
            own_rows = own_layer(layer - 1, own_rows, sends, table, edge_inner, edge_outer, edge_gain)
        fine, fine_sum = fine_layer(
            layer, fine, picks, latents, left, right, sides, edge_inner, edge_outer, edge_gain, rows, columns
        )
        first, *others, fine_sum, own_rows, long_rows = tie(*pieces, fine_sum, own_rows, long_rows)
        pieces = [first] + others
        pieces = pieces + [shift(piece, CORE, 1) for piece in pieces]
        latents, *rest = coarse_layer(
            layer, long_rows, own_rows, sends, recvs, adds, choose, pieces, latents, fine_sum,
            edge_inner, edge_outer, edge_gain, node_inner, node_outer, node_gain, coarse_count, last,
        )
        if last:
            own_rows = rest[0]
        else:
            long_rows, up, down, own, table = rest
    return (
        latents.reshape(columns, rows, features).transpose(1, 0, 2),
        fine.reshape(columns, degree, rows, features).transpose(2, 0, 1, 3),
        own_rows,
    )


def solution(mesh):
    in_specs = (
        P("px", "py", None),
        P("px", "py", None, None),
        P(AXES, None),
        P("px", "py", None),
        P(AXES),
        P(AXES),
        P(AXES),
        P(),
        P(),
        P(),
        P(),
        P(),
        P(),
    )
    out_specs = (P("px", "py", None), P("px", "py", None, None), P(AXES, None))
    return jax.shard_map(shards, mesh=mesh, in_specs=in_specs, out_specs=out_specs, check_vma=False)
```

```python
import jax
import jax.numpy as jnp
from jax import lax
from jax.experimental import pallas as pl
from jax.experimental.pallas import tpu as pltpu
from jax.sharding import PartitionSpec as P

EPSILON = 1e-05
AXES = ("px", "py")
RING = 16
Z, CORE = (2, 4), (1, 2)
BAND = 4
TAGS = 128
LOW = 64
CAP = 3
ABOVE, BELOW = 160, 192
MIB = 1024 * 1024


def shift(values, digit, step):
    stride, size = digit
    pairs = []
    for i in range(8):
        here = i // stride % size
        pairs.append((i, i + ((here + step) % size - here) * stride))
    return lax.ppermute(values, "py", pairs)


def tie(*values):
    return lax.optimization_barrier(values)


def table_row(px, py, coarse, coarse_count):
    home = jnp.floor((coarse.astype(jnp.float32) + 0.5) * (1.0 / coarse_count)).astype(jnp.int32)
    row = coarse - home * coarse_count
    away = (px - lax.shift_right_logical(home, 3)) & (RING - 1)
    near, far = away & 3, lax.shift_right_logical(away + 1, 2) & 3
    home_z, home_core = lax.shift_right_logical(home, 1) & 3, home & 1
    kz = (lax.shift_right_logical(py, 1) - home_z) & 3
    kc = (py - home_core) & 1
    return (((kc * 4 + kz) * 4 + near) * 4 + far) * coarse_count + row, home


def along(values, axis, step):
    count = lax.axis_size(axis)
    return lax.ppermute(values, axis, [(i, (i + step) % count) for i in range(count)])


def selection(neighbours):
    rows, columns, degree = neighbours.shape

    def body(codes_ref, picks_ref):
        codes = codes_ref[...]
        q = codes + (codes >= 4).astype(jnp.int32)
        down = (q >= 3).astype(jnp.int32) + (q >= 6).astype(jnp.int32)
        step = q - 3 * down
        from_row = lax.broadcasted_iota(jnp.int32, codes.shape, 1) + down - 1
        column = lax.broadcasted_iota(jnp.int32, codes.shape, 2)
        near = ((column & (BAND - 1)) + step) * rows + from_row
        sender = jnp.where(from_row < 0, ABOVE + column + step, jnp.where(from_row >= rows, BELOW + column + step, near))
        lanes = lax.broadcasted_iota(jnp.int32, (rows, 256), 1)
        row = lax.broadcasted_iota(jnp.int32, (rows, 256), 0)
        for c in range(columns):
            receiver = lanes == (BAND + 2 + c % BAND) * rows + row
            for k in range(degree):
                picks = (lanes == sender[k, :, c : c + 1]) | receiver
                picks_ref[(c * degree + k) * rows : (c * degree + k + 1) * rows, :] = picks.astype(jnp.bfloat16)

    held = pl.BlockSpec(memory_space=pltpu.VMEM)
    return pl.pallas_call(
        body,
        name="selection",
        out_shape=jax.ShapeDtypeStruct((rows * columns * degree, 256), jnp.bfloat16),
        in_specs=[held],
        out_specs=held,
        compiler_params=pltpu.CompilerParams(vmem_limit_bytes=4 * MIB),
    )(neighbours.transpose(2, 0, 1))


def dot(a, b):
    return jnp.dot(a, b, preferred_element_type=jnp.float32)


def finish(before, inner_sum, outer, gains):
    hidden = jax.nn.silu(inner_sum).astype(jnp.bfloat16)
    output = dot(hidden, outer)
    center = output - jnp.mean(output, axis=-1, keepdims=True)
    spread_of = jnp.mean(center * center, axis=-1, keepdims=True)
    scaled = center * lax.rsqrt(spread_of + EPSILON) * gains
    return (before.astype(jnp.float32) + scaled).astype(jnp.bfloat16)


def fine_layer(layer, fine, picks, latents, left, right, sides, inner, outer, gain, rows):
    edges, features = fine.shape
    nodes = latents.shape[0]
    hidden = inner.shape[2]
    near = (BAND + 2) * rows
    own = BAND * rows
    steps = nodes // own
    block = edges // steps
    degree = edges // nodes

    def body(fine_ref, picks_ref, latents_ref, left_ref, right_ref, sides_ref, inner_ref, outer_ref, gain_ref,
             next_ref, sum_ref, send_ref, recv_ref, table_ref):
        step = pl.program_id(0)

        @pl.when(step == 0)
        def _():
            send = inner_ref[layer, features : 2 * features, :]
            project = lambda ref: dot(ref[...], send).astype(jnp.bfloat16)
            table_ref[ABOVE : ABOVE + sides.shape[0], :] = project(sides_ref)
            table_ref[ABOVE + sides.shape[0] :, :] = jnp.zeros((256 - ABOVE - sides.shape[0], hidden), jnp.bfloat16)
            send_ref[rows : rows + nodes, :] = project(latents_ref)
            recv_ref[...] = dot(latents_ref[...], inner_ref[layer, 2 * features :, :]).astype(jnp.bfloat16)
            send_ref[:rows, :] = project(left_ref)
            send_ref[rows + nodes :, :] = project(right_ref)

        start = pl.multiple_of(step * own, own)
        table_ref[:near, :] = send_ref[pl.ds(start, near), :]
        table_ref[near : near + own, :] = recv_ref[pl.ds(start, own), :]
        before = fine_ref[...]
        total = dot(before, inner_ref[layer, :features, :]) + dot(picks_ref[...], table_ref[...])
        after = finish(before, total, outer_ref[layer], gain_ref[layer : layer + 1, :])
        next_ref[...] = after
        split = after.astype(jnp.float32).reshape(BAND, degree, rows, features)
        sum_ref[...] = jnp.sum(split, axis=1).reshape(own, features)

    held = pl.BlockSpec(memory_space=pltpu.VMEM)
    return pl.pallas_call(
        body,
        name=f"fine{layer}",
        out_shape=(
            jax.ShapeDtypeStruct(fine.shape, jnp.bfloat16),
            jax.ShapeDtypeStruct((nodes, features), jnp.float32),
        ),
        grid=(steps,),
        in_specs=[
            pl.BlockSpec((block, features), lambda i: (i, 0)),
            pl.BlockSpec((block, 256), lambda i: (i, 0)),
        ]
        + [held] * 7,
        out_specs=(
            pl.BlockSpec((block, features), lambda i: (i, 0)),
            pl.BlockSpec((own, features), lambda i: (i, 0)),
        ),
        scratch_shapes=[
            pltpu.VMEM((nodes + 2 * rows, hidden), jnp.bfloat16),
            pltpu.VMEM((nodes, hidden), jnp.bfloat16),
            pltpu.VMEM((256, hidden), jnp.bfloat16),
        ],
        compiler_params=pltpu.CompilerParams(dimension_semantics=("arbitrary",), vmem_limit_bytes=14 * MIB),
    )(fine, picks, latents, left, right, sides, inner, outer, gain)


def pick(index, width):
    lanes = lax.broadcasted_iota(jnp.int32, (index.shape[0], width), 1)
    return (lanes == index).astype(jnp.bfloat16)


def rows_to_columns(left, right):
    return lax.dot_general(left, right, (((1,), (1,)), ((), ())), preferred_element_type=jnp.float32)


def decode(tags, at):
    numbers = tags.astype(jnp.int32)
    return jnp.where(numbers[:, 4:5] > 0, numbers[:, at : at + 1] * LOW + numbers[:, at + 1 : at + 2], -1)


def blocks_of(*arrays):
    return [pl.BlockSpec(a.shape, lambda i, n=len(a.shape): (0,) * n) for a in arrays]


def send_rows(both, own_ref, last_ref, first_ref):
    rows = both.astype(jnp.bfloat16)
    count, columns = own_ref.shape[0], last_ref.shape[0]
    own_ref[...] = rows[:count]
    last_ref[...] = rows[count : count + columns]
    first_ref[...] = rows[count + columns :]


def join_far(own, fars, left, right, last, first):
    count, features = own.shape
    rows = left.shape[0]
    four = 4 * count
    columns = last.shape[0]

    def body(own_ref, far1_ref, far2_ref, far3_ref, left_ref, right_ref, last_ref, first_ref, two_ref, up_ref, down_ref):
        for at, ref in enumerate((own_ref, far1_ref, far2_ref, far3_ref)):
            two_ref[at * count : (at + 1) * count, :] = ref[...]
        for out_ref, line_ref, row in ((up_ref, last_ref, rows - 1), (down_ref, first_ref, 0)):
            out_ref[:four, :] = two_ref[...]
            out_ref[four:, :] = jnp.zeros((out_ref.shape[0] - four, features), jnp.bfloat16)
            out_ref[four : four + 1, :] = left_ref[row : row + 1, :]
            out_ref[four + 1 : four + 1 + columns, :] = line_ref[...]
            out_ref[four + 1 + columns : four + 2 + columns, :] = right_ref[row : row + 1, :]

    held = pl.BlockSpec(memory_space=pltpu.VMEM)
    return pl.pallas_call(
        body,
        name="join_far",
        out_shape=tuple(jax.ShapeDtypeStruct((n, features), jnp.bfloat16) for n in (four, four + 32, four + 32)),
        in_specs=[held] * 8,
        out_specs=(held,) * 3,
        compiler_params=pltpu.CompilerParams(vmem_limit_bytes=2 * MIB),
    )(own, *fars, left, right, last, first)


def join_near(own, up, two, down):
    each, features = own.shape

    def body(own_ref, up_ref, two_ref, down_ref, joined_ref, sides_ref):
        for at, ref in enumerate((own_ref, up_ref, two_ref, down_ref)):
            joined_ref[at * each : (at + 1) * each, :] = ref[:each, :]
        sides_ref[: BELOW - ABOVE, :] = up_ref[each:, :]
        sides_ref[BELOW - ABOVE :, :] = down_ref[each:, :]

    held = pl.BlockSpec(memory_space=pltpu.VMEM)
    return pl.pallas_call(
        body,
        name="join_near",
        cost_estimate=pl.CostEstimate(flops=3_000_000_000, bytes_accessed=0, transcendentals=0),
        out_shape=tuple(jax.ShapeDtypeStruct((n, features), jnp.bfloat16) for n in (4 * each, 2 * (BELOW - ABOVE))),
        in_specs=[held] * 4,
        out_specs=(held,) * 2,
        compiler_params=pltpu.CompilerParams(vmem_limit_bytes=2 * MIB),
    )(own, up, two, down)


def coarse_start(coarse_slots, latents, rows, columns):
    count = coarse_slots.shape[1]
    nodes, features = latents.shape
    size = count + 2 * columns

    def body(slots_ref, latents_ref, own_ref, last_ref, first_ref, choose_ref):
        slot = slots_ref[...]
        row = jnp.floor((slot.astype(jnp.float32) + 0.5) * (1.0 / columns)).astype(jnp.int32)
        at = (slot - row * columns) * rows + row
        place = (lax.broadcasted_iota(jnp.int32, (nodes, count), 0) == at).astype(jnp.bfloat16)
        out = lax.broadcasted_iota(jnp.int32, (size, count), 0)
        same = (out == lax.broadcasted_iota(jnp.int32, (size, count), 1)).astype(jnp.bfloat16)
        out = lax.broadcasted_iota(jnp.int32, (size, nodes), 0)
        node = lax.broadcasted_iota(jnp.int32, (size, nodes), 1)
        edge = ((out >= count) & (out < count + columns) & (node == (out - count) * rows + rows - 1)) | (
            (out >= count + columns) & (node == (out - count - columns) * rows)
        )
        choose = (rows_to_columns(same, place) + edge.astype(jnp.float32)).astype(jnp.bfloat16)
        choose_ref[...] = choose
        send_rows(dot(choose, latents_ref[...]), own_ref, last_ref, first_ref)

    shapes = (
        *(jax.ShapeDtypeStruct((n, features), jnp.bfloat16) for n in (count, columns, columns)),
        jax.ShapeDtypeStruct((size, nodes), jnp.bfloat16),
    )
    return pl.pallas_call(
        body,
        name="coarse_start",
        out_shape=shapes,
        grid=(1,),
        in_specs=blocks_of(coarse_slots, latents),
        out_specs=blocks_of(*shapes),
        compiler_params=pltpu.CompilerParams(vmem_limit_bytes=4 * MIB),
    )(coarse_slots, latents)


def pack_edges(long_edges, senders, receivers, me, coarse_count, devices):
    count, features = long_edges.shape
    blocks = features // TAGS
    slots = devices * CAP

    def body(me_ref, long_ref, send_ref, recv_ref, sent_ref, mine_ref, wide):
        send, recv = send_ref[...], recv_ref[...]
        _, owner = table_row(0, 0, recv, coarse_count)
        here = (lax.shift_right_logical(me_ref[0], 3), me_ref[0] & 7)
        there = (lax.shift_right_logical(owner, 3), owner & 7)
        field = lax.broadcasted_iota(jnp.int32, (TAGS, count), 0)

        def fields(digits):
            sender = table_row(*digits, send, coarse_count)[0]
            receiver = table_row(*digits, recv, coarse_count)[0]
            both = jnp.where(field < 2, sender, receiver)
            high = lax.shift_right_logical(both, LOW.bit_length() - 1)
            value = jnp.where(field % 2 == 0, high, both & (LOW - 1))
            value = jnp.where(field == 4, 1, jnp.where(field == 5, owner, value))
            return jnp.where(field < 6, value, 0).astype(jnp.float32).astype(jnp.bfloat16)

        down = lax.broadcasted_iota(jnp.int32, (count, count), 0)
        across = lax.broadcasted_iota(jnp.int32, (count, count), 1)
        mine = rows_to_columns((down == across).astype(jnp.bfloat16), fields(here))
        mine_ref[...] = mine.astype(jnp.bfloat16)
        same = (mine[:, 5:6].astype(jnp.int32) == owner) & (down < across)
        rank = jnp.sum(same.astype(jnp.float32), axis=0, keepdims=True).astype(jnp.int32)
        spot = rank * devices + owner
        place = (lax.broadcasted_iota(jnp.int32, (slots, count), 0) == spot).astype(jnp.bfloat16)
        edges = dot(place, long_ref[...])
        tags = rows_to_columns(place, fields(there))
        for j in range(CAP):
            part = slice(j * devices, (j + 1) * devices)
            for b in range(blocks):
                wide[pl.ds(j * blocks + b, devices, stride=16), :] = edges[part, b * TAGS : (b + 1) * TAGS]
            wide[pl.ds(CAP * blocks + j, devices, stride=16), :] = tags[part]
        wide[pl.ds(15, devices, stride=16), :] = jnp.zeros((devices, TAGS), jnp.float32)
        sent_ref[...] = wide[...].astype(jnp.bfloat16)

    shapes = (
        jax.ShapeDtypeStruct((devices * 16, TAGS), jnp.bfloat16),
        jax.ShapeDtypeStruct((count, TAGS), jnp.bfloat16),
    )
    return pl.pallas_call(
        body,
        name="pack_edges",
        out_shape=shapes,
        grid=(1,),
        cost_estimate=pl.CostEstimate(flops=12_000_000_000, bytes_accessed=0, transcendentals=0),
        in_specs=[pl.BlockSpec(memory_space=pltpu.SMEM)] + blocks_of(long_edges, senders, receivers),
        out_specs=blocks_of(*shapes),
        scratch_shapes=[pltpu.VMEM((devices * 16, TAGS), jnp.float32)],
        compiler_params=pltpu.CompilerParams(vmem_limit_bytes=8 * MIB),
    )(me, long_edges, senders, receivers)


def unpack_edges(arrived, own_tags, choose, features, table_rows, coarse_count):
    devices = arrived.shape[0] // 16
    blocks = features // TAGS
    slots = devices * CAP
    count = own_tags.shape[0]
    nodes = choose.shape[1]

    def body(arrived_ref, tags_ref, choose_ref, rows_ref, send_ref, recv_ref, adds_ref, wide):
        wide[...] = arrived_ref[...].astype(jnp.float32)
        for j in range(CAP):
            part = slice(j * devices, (j + 1) * devices)
            for b in range(blocks):
                lanes = slice(b * TAGS, (b + 1) * TAGS)
                rows_ref[part, lanes] = wide[pl.ds(j * blocks + b, devices, stride=16), :].astype(jnp.bfloat16)
            tags = wide[pl.ds(CAP * blocks + j, devices, stride=16), :]
            send_ref[part, :] = pick(decode(tags, 0), table_rows)
            recv_ref[part, :] = pick(decode(tags, 2), TAGS)
        mine = tags_ref[...].astype(jnp.float32)
        send_ref[slots : slots + count, :] = pick(decode(mine, 0), table_rows)
        send_ref[slots + count :, :] = pick(decode(mine, 2), table_rows)
        here = recv_ref[:, :coarse_count]
        place = lax.dot_general(
            choose_ref[:coarse_count, :], here, (((0,), (1,)), ((), ())), preferred_element_type=jnp.float32
        )
        adds_ref[...] = place.astype(jnp.bfloat16)

    held = pl.BlockSpec(memory_space=pltpu.VMEM)
    return pl.pallas_call(
        body,
        name="unpack_edges",
        out_shape=(
            jax.ShapeDtypeStruct((slots, features), jnp.bfloat16),
            jax.ShapeDtypeStruct((slots + 2 * count, table_rows), jnp.bfloat16),
            jax.ShapeDtypeStruct((slots, TAGS), jnp.bfloat16),
            jax.ShapeDtypeStruct((nodes, slots), jnp.bfloat16),
        ),
        in_specs=[held] * 3,
        out_specs=(held,) * 4,
        scratch_shapes=[pltpu.VMEM(arrived.shape, jnp.float32)],
        compiler_params=pltpu.CompilerParams(vmem_limit_bytes=8 * MIB),
    )(arrived, own_tags, choose)


def long_step(before, sent, got, inner_ref, outer_ref, gain_ref, layer):
    features = before.shape[1]
    total = dot(before, inner_ref[layer, :features, :])
    total += dot(sent, inner_ref[layer, features : 2 * features, :])
    total += dot(got, inner_ref[layer, 2 * features :, :])
    return finish(before, total, outer_ref[layer], gain_ref[layer : layer + 1, :])


def coarse_layer(layer, long_rows, own_rows, sends, recvs, adds, choose, pieces, latents, fine_sum,
                 edge_inner, edge_outer, edge_gain, node_inner, node_outer, node_gain, coarse_count, last):
    slots = long_rows.shape[0]
    nodes, features = latents.shape
    count = len(pieces)
    each = pieces[0].shape[0]
    table_rows = count * each
    both = slots + own_rows.shape[0]

    def body(long_ref, own_ref, sends_ref, recvs_ref, adds_ref, choose_ref, latents_ref, sum_ref,
             ei_ref, eo_ref, eg_ref, ni_ref, no_ref, ng_ref, *rest):
        piece_refs = rest[:count]
        next_ref, *outs, ni, no, sems = rest[count:]
        table = outs[1] if last else outs[4]
        weights = [
            pltpu.make_async_copy(ni_ref.at[layer], ni, sems.at[0]),
            pltpu.make_async_copy(no_ref.at[layer], no, sems.at[1]),
        ]
        for copy in weights:
            copy.start()
        for p in range(count):
            table[p * each : (p + 1) * each, :] = piece_refs[p][...]
        got = dot(recvs_ref[...], table[:TAGS, :]).astype(jnp.bfloat16)
        if last:
            picked = dot(sends_ref[...], table[...]).astype(jnp.bfloat16)
            before = jnp.concatenate([long_ref[...], own_ref[...]], axis=0)
            got = jnp.concatenate([got, picked[both:]], axis=0)
            after = long_step(before, picked[:both], got, ei_ref, eo_ref, eg_ref, layer)
            outs[0][...] = after[slots:]
            after = after[:slots]
        else:
            sent = dot(sends_ref[:slots, :], table[...]).astype(jnp.bfloat16)
            after = long_step(long_ref[...], sent, got, ei_ref, eo_ref, eg_ref, layer)
            outs[0][...] = after
        incoming = (sum_ref[...] + dot(adds_ref[...], after)).astype(jnp.bfloat16)
        old = latents_ref[...]
        for copy in weights:
            copy.wait()
        total = dot(old, ni[:features, :]) + dot(incoming, ni[features:, :])
        new = finish(old, total, no[...], ng_ref[layer : layer + 1, :])
        next_ref[...] = new
        if not last:
            send_rows(dot(choose_ref[...], new), *outs[1:4])

    held = pl.BlockSpec(memory_space=pltpu.VMEM)
    away = pl.BlockSpec(memory_space=pl.ANY)
    table_shape = (table_rows, features)
    side = (choose.shape[0] - coarse_count) // 2
    kept = (both - slots,) if last else (slots, coarse_count, side, side, table_rows)
    shapes = [jax.ShapeDtypeStruct((n, features), jnp.bfloat16) for n in (nodes, *kept)]

    return pl.pallas_call(
        body,
        name=f"coarse{layer}",
        out_shape=tuple(shapes),
        in_specs=[held] * 11 + [away] * 2 + [held] * (1 + count),
        out_specs=(held,) * len(shapes),
        scratch_shapes=([pltpu.VMEM(table_shape, jnp.bfloat16)] if last else [])
        + [
            pltpu.VMEM(node_inner.shape[1:], jnp.bfloat16),
            pltpu.VMEM(node_outer.shape[1:], jnp.bfloat16),
            pltpu.SemaphoreType.DMA((2,)),
        ],
        compiler_params=pltpu.CompilerParams(vmem_limit_bytes=(18 if last else 14) * MIB),
    )(long_rows, own_rows, sends, recvs, adds, choose, latents, fine_sum,
      edge_inner, edge_outer, edge_gain, node_inner, node_outer, node_gain, *pieces)


def own_layer(layer, long_rows, sends, table, edge_inner, edge_outer, edge_gain):
    count = long_rows.shape[0]

    def body(long_ref, sends_ref, table_ref, ei_ref, eo_ref, eg_ref, next_ref):
        picked = dot(sends_ref[-2 * count :, :], table_ref[...]).astype(jnp.bfloat16)
        next_ref[...] = long_step(long_ref[...], picked[:count], picked[count:], ei_ref, eo_ref, eg_ref, layer)

    held = pl.BlockSpec(memory_space=pltpu.VMEM)
    return pl.pallas_call(
        body,
        name=f"own{layer}",
        out_shape=jax.ShapeDtypeStruct(long_rows.shape, jnp.bfloat16),
        in_specs=[held] * 6,
        out_specs=held,
        compiler_params=pltpu.CompilerParams(vmem_limit_bytes=8 * MIB),
    )(long_rows, sends, table, edge_inner, edge_outer, edge_gain)


def shards(
    node_latents,
    fine_edges,
    long_edges,
    neighbours,
    coarse_slots,
    long_senders,
    long_receivers,
    edge_inner,
    edge_outer,
    edge_gain,
    node_inner,
    node_outer,
    node_gain,
):
    rows, columns, features = node_latents.shape
    degree = fine_edges.shape[2]
    nodes = rows * columns
    coarse_count = coarse_slots.shape[0]
    layers = edge_inner.shape[0]
    devices = lax.axis_size("px") * lax.axis_size("py")

    latents = node_latents.transpose(1, 0, 2).reshape(nodes, features)
    fine = fine_edges.transpose(1, 2, 0, 3).reshape(nodes * degree, features)
    own, last_row, first_row, choose = coarse_start(coarse_slots[None, :], latents, rows, columns)
    long_edges, own = tie(long_edges, own)
    own_rows = long_edges
    me = lax.axis_index(AXES).reshape(1)
    payload, own_tags = pack_edges(long_edges, long_senders[None, :], long_receivers[None, :], me, coarse_count, devices)
    for layer in range(layers):
        last = layer == layers - 1
        fars = [along(own, "px", 4 * s) for s in (1, 2, 3)]
        left = along(latents[-rows:], "py", 1)
        right = along(latents[:rows], "py", -1)
        if layer == 0:
            *fars, left, right, payload = tie(*fars, left, right, payload)
        joined, up, down = join_far(own, fars, left, right, last_row, first_row)
        if layer == 0:
            packed = payload.reshape(devices, 16, TAGS)
            arrived = lax.all_to_all(packed, AXES, split_axis=0, concat_axis=0, tiled=True).reshape(payload.shape)
        up = along(up, "px", 1)
        down = along(down, "px", -1)
        two = along(joined, "px", 2)
        joined, sides = join_near(joined, up, two, down)
        joined, sides, own_rows = tie(joined, sides, own_rows)
        pieces = [joined] + [shift(joined, Z, s) for s in (1, 2, 3)]
        if layer == 0:
            table_rows = 2 * len(pieces) * joined.shape[0]
            long_rows, sends, recvs, adds = unpack_edges(arrived, own_tags, choose, features, table_rows, coarse_count)
            left, long_rows, neighbours = tie(left, long_rows, neighbours)
            picks = selection(neighbours)
        else:
            own_rows = own_layer(layer - 1, own_rows, sends, table, edge_inner, edge_outer, edge_gain)
        fine, fine_sum = fine_layer(
            layer, fine, picks, latents, left, right, sides, edge_inner, edge_outer, edge_gain, rows
        )
        first, *others, fine_sum, own_rows, long_rows = tie(*pieces, fine_sum, own_rows, long_rows)
        pieces = [first] + others
        pieces = pieces + [shift(piece, CORE, 1) for piece in pieces]
        latents, *rest = coarse_layer(
            layer, long_rows, own_rows, sends, recvs, adds, choose, pieces, latents, fine_sum,
            edge_inner, edge_outer, edge_gain, node_inner, node_outer, node_gain, coarse_count, last,
        )
        if last:
            own_rows = rest[0]
        else:
            long_rows, own, last_row, first_row, table = rest
    return (
        latents.reshape(columns, rows, features).transpose(1, 0, 2),
        fine.reshape(columns, degree, rows, features).transpose(2, 0, 1, 3),
        own_rows,
    )


def solution(mesh):
    in_specs = (
        P("px", "py", None),
        P("px", "py", None, None),
        P(AXES, None),
        P("px", "py", None),
        P(AXES),
        P(AXES),
        P(AXES),
        P(),
        P(),
        P(),
        P(),
        P(),
        P(),
    )
    out_specs = (P("px", "py", None), P("px", "py", None, None), P(AXES, None))
    return jax.shard_map(shards, mesh=mesh, in_specs=in_specs, out_specs=out_specs, check_vma=False)
```

```python
import jax
import jax.numpy as jnp
from jax import lax
from jax.experimental import pallas as pl
from jax.experimental.pallas import tpu as pltpu
from jax.sharding import PartitionSpec as P

EPSILON = 1e-05
AXES = ("px", "py")
RING = 16
Z, CORE = (2, 4), (1, 2)
BAND = 4
TAGS = 128
LOW = 64
CAP = 3
ABOVE, BELOW = 160, 192
MIB = 1024 * 1024


def shift(values, digit, step):
    stride, size = digit
    pairs = []
    for i in range(8):
        here = i // stride % size
        pairs.append((i, i + ((here + step) % size - here) * stride))
    return lax.ppermute(values, "py", pairs)


def tie(*values):
    return lax.optimization_barrier(values)


def table_row(px, py, coarse, coarse_count):
    home = jnp.floor((coarse.astype(jnp.float32) + 0.5) * (1.0 / coarse_count)).astype(jnp.int32)
    row = coarse - home * coarse_count
    away = (px - lax.shift_right_logical(home, 3)) & (RING - 1)
    near, far = away & 3, lax.shift_right_logical(away + 1, 2) & 3
    home_z, home_core = lax.shift_right_logical(home, 1) & 3, home & 1
    kz = (lax.shift_right_logical(py, 1) - home_z) & 3
    kc = (py - home_core) & 1
    return (((kc * 4 + kz) * 4 + near) * 4 + far) * coarse_count + row, home


def along(values, axis, step):
    count = lax.axis_size(axis)
    return lax.ppermute(values, axis, [(i, (i + step) % count) for i in range(count)])


def selection(neighbours):
    rows, columns, degree = neighbours.shape

    def body(codes_ref, picks_ref):
        codes = codes_ref[...]
        q = codes + (codes >= 4).astype(jnp.int32)
        down = (q >= 3).astype(jnp.int32) + (q >= 6).astype(jnp.int32)
        step = q - 3 * down
        from_row = lax.broadcasted_iota(jnp.int32, codes.shape, 1) + down - 1
        column = lax.broadcasted_iota(jnp.int32, codes.shape, 2)
        near = ((column & (BAND - 1)) + step) * rows + from_row
        sender = jnp.where(from_row < 0, ABOVE + column + step, jnp.where(from_row >= rows, BELOW + column + step, near))
        lanes = lax.broadcasted_iota(jnp.int32, (rows, 256), 1)
        row = lax.broadcasted_iota(jnp.int32, (rows, 256), 0)
        for c in range(columns):
            receiver = lanes == (BAND + 2 + c % BAND) * rows + row
            for k in range(degree):
                picks = (lanes == sender[k, :, c : c + 1]) | receiver
                picks_ref[(c * degree + k) * rows : (c * degree + k + 1) * rows, :] = picks.astype(jnp.bfloat16)

    held = pl.BlockSpec(memory_space=pltpu.VMEM)
    return pl.pallas_call(
        body,
        name="selection",
        out_shape=jax.ShapeDtypeStruct((rows * columns * degree, 256), jnp.bfloat16),
        in_specs=[held],
        out_specs=held,
        compiler_params=pltpu.CompilerParams(vmem_limit_bytes=4 * MIB),
    )(neighbours.transpose(2, 0, 1))


def dot(a, b):
    return jnp.dot(a, b, preferred_element_type=jnp.float32)


def finish(before, inner_sum, outer, gains):
    hidden = jax.nn.silu(inner_sum).astype(jnp.bfloat16)
    output = dot(hidden, outer)
    center = output - jnp.mean(output, axis=-1, keepdims=True)
    spread_of = jnp.mean(center * center, axis=-1, keepdims=True)
    scaled = center * lax.rsqrt(spread_of + EPSILON) * gains
    return (before.astype(jnp.float32) + scaled).astype(jnp.bfloat16)


def fine_layer(layer, fine, picks, latents, left, right, sides, inner, outer, gain, rows):
    edges, features = fine.shape
    nodes = latents.shape[0]
    hidden = inner.shape[2]
    near = (BAND + 2) * rows
    own = BAND * rows
    steps = nodes // own
    block = edges // steps
    degree = edges // nodes

    def body(fine_ref, picks_ref, latents_ref, left_ref, right_ref, sides_ref, inner_ref, outer_ref, gain_ref,
             next_ref, sum_ref, send_ref, recv_ref, table_ref):
        step = pl.program_id(0)

        @pl.when(step == 0)
        def _():
            send = inner_ref[layer, features : 2 * features, :]
            project = lambda ref: dot(ref[...], send).astype(jnp.bfloat16)
            table_ref[ABOVE : ABOVE + sides.shape[0], :] = project(sides_ref)
            table_ref[ABOVE + sides.shape[0] :, :] = jnp.zeros((256 - ABOVE - sides.shape[0], hidden), jnp.bfloat16)
            send_ref[rows : rows + nodes, :] = project(latents_ref)
            recv_ref[...] = dot(latents_ref[...], inner_ref[layer, 2 * features :, :]).astype(jnp.bfloat16)
            send_ref[:rows, :] = project(left_ref)
            send_ref[rows + nodes :, :] = project(right_ref)

        start = pl.multiple_of(step * own, own)
        table_ref[:near, :] = send_ref[pl.ds(start, near), :]
        table_ref[near : near + own, :] = recv_ref[pl.ds(start, own), :]
        before = fine_ref[...]
        total = dot(before, inner_ref[layer, :features, :]) + dot(picks_ref[...], table_ref[...])
        after = finish(before, total, outer_ref[layer], gain_ref[layer : layer + 1, :])
        next_ref[...] = after
        split = after.astype(jnp.float32).reshape(BAND, degree, rows, features)
        sum_ref[...] = jnp.sum(split, axis=1).reshape(own, features)

    held = pl.BlockSpec(memory_space=pltpu.VMEM)
    return pl.pallas_call(
        body,
        name=f"fine{layer}",
        out_shape=(
            pltpu.HBM(fine.shape, jnp.bfloat16),
            jax.ShapeDtypeStruct((nodes, features), jnp.float32),
        ),
        grid=(steps,),
        in_specs=[
            pl.BlockSpec((block, features), lambda i: (i, 0)),
            pl.BlockSpec((block, 256), lambda i: (i, 0)),
        ]
        + [held] * 7,
        out_specs=(
            pl.BlockSpec((block, features), lambda i: (i, 0)),
            pl.BlockSpec((own, features), lambda i: (i, 0)),
        ),
        scratch_shapes=[
            pltpu.VMEM((nodes + 2 * rows, hidden), jnp.bfloat16),
            pltpu.VMEM((nodes, hidden), jnp.bfloat16),
            pltpu.VMEM((256, hidden), jnp.bfloat16),
        ],
        compiler_params=pltpu.CompilerParams(dimension_semantics=("arbitrary",), vmem_limit_bytes=14 * MIB),
    )(in_hbm(fine), picks, latents, left, right, sides, inner, outer, gain)


def pick(index, width):
    lanes = lax.broadcasted_iota(jnp.int32, (index.shape[0], width), 1)
    return (lanes == index).astype(jnp.bfloat16)


def rows_to_columns(left, right):
    return lax.dot_general(left, right, (((1,), (1,)), ((), ())), preferred_element_type=jnp.float32)


def decode(tags, at):
    numbers = tags.astype(jnp.int32)
    return jnp.where(numbers[:, 4:5] > 0, numbers[:, at : at + 1] * LOW + numbers[:, at + 1 : at + 2], -1)


def send_rows(both, own_ref, last_ref, first_ref):
    rows = both.astype(jnp.bfloat16)
    count, columns = own_ref.shape[0], last_ref.shape[0]
    own_ref[...] = rows[:count]
    last_ref[...] = rows[count : count + columns]
    first_ref[...] = rows[count + columns :]


def join_far(own, fars, left, right, last, first):
    count, features = own.shape
    rows = left.shape[0]
    four = 4 * count
    columns = last.shape[0]

    def body(own_ref, far1_ref, far2_ref, far3_ref, left_ref, right_ref, last_ref, first_ref, two_ref, up_ref, down_ref):
        for at, ref in enumerate((own_ref, far1_ref, far2_ref, far3_ref)):
            two_ref[at * count : (at + 1) * count, :] = ref[...]
        for out_ref, line_ref, row in ((up_ref, last_ref, rows - 1), (down_ref, first_ref, 0)):
            out_ref[:four, :] = two_ref[...]
            out_ref[four:, :] = jnp.zeros((out_ref.shape[0] - four, features), jnp.bfloat16)
            out_ref[four : four + 1, :] = left_ref[row : row + 1, :]
            out_ref[four + 1 : four + 1 + columns, :] = line_ref[...]
            out_ref[four + 1 + columns : four + 2 + columns, :] = right_ref[row : row + 1, :]

    held = pl.BlockSpec(memory_space=pltpu.VMEM)
    return pl.pallas_call(
        body,
        name="join_far",
        out_shape=tuple(jax.ShapeDtypeStruct((n, features), jnp.bfloat16) for n in (four, four + 32, four + 32)),
        in_specs=[held] * 8,
        out_specs=(held,) * 3,
        compiler_params=pltpu.CompilerParams(vmem_limit_bytes=2 * MIB),
    )(own, *fars, left, right, last, first)


def in_hbm(values):
    return pltpu.with_memory_space_constraint(values, pltpu.HBM)


def fetch(pairs, sems):
    copies = [pltpu.make_async_copy(here, there, sems.at[i]) for i, (here, there) in enumerate(pairs)]
    for copy in copies:
        copy.start()
    for copy in copies:
        copy.wait()


def join_near(layer, own, up, two, down):
    each, features = own.shape
    side = BELOW - ABOVE

    def body(own_ref, up_ref, two_ref, down_ref, joined_ref, sides_ref, sems):
        part = lambda at: joined_ref.at[pl.ds(at * each, each), :]
        fetch(
            [
                (own_ref, part(0)),
                (up_ref.at[pl.ds(0, each), :], part(1)),
                (two_ref, part(2)),
                (down_ref.at[pl.ds(0, each), :], part(3)),
                (up_ref.at[pl.ds(each, side), :], sides_ref.at[pl.ds(0, side), :]),
                (down_ref.at[pl.ds(each, side), :], sides_ref.at[pl.ds(side, side), :]),
            ],
            sems,
        )

    away = pl.BlockSpec(memory_space=pltpu.HBM)
    return pl.pallas_call(
        body,
        name="join_near",
        cost_estimate=pl.CostEstimate(flops=3_000_000_000, bytes_accessed=0, transcendentals=0),
        out_shape=tuple(jax.ShapeDtypeStruct((n, features), jnp.bfloat16) for n in (4 * each, 2 * side)),
        in_specs=[away] * 4,
        out_specs=(away,) * 2,
        scratch_shapes=[pltpu.SemaphoreType.DMA((6,))],
        compiler_params=pltpu.CompilerParams(vmem_limit_bytes=2 * MIB),
    )(*(map(in_hbm, (own, up, two, down)) if layer == 0 else (own, up, two, down)))


def coarse_start(coarse_slots, latents, rows, columns):
    count = coarse_slots.shape[1]
    nodes, features = latents.shape
    size = count + 2 * columns

    def body(slots_away, latents_away, own_ref, last_ref, first_ref, left_ref, right_ref, choose_ref, slots_ref, latents_ref, sems):
        fetch([(slots_away, slots_ref), (latents_away, latents_ref)], sems)
        slot = slots_ref[...]
        row = jnp.floor((slot.astype(jnp.float32) + 0.5) * (1.0 / columns)).astype(jnp.int32)
        at = (slot - row * columns) * rows + row
        place = (lax.broadcasted_iota(jnp.int32, (nodes, count), 0) == at).astype(jnp.bfloat16)
        out = lax.broadcasted_iota(jnp.int32, (size, count), 0)
        same = (out == lax.broadcasted_iota(jnp.int32, (size, count), 1)).astype(jnp.bfloat16)
        out = lax.broadcasted_iota(jnp.int32, (size, nodes), 0)
        node = lax.broadcasted_iota(jnp.int32, (size, nodes), 1)
        edge = ((out >= count) & (out < count + columns) & (node == (out - count) * rows + rows - 1)) | (
            (out >= count + columns) & (node == (out - count - columns) * rows)
        )
        choose = (rows_to_columns(same, place) + edge.astype(jnp.float32)).astype(jnp.bfloat16)
        choose_ref[...] = choose
        send_rows(dot(choose, latents_ref[...]), own_ref, last_ref, first_ref)
        left_ref[...] = latents_ref[:rows, :]
        right_ref[...] = latents_ref[-rows:, :]

    shapes = (
        *(jax.ShapeDtypeStruct((n, features), jnp.bfloat16) for n in (count, columns, columns, rows, rows)),
        jax.ShapeDtypeStruct((size, nodes), jnp.bfloat16),
    )
    away = pl.BlockSpec(memory_space=pltpu.HBM)
    held = pl.BlockSpec(memory_space=pltpu.VMEM)
    return pl.pallas_call(
        body,
        name="coarse_start",
        out_shape=shapes,
        in_specs=[away] * 2,
        out_specs=(held,) * len(shapes),
        scratch_shapes=[
            pltpu.VMEM(coarse_slots.shape, jnp.int32),
            pltpu.VMEM(latents.shape, jnp.bfloat16),
            pltpu.SemaphoreType.DMA((2,)),
        ],
        compiler_params=pltpu.CompilerParams(vmem_limit_bytes=4 * MIB),
    )(*map(in_hbm, (coarse_slots, latents)))


def pack_edges(long_edges, senders, receivers, me, coarse_count, devices):
    count, features = long_edges.shape
    blocks = features // TAGS
    slots = devices * CAP

    def body(me_ref, long_away, send_away, recv_away, sent_ref, mine_ref, wide, long_ref, send_ref, recv_ref, sems):
        fetch([(long_away, long_ref), (send_away, send_ref), (recv_away, recv_ref)], sems)
        send, recv = send_ref[...], recv_ref[...]
        _, owner = table_row(0, 0, recv, coarse_count)
        here = (lax.shift_right_logical(me_ref[0], 3), me_ref[0] & 7)
        there = (lax.shift_right_logical(owner, 3), owner & 7)
        field = lax.broadcasted_iota(jnp.int32, (TAGS, count), 0)

        def fields(digits):
            sender = table_row(*digits, send, coarse_count)[0]
            receiver = table_row(*digits, recv, coarse_count)[0]
            both = jnp.where(field < 2, sender, receiver)
            high = lax.shift_right_logical(both, LOW.bit_length() - 1)
            value = jnp.where(field % 2 == 0, high, both & (LOW - 1))
            value = jnp.where(field == 4, 1, jnp.where(field == 5, owner, value))
            return jnp.where(field < 6, value, 0).astype(jnp.float32).astype(jnp.bfloat16)

        down = lax.broadcasted_iota(jnp.int32, (count, count), 0)
        across = lax.broadcasted_iota(jnp.int32, (count, count), 1)
        mine = rows_to_columns((down == across).astype(jnp.bfloat16), fields(here))
        mine_ref[...] = mine.astype(jnp.bfloat16)
        same = (mine[:, 5:6].astype(jnp.int32) == owner) & (down < across)
        rank = jnp.sum(same.astype(jnp.float32), axis=0, keepdims=True).astype(jnp.int32)
        spot = rank * devices + owner
        place = (lax.broadcasted_iota(jnp.int32, (slots, count), 0) == spot).astype(jnp.bfloat16)
        edges = dot(place, long_ref[...])
        tags = rows_to_columns(place, fields(there))
        for j in range(CAP):
            part = slice(j * devices, (j + 1) * devices)
            for b in range(blocks):
                wide[pl.ds(j * blocks + b, devices, stride=16), :] = edges[part, b * TAGS : (b + 1) * TAGS]
            wide[pl.ds(CAP * blocks + j, devices, stride=16), :] = tags[part]
        wide[pl.ds(15, devices, stride=16), :] = jnp.zeros((devices, TAGS), jnp.float32)
        sent_ref[...] = wide[...].astype(jnp.bfloat16)

    shapes = (
        jax.ShapeDtypeStruct((devices * 16, TAGS), jnp.bfloat16),
        jax.ShapeDtypeStruct((count, TAGS), jnp.bfloat16),
    )
    return pl.pallas_call(
        body,
        name="pack_edges",
        out_shape=shapes,
        cost_estimate=pl.CostEstimate(flops=12_000_000_000, bytes_accessed=0, transcendentals=0),
        in_specs=[pl.BlockSpec(memory_space=pltpu.SMEM)] + [pl.BlockSpec(memory_space=pltpu.HBM)] * 3,
        out_specs=(pl.BlockSpec(memory_space=pltpu.VMEM),) * 2,
        scratch_shapes=[
            pltpu.VMEM((devices * 16, TAGS), jnp.float32),
            pltpu.VMEM(long_edges.shape, jnp.bfloat16),
            pltpu.VMEM(senders.shape, jnp.int32),
            pltpu.VMEM(receivers.shape, jnp.int32),
            pltpu.SemaphoreType.DMA((3,)),
        ],
        compiler_params=pltpu.CompilerParams(vmem_limit_bytes=8 * MIB),
    )(me, *map(in_hbm, (long_edges, senders, receivers)))


def unpack_edges(arrived, choose, features, table_rows, coarse_count):
    devices = arrived.shape[0] // 16
    blocks = features // TAGS
    slots = devices * CAP
    nodes = choose.shape[1]

    def body(arrived_ref, choose_ref, rows_ref, send_ref, recv_ref, adds_ref, wide):
        wide[...] = arrived_ref[...].astype(jnp.float32)
        for j in range(CAP):
            part = slice(j * devices, (j + 1) * devices)
            for b in range(blocks):
                lanes = slice(b * TAGS, (b + 1) * TAGS)
                rows_ref[part, lanes] = wide[pl.ds(j * blocks + b, devices, stride=16), :].astype(jnp.bfloat16)
            tags = wide[pl.ds(CAP * blocks + j, devices, stride=16), :]
            send_ref[part, :] = pick(decode(tags, 0), table_rows)
            recv_ref[part, :] = pick(decode(tags, 2), TAGS)
        here = recv_ref[:, :coarse_count]
        place = lax.dot_general(
            choose_ref[:coarse_count, :], here, (((0,), (1,)), ((), ())), preferred_element_type=jnp.float32
        )
        adds_ref[...] = place.astype(jnp.bfloat16)

    held = pl.BlockSpec(memory_space=pltpu.VMEM)
    return pl.pallas_call(
        body,
        name="unpack_edges",
        out_shape=(
            jax.ShapeDtypeStruct((slots, features), jnp.bfloat16),
            jax.ShapeDtypeStruct((slots, table_rows), jnp.bfloat16),
            jax.ShapeDtypeStruct((slots, TAGS), jnp.bfloat16),
            jax.ShapeDtypeStruct((nodes, slots), jnp.bfloat16),
        ),
        in_specs=[held] * 2,
        out_specs=(held,) * 4,
        scratch_shapes=[pltpu.VMEM(arrived.shape, jnp.float32)],
        compiler_params=pltpu.CompilerParams(vmem_limit_bytes=8 * MIB),
    )(arrived, choose)


def long_step(before, sent, got, inner_ref, outer_ref, gain_ref, layer):
    features = before.shape[1]
    total = dot(before, inner_ref[layer, :features, :])
    total += dot(sent, inner_ref[layer, features : 2 * features, :])
    total += dot(got, inner_ref[layer, 2 * features :, :])
    return finish(before, total, outer_ref[layer], gain_ref[layer : layer + 1, :])


def coarse_layer(layer, long_rows, own_rows, sends, recvs, adds, choose, pieces, latents, fine_sum,
                 edge_inner, edge_outer, edge_gain, node_inner, node_outer, node_gain, coarse_count, last):
    slots = long_rows.shape[0]
    nodes, features = latents.shape
    count = len(pieces)
    each = pieces[0].shape[0]
    table_rows = count * each
    both = slots + own_rows.shape[0]

    def body(long_ref, own_ref, sends_ref, recvs_ref, adds_ref, choose_ref, latents_ref, sum_ref,
             ei_ref, eo_ref, eg_ref, ni_ref, no_ref, ng_ref, *rest):
        piece_refs = rest[:count]
        next_ref, *outs, ni, no, sems = rest[count:]
        table = outs[1] if last else outs[4]
        weights = [
            pltpu.make_async_copy(ni_ref.at[layer], ni, sems.at[0]),
            pltpu.make_async_copy(no_ref.at[layer], no, sems.at[1]),
        ]
        for copy in weights:
            copy.start()
        for p in range(count):
            table[p * each : (p + 1) * each, :] = piece_refs[p][...]
        got = dot(recvs_ref[...], table[:TAGS, :]).astype(jnp.bfloat16)
        if last:
            picked = dot(sends_ref[...], table[...]).astype(jnp.bfloat16)
            before = jnp.concatenate([long_ref[...], own_ref[...]], axis=0)
            got = jnp.concatenate([got, picked[both:]], axis=0)
            after = long_step(before, picked[:both], got, ei_ref, eo_ref, eg_ref, layer)
            outs[0][...] = after[slots:]
            after = after[:slots]
        else:
            sent = dot(sends_ref[...], table[...]).astype(jnp.bfloat16)
            after = long_step(long_ref[...], sent, got, ei_ref, eo_ref, eg_ref, layer)
            outs[0][...] = after
        incoming = (sum_ref[...] + dot(adds_ref[...], after)).astype(jnp.bfloat16)
        old = latents_ref[...]
        for copy in weights:
            copy.wait()
        total = dot(old, ni[:features, :]) + dot(incoming, ni[features:, :])
        new = finish(old, total, no[...], ng_ref[layer : layer + 1, :])
        next_ref[...] = new
        if not last:
            send_rows(dot(choose_ref[...], new), *outs[1:4])
            outs[5][...] = new[:rows]
            outs[6][...] = new[-rows:]

    held = pl.BlockSpec(memory_space=pltpu.VMEM)
    away = pl.BlockSpec(memory_space=pltpu.HBM)
    table_shape = (table_rows, features)
    side = (choose.shape[0] - coarse_count) // 2
    rows = nodes // side
    kept = (both - slots,) if last else (slots, coarse_count, side, side, table_rows, rows, rows)
    shapes = [jax.ShapeDtypeStruct((n, features), jnp.bfloat16) for n in (nodes, *kept)]

    return pl.pallas_call(
        body,
        name=f"coarse{layer}",
        out_shape=tuple(shapes),
        in_specs=[held] * 11 + [away] * 2 + [held] * (1 + count),
        out_specs=(held,) * len(shapes),
        scratch_shapes=([pltpu.VMEM(table_shape, jnp.bfloat16)] if last else [])
        + [
            pltpu.VMEM(node_inner.shape[1:], jnp.bfloat16),
            pltpu.VMEM(node_outer.shape[1:], jnp.bfloat16),
            pltpu.SemaphoreType.DMA((2,)),
        ],
        compiler_params=pltpu.CompilerParams(vmem_limit_bytes=(18 if last else 14) * MIB),
    )(long_rows, own_rows, sends, recvs, adds, choose, latents, fine_sum,
      edge_inner, edge_outer, edge_gain, node_inner, node_outer, node_gain, *pieces)


def own_layer(layer, long_rows, tags, sends, table, edge_inner, edge_outer, edge_gain):
    count = long_rows.shape[0]
    slots, rows = sends.shape

    def body(long_ref, tags_ref, sends_ref, table_ref, ei_ref, eo_ref, eg_ref, next_ref, all_ref):
        mine = tags_ref[...].astype(jnp.float32)
        all_ref[:slots, :] = sends_ref[...]
        all_ref[slots : slots + count, :] = pick(decode(mine, 0), rows)
        all_ref[slots + count :, :] = pick(decode(mine, 2), rows)
        picked = dot(all_ref[slots:, :], table_ref[...]).astype(jnp.bfloat16)
        next_ref[...] = long_step(long_ref[...], picked[:count], picked[count:], ei_ref, eo_ref, eg_ref, layer)

    held = pl.BlockSpec(memory_space=pltpu.VMEM)
    return pl.pallas_call(
        body,
        name=f"own{layer}",
        out_shape=(
            jax.ShapeDtypeStruct(long_rows.shape, jnp.bfloat16),
            jax.ShapeDtypeStruct((slots + 2 * count, rows), jnp.bfloat16),
        ),
        in_specs=[held] * 7,
        out_specs=(held, held),
        compiler_params=pltpu.CompilerParams(vmem_limit_bytes=8 * MIB),
    )(long_rows, tags, sends, table, edge_inner, edge_outer, edge_gain)


def shards(
    node_latents,
    fine_edges,
    long_edges,
    neighbours,
    coarse_slots,
    long_senders,
    long_receivers,
    edge_inner,
    edge_outer,
    edge_gain,
    node_inner,
    node_outer,
    node_gain,
):
    rows, columns, features = node_latents.shape
    degree = fine_edges.shape[2]
    nodes = rows * columns
    coarse_count = coarse_slots.shape[0]
    layers = edge_inner.shape[0]
    devices = lax.axis_size("px") * lax.axis_size("py")

    latents = node_latents.transpose(1, 0, 2).reshape(nodes, features)
    fine = fine_edges.transpose(1, 2, 0, 3).reshape(nodes * degree, features)
    own, last_row, first_row, to_left, to_right, choose = coarse_start(coarse_slots[None, :], latents, rows, columns)
    long_edges, own = tie(long_edges, own)
    own_rows = long_edges
    me = lax.axis_index(AXES).reshape(1)
    payload, own_tags = pack_edges(long_edges, long_senders[None, :], long_receivers[None, :], me, coarse_count, devices)
    for layer in range(layers):
        last = layer == layers - 1
        fars = [along(own, "px", 4 * s) for s in (1, 2, 3)]
        left = along(to_right, "py", 1)
        right = along(to_left, "py", -1)
        if layer == 0:
            *fars, left, right, payload = tie(*fars, left, right, payload)
        joined, up, down = join_far(own, fars, left, right, last_row, first_row)
        if layer == 0:
            packed = payload.reshape(devices, 16, TAGS)
            arrived = lax.all_to_all(packed, AXES, split_axis=0, concat_axis=0, tiled=True).reshape(payload.shape)
        two = along(joined, "px", 2)
        up = along(up, "px", 1)
        down = along(down, "px", -1)
        joined, sides = join_near(layer, joined, up, two, down)
        joined, sides, own_rows = tie(joined, sides, own_rows)
        pieces = [joined] + [shift(joined, Z, s) for s in (1, 2, 3)]
        if layer == 0:
            table_rows = 2 * len(pieces) * joined.shape[0]
            long_rows, sends, recvs, adds = unpack_edges(arrived, choose, features, table_rows, coarse_count)
            left, long_rows, neighbours = tie(left, long_rows, neighbours)
            picks = selection(neighbours)
        else:
            own_rows, sends = own_layer(layer - 1, own_rows, own_tags, sends, table, edge_inner, edge_outer, edge_gain)
        fine, fine_sum = fine_layer(
            layer, fine, picks, latents, left, right, sides, edge_inner, edge_outer, edge_gain, rows
        )
        swapped = shift(joined, CORE, 1)
        *others, fine_sum, own_rows, long_rows = tie(*pieces[1:], fine_sum, own_rows, long_rows)
        pieces = [joined] + others + [swapped] + [shift(piece, CORE, 1) for piece in others]
        latents, *rest = coarse_layer(
            layer, long_rows, own_rows, sends, recvs, adds, choose, pieces, latents, fine_sum,
            edge_inner, edge_outer, edge_gain, node_inner, node_outer, node_gain, coarse_count, last,
        )
        if last:
            own_rows = rest[0]
        else:
            long_rows, own, last_row, first_row, table, to_left, to_right = rest
    return (
        latents.reshape(columns, rows, features).transpose(1, 0, 2),
        fine.reshape(columns, degree, rows, features).transpose(2, 0, 1, 3),
        own_rows,
    )


def solution(mesh):
    in_specs = (
        P("px", "py", None),
        P("px", "py", None, None),
        P(AXES, None),
        P("px", "py", None),
        P(AXES),
        P(AXES),
        P(AXES),
        P(),
        P(),
        P(),
        P(),
        P(),
        P(),
    )
    out_specs = (P("px", "py", None), P("px", "py", None, None), P(AXES, None))
    return jax.shard_map(shards, mesh=mesh, in_specs=in_specs, out_specs=out_specs, check_vma=False)
```

```python
import jax
import jax.numpy as jnp
from jax import lax
from jax.experimental import pallas as pl
from jax.experimental.pallas import tpu as pltpu
from jax.sharding import PartitionSpec as P

EPSILON = 1e-05
AXES = ("px", "py")
RING = 16
Z, CORE = (2, 4), (1, 2)
BAND = 4
TAGS = 128
LOW = 64
CAP = 3
ABOVE, BELOW = 160, 192
MIB = 1024 * 1024


def shift(values, digit, step):
    stride, size = digit
    pairs = []
    for i in range(8):
        here = i // stride % size
        pairs.append((i, i + ((here + step) % size - here) * stride))
    return lax.ppermute(values, "py", pairs)


def tie(*values):
    return lax.optimization_barrier(values)


def table_row(px, py, coarse, coarse_count):
    home = jnp.floor((coarse.astype(jnp.float32) + 0.5) * (1.0 / coarse_count)).astype(jnp.int32)
    row = coarse - home * coarse_count
    away = (px - lax.shift_right_logical(home, 3)) & (RING - 1)
    near, far = away & 3, lax.shift_right_logical(away + 1, 2) & 3
    home_z, home_core = lax.shift_right_logical(home, 1) & 3, home & 1
    kz = (lax.shift_right_logical(py, 1) - home_z) & 3
    kc = (py - home_core) & 1
    return (((kc * 4 + kz) * 4 + near) * 4 + far) * coarse_count + row, home


def along(values, axis, step):
    count = lax.axis_size(axis)
    return lax.ppermute(values, axis, [(i, (i + step) % count) for i in range(count)])


def selection(neighbours):
    rows, columns, degree = neighbours.shape

    def body(codes_ref, picks_ref):
        codes = codes_ref[...]
        q = codes + (codes >= 4).astype(jnp.int32)
        down = (q >= 3).astype(jnp.int32) + (q >= 6).astype(jnp.int32)
        step = q - 3 * down
        from_row = lax.broadcasted_iota(jnp.int32, codes.shape, 1) + down - 1
        column = lax.broadcasted_iota(jnp.int32, codes.shape, 2)
        near = ((column & (BAND - 1)) + step) * rows + from_row
        sender = jnp.where(from_row < 0, ABOVE + column + step, jnp.where(from_row >= rows, BELOW + column + step, near))
        lanes = lax.broadcasted_iota(jnp.int32, (rows, 256), 1)
        row = lax.broadcasted_iota(jnp.int32, (rows, 256), 0)
        for c in range(columns):
            receiver = lanes == (BAND + 2 + c % BAND) * rows + row
            for k in range(degree):
                picks = (lanes == sender[k, :, c : c + 1]) | receiver
                picks_ref[(c * degree + k) * rows : (c * degree + k + 1) * rows, :] = picks.astype(jnp.bfloat16)

    held = pl.BlockSpec(memory_space=pltpu.VMEM)
    return pl.pallas_call(
        body,
        name="selection",
        out_shape=jax.ShapeDtypeStruct((rows * columns * degree, 256), jnp.bfloat16),
        in_specs=[held],
        out_specs=held,
        compiler_params=pltpu.CompilerParams(vmem_limit_bytes=4 * MIB),
    )(neighbours.transpose(2, 0, 1))


def dot(a, b):
    return jnp.dot(a, b, preferred_element_type=jnp.float32)


def finish(before, inner_sum, outer, gains):
    hidden = jax.nn.silu(inner_sum).astype(jnp.bfloat16)
    output = dot(hidden, outer)
    center = output - jnp.mean(output, axis=-1, keepdims=True)
    spread_of = jnp.mean(center * center, axis=-1, keepdims=True)
    scaled = center * lax.rsqrt(spread_of + EPSILON) * gains
    return (before.astype(jnp.float32) + scaled).astype(jnp.bfloat16)


def fine_layer(layer, fine, picks, latents, left, right, sides, inner, outer, gain, rows):
    edges, features = fine.shape
    nodes = latents.shape[0]
    hidden = inner.shape[2]
    near = (BAND + 2) * rows
    own = BAND * rows
    steps = nodes // own
    block = edges // steps
    degree = edges // nodes

    def body(fine_ref, picks_ref, latents_ref, left_ref, right_ref, sides_ref, inner_ref, outer_ref, gain_ref,
             next_ref, sum_ref, send_ref, recv_ref, table_ref):
        step = pl.program_id(0)

        @pl.when(step == 0)
        def _():
            send = inner_ref[layer, features : 2 * features, :]
            project = lambda ref: dot(ref[...], send).astype(jnp.bfloat16)
            table_ref[ABOVE : ABOVE + sides.shape[0], :] = project(sides_ref)
            table_ref[ABOVE + sides.shape[0] :, :] = jnp.zeros((256 - ABOVE - sides.shape[0], hidden), jnp.bfloat16)
            send_ref[rows : rows + nodes, :] = project(latents_ref)
            recv_ref[...] = dot(latents_ref[...], inner_ref[layer, 2 * features :, :]).astype(jnp.bfloat16)
            send_ref[:rows, :] = project(left_ref)
            send_ref[rows + nodes :, :] = project(right_ref)

        start = pl.multiple_of(step * own, own)
        table_ref[:near, :] = send_ref[pl.ds(start, near), :]
        table_ref[near : near + own, :] = recv_ref[pl.ds(start, own), :]
        before = fine_ref[...]
        total = dot(before, inner_ref[layer, :features, :]) + dot(picks_ref[...], table_ref[...])
        after = finish(before, total, outer_ref[layer], gain_ref[layer : layer + 1, :])
        next_ref[...] = after
        split = after.astype(jnp.float32).reshape(BAND, degree, rows, features)
        sum_ref[...] = jnp.sum(split, axis=1).reshape(own, features)

    held = pl.BlockSpec(memory_space=pltpu.VMEM)
    return pl.pallas_call(
        body,
        name=f"fine{layer}",
        out_shape=(
            jax.ShapeDtypeStruct(fine.shape, jnp.bfloat16),
            jax.ShapeDtypeStruct((nodes, features), jnp.float32),
        ),
        grid=(steps,),
        in_specs=[
            pl.BlockSpec((block, features), lambda i: (i, 0)),
            pl.BlockSpec((block, 256), lambda i: (i, 0)),
        ]
        + [held] * 7,
        out_specs=(
            pl.BlockSpec((block, features), lambda i: (i, 0)),
            pl.BlockSpec((own, features), lambda i: (i, 0)),
        ),
        scratch_shapes=[
            pltpu.VMEM((nodes + 2 * rows, hidden), jnp.bfloat16),
            pltpu.VMEM((nodes, hidden), jnp.bfloat16),
            pltpu.VMEM((256, hidden), jnp.bfloat16),
        ],
        compiler_params=pltpu.CompilerParams(dimension_semantics=("arbitrary",), vmem_limit_bytes=14 * MIB),
    )(fine, picks, latents, left, right, sides, inner, outer, gain)


def pick(index, width):
    lanes = lax.broadcasted_iota(jnp.int32, (index.shape[0], width), 1)
    return (lanes == index).astype(jnp.bfloat16)


def rows_to_columns(left, right):
    return lax.dot_general(left, right, (((1,), (1,)), ((), ())), preferred_element_type=jnp.float32)


def decode(tags, at):
    numbers = tags.astype(jnp.int32)
    return jnp.where(numbers[:, 4:5] > 0, numbers[:, at : at + 1] * LOW + numbers[:, at + 1 : at + 2], -1)


def send_rows(both, own_ref, last_ref, first_ref):
    rows = both.astype(jnp.bfloat16)
    count, columns = own_ref.shape[0], last_ref.shape[0]
    own_ref[...] = rows[:count]
    last_ref[...] = rows[count : count + columns]
    first_ref[...] = rows[count + columns :]


def join_far(own, fars, left, right, last, first):
    count, features = own.shape
    rows = left.shape[0]
    four = 4 * count
    columns = last.shape[0]

    def body(own_ref, far1_ref, far2_ref, far3_ref, left_ref, right_ref, last_ref, first_ref, two_ref, up_ref, down_ref):
        for at, ref in enumerate((own_ref, far1_ref, far2_ref, far3_ref)):
            two_ref[at * count : (at + 1) * count, :] = ref[...]
        for out_ref, line_ref, row in ((up_ref, last_ref, rows - 1), (down_ref, first_ref, 0)):
            out_ref[:four, :] = two_ref[...]
            out_ref[four:, :] = jnp.zeros((out_ref.shape[0] - four, features), jnp.bfloat16)
            out_ref[four : four + 1, :] = left_ref[row : row + 1, :]
            out_ref[four + 1 : four + 1 + columns, :] = line_ref[...]
            out_ref[four + 1 + columns : four + 2 + columns, :] = right_ref[row : row + 1, :]

    held = pl.BlockSpec(memory_space=pltpu.VMEM)
    return pl.pallas_call(
        body,
        name="join_far",
        out_shape=tuple(jax.ShapeDtypeStruct((n, features), jnp.bfloat16) for n in (four, four + 32, four + 32)),
        in_specs=[held] * 8,
        out_specs=(held,) * 3,
        compiler_params=pltpu.CompilerParams(vmem_limit_bytes=2 * MIB),
    )(own, *fars, left, right, last, first)


def in_hbm(values):
    return pltpu.with_memory_space_constraint(values, pltpu.HBM)


def fetch(pairs, sems):
    copies = [pltpu.make_async_copy(here, there, sems.at[i]) for i, (here, there) in enumerate(pairs)]
    for copy in copies:
        copy.start()
    for copy in copies:
        copy.wait()


def join_near(layer, own, up, two, down):
    each, features = own.shape
    side = BELOW - ABOVE

    far = layer == 0

    def body(own_ref, two_ref, up_ref, down_ref, joined_ref, sides_ref, sems, *near):
        to, beside = near or (joined_ref, sides_ref)
        part = lambda at: to.at[pl.ds(at * each, each), :]
        fetch(
            [
                (own_ref, part(0)),
                (up_ref.at[pl.ds(0, each), :], part(1)),
                (two_ref, part(2)),
                (down_ref.at[pl.ds(0, each), :], part(3)),
                (up_ref.at[pl.ds(each, side), :], beside.at[pl.ds(0, side), :]),
                (down_ref.at[pl.ds(each, side), :], beside.at[pl.ds(side, side), :]),
            ],
            sems,
        )
        if near:
            fetch([(to, joined_ref), (beside, sides_ref)], sems)

    away = pl.BlockSpec(memory_space=pl.ANY)
    place = pltpu.HBM if far else jax.ShapeDtypeStruct
    shapes = ((4 * each, features), (2 * side, features))
    operands = (own, two, up, down)
    return pl.pallas_call(
        body,
        name="join_near",
        cost_estimate=pl.CostEstimate(flops=3_000_000_000, bytes_accessed=0, transcendentals=0),
        out_shape=tuple(place(shape, jnp.bfloat16) for shape in shapes),
        in_specs=[away] * 4,
        out_specs=(away,) * 2,
        scratch_shapes=[pltpu.SemaphoreType.DMA((6,))]
        + [pltpu.VMEM(shape, jnp.bfloat16) for shape in shapes if far],
        compiler_params=pltpu.CompilerParams(vmem_limit_bytes=2 * MIB),
    )(*(map(in_hbm, operands) if far else operands))


def coarse_start(coarse_slots, latents, rows, columns):
    count = coarse_slots.shape[1]
    nodes, features = latents.shape
    size = count + 2 * columns

    def body(slots_away, latents_away, own_ref, last_ref, first_ref, left_ref, right_ref, choose_ref, slots_ref, latents_ref, sems):
        fetch([(slots_away, slots_ref), (latents_away, latents_ref)], sems)
        slot = slots_ref[...]
        row = jnp.floor((slot.astype(jnp.float32) + 0.5) * (1.0 / columns)).astype(jnp.int32)
        at = (slot - row * columns) * rows + row
        place = (lax.broadcasted_iota(jnp.int32, (nodes, count), 0) == at).astype(jnp.bfloat16)
        out = lax.broadcasted_iota(jnp.int32, (size, count), 0)
        same = (out == lax.broadcasted_iota(jnp.int32, (size, count), 1)).astype(jnp.bfloat16)
        out = lax.broadcasted_iota(jnp.int32, (size, nodes), 0)
        node = lax.broadcasted_iota(jnp.int32, (size, nodes), 1)
        edge = ((out >= count) & (out < count + columns) & (node == (out - count) * rows + rows - 1)) | (
            (out >= count + columns) & (node == (out - count - columns) * rows)
        )
        choose = (rows_to_columns(same, place) + edge.astype(jnp.float32)).astype(jnp.bfloat16)
        choose_ref[...] = choose
        send_rows(dot(choose, latents_ref[...]), own_ref, last_ref, first_ref)
        left_ref[...] = latents_ref[:rows, :]
        right_ref[...] = latents_ref[-rows:, :]

    shapes = (
        *(jax.ShapeDtypeStruct((n, features), jnp.bfloat16) for n in (count, columns, columns, rows, rows)),
        jax.ShapeDtypeStruct((size, nodes), jnp.bfloat16),
    )
    away = pl.BlockSpec(memory_space=pltpu.HBM)
    held = pl.BlockSpec(memory_space=pltpu.VMEM)
    return pl.pallas_call(
        body,
        name="coarse_start",
        out_shape=shapes,
        in_specs=[away] * 2,
        out_specs=(held,) * len(shapes),
        scratch_shapes=[
            pltpu.VMEM(coarse_slots.shape, jnp.int32),
            pltpu.VMEM(latents.shape, jnp.bfloat16),
            pltpu.SemaphoreType.DMA((2,)),
        ],
        compiler_params=pltpu.CompilerParams(vmem_limit_bytes=4 * MIB),
    )(*map(in_hbm, (coarse_slots, latents)))


def pack_edges(long_edges, senders, receivers, me, coarse_count, devices):
    count, features = long_edges.shape
    blocks = features // TAGS
    slots = devices * CAP

    def body(me_ref, long_away, send_away, recv_away, sent_ref, mine_ref, wide, long_ref, send_ref, recv_ref, sems):
        fetch([(long_away, long_ref), (send_away, send_ref), (recv_away, recv_ref)], sems)
        send, recv = send_ref[...], recv_ref[...]
        _, owner = table_row(0, 0, recv, coarse_count)
        here = (lax.shift_right_logical(me_ref[0], 3), me_ref[0] & 7)
        there = (lax.shift_right_logical(owner, 3), owner & 7)
        field = lax.broadcasted_iota(jnp.int32, (TAGS, count), 0)

        def fields(digits):
            sender = table_row(*digits, send, coarse_count)[0]
            receiver = table_row(*digits, recv, coarse_count)[0]
            both = jnp.where(field < 2, sender, receiver)
            high = lax.shift_right_logical(both, LOW.bit_length() - 1)
            value = jnp.where(field % 2 == 0, high, both & (LOW - 1))
            value = jnp.where(field == 4, 1, jnp.where(field == 5, owner, value))
            return jnp.where(field < 6, value, 0).astype(jnp.float32).astype(jnp.bfloat16)

        down = lax.broadcasted_iota(jnp.int32, (count, count), 0)
        across = lax.broadcasted_iota(jnp.int32, (count, count), 1)
        mine = rows_to_columns((down == across).astype(jnp.bfloat16), fields(here))
        mine_ref[...] = mine.astype(jnp.bfloat16)
        same = (mine[:, 5:6].astype(jnp.int32) == owner) & (down < across)
        rank = jnp.sum(same.astype(jnp.float32), axis=0, keepdims=True).astype(jnp.int32)
        spot = rank * devices + owner
        place = (lax.broadcasted_iota(jnp.int32, (slots, count), 0) == spot).astype(jnp.bfloat16)
        edges = dot(place, long_ref[...])
        tags = rows_to_columns(place, fields(there))
        for j in range(CAP):
            part = slice(j * devices, (j + 1) * devices)
            for b in range(blocks):
                wide[pl.ds(j * blocks + b, devices, stride=16), :] = edges[part, b * TAGS : (b + 1) * TAGS]
            wide[pl.ds(CAP * blocks + j, devices, stride=16), :] = tags[part]
        wide[pl.ds(15, devices, stride=16), :] = jnp.zeros((devices, TAGS), jnp.float32)
        sent_ref[...] = wide[...].astype(jnp.bfloat16)

    shapes = (
        jax.ShapeDtypeStruct((devices * 16, TAGS), jnp.bfloat16),
        jax.ShapeDtypeStruct((count, TAGS), jnp.bfloat16),
    )
    return pl.pallas_call(
        body,
        name="pack_edges",
        out_shape=shapes,
        cost_estimate=pl.CostEstimate(flops=12_000_000_000, bytes_accessed=0, transcendentals=0),
        in_specs=[pl.BlockSpec(memory_space=pltpu.SMEM)] + [pl.BlockSpec(memory_space=pltpu.HBM)] * 3,
        out_specs=(pl.BlockSpec(memory_space=pltpu.VMEM),) * 2,
        scratch_shapes=[
            pltpu.VMEM((devices * 16, TAGS), jnp.float32),
            pltpu.VMEM(long_edges.shape, jnp.bfloat16),
            pltpu.VMEM(senders.shape, jnp.int32),
            pltpu.VMEM(receivers.shape, jnp.int32),
            pltpu.SemaphoreType.DMA((3,)),
        ],
        compiler_params=pltpu.CompilerParams(vmem_limit_bytes=8 * MIB),
    )(me, *map(in_hbm, (long_edges, senders, receivers)))


def unpack_edges(arrived, choose, features, table_rows, coarse_count):
    devices = arrived.shape[0] // 16
    blocks = features // TAGS
    slots = devices * CAP
    nodes = choose.shape[1]

    def body(arrived_ref, choose_ref, rows_ref, send_ref, recv_ref, adds_ref, wide):
        wide[...] = arrived_ref[...].astype(jnp.float32)
        for j in range(CAP):
            part = slice(j * devices, (j + 1) * devices)
            for b in range(blocks):
                lanes = slice(b * TAGS, (b + 1) * TAGS)
                rows_ref[part, lanes] = wide[pl.ds(j * blocks + b, devices, stride=16), :].astype(jnp.bfloat16)
            tags = wide[pl.ds(CAP * blocks + j, devices, stride=16), :]
            send_ref[part, :] = pick(decode(tags, 0), table_rows)
            recv_ref[part, :] = pick(decode(tags, 2), TAGS)
        here = recv_ref[:, :coarse_count]
        place = lax.dot_general(
            choose_ref[:coarse_count, :], here, (((0,), (1,)), ((), ())), preferred_element_type=jnp.float32
        )
        adds_ref[...] = place.astype(jnp.bfloat16)

    held = pl.BlockSpec(memory_space=pltpu.VMEM)
    return pl.pallas_call(
        body,
        name="unpack_edges",
        out_shape=(
            jax.ShapeDtypeStruct((slots, features), jnp.bfloat16),
            jax.ShapeDtypeStruct((slots, table_rows), jnp.bfloat16),
            jax.ShapeDtypeStruct((slots, TAGS), jnp.bfloat16),
            jax.ShapeDtypeStruct((nodes, slots), jnp.bfloat16),
        ),
        in_specs=[held] * 2,
        out_specs=(held,) * 4,
        scratch_shapes=[pltpu.VMEM(arrived.shape, jnp.float32)],
        compiler_params=pltpu.CompilerParams(vmem_limit_bytes=8 * MIB),
    )(arrived, choose)


def long_step(before, sent, got, inner_ref, outer_ref, gain_ref, layer):
    features = before.shape[1]
    total = dot(before, inner_ref[layer, :features, :])
    total += dot(sent, inner_ref[layer, features : 2 * features, :])
    total += dot(got, inner_ref[layer, 2 * features :, :])
    return finish(before, total, outer_ref[layer], gain_ref[layer : layer + 1, :])


def coarse_layer(layer, long_rows, own_rows, sends, recvs, adds, choose, pieces, latents, fine_sum,
                 edge_inner, edge_outer, edge_gain, node_inner, node_outer, node_gain, coarse_count, last):
    slots = long_rows.shape[0]
    nodes, features = latents.shape
    count = len(pieces)
    each = pieces[0].shape[0]
    table_rows = count * each
    both = slots + own_rows.shape[0]

    def body(long_ref, own_ref, sends_ref, recvs_ref, adds_ref, choose_ref, latents_ref, sum_ref,
             ei_ref, eo_ref, eg_ref, ni_ref, no_ref, ng_ref, *rest):
        piece_refs = rest[:count]
        next_ref, *outs, ni, no, sems = rest[count:]
        table = outs[1] if last else outs[4]
        weights = [
            pltpu.make_async_copy(ni_ref.at[layer], ni, sems.at[0]),
            pltpu.make_async_copy(no_ref.at[layer], no, sems.at[1]),
        ]
        for copy in weights:
            copy.start()
        for p in range(count):
            table[p * each : (p + 1) * each, :] = piece_refs[p][...]
        got = dot(recvs_ref[...], table[:TAGS, :]).astype(jnp.bfloat16)
        if last:
            picked = dot(sends_ref[...], table[...]).astype(jnp.bfloat16)
            before = jnp.concatenate([long_ref[...], own_ref[...]], axis=0)
            got = jnp.concatenate([got, picked[both:]], axis=0)
            after = long_step(before, picked[:both], got, ei_ref, eo_ref, eg_ref, layer)
            outs[0][...] = after[slots:]
            after = after[:slots]
        else:
            sent = dot(sends_ref[...], table[...]).astype(jnp.bfloat16)
            after = long_step(long_ref[...], sent, got, ei_ref, eo_ref, eg_ref, layer)
            outs[0][...] = after
        incoming = (sum_ref[...] + dot(adds_ref[...], after)).astype(jnp.bfloat16)
        old = latents_ref[...]
        for copy in weights:
            copy.wait()
        total = dot(old, ni[:features, :]) + dot(incoming, ni[features:, :])
        new = finish(old, total, no[...], ng_ref[layer : layer + 1, :])
        next_ref[...] = new
        if not last:
            send_rows(dot(choose_ref[...], new), *outs[1:4])
            outs[5][...] = new[:rows]
            outs[6][...] = new[-rows:]

    held = pl.BlockSpec(memory_space=pltpu.VMEM)
    away = pl.BlockSpec(memory_space=pltpu.HBM)
    table_shape = (table_rows, features)
    side = (choose.shape[0] - coarse_count) // 2
    rows = nodes // side
    kept = (both - slots,) if last else (slots, coarse_count, side, side, table_rows, rows, rows)
    shapes = [jax.ShapeDtypeStruct((n, features), jnp.bfloat16) for n in (nodes, *kept)]

    return pl.pallas_call(
        body,
        name=f"coarse{layer}",
        out_shape=tuple(shapes),
        in_specs=[held] * 11 + [away] * 2 + [held] * (1 + count),
        out_specs=(held,) * len(shapes),
        scratch_shapes=([pltpu.VMEM(table_shape, jnp.bfloat16)] if last else [])
        + [
            pltpu.VMEM(node_inner.shape[1:], jnp.bfloat16),
            pltpu.VMEM(node_outer.shape[1:], jnp.bfloat16),
            pltpu.SemaphoreType.DMA((2,)),
        ],
        compiler_params=pltpu.CompilerParams(vmem_limit_bytes=(18 if last else 14) * MIB),
    )(long_rows, own_rows, sends, recvs, adds, choose, latents, fine_sum,
      edge_inner, edge_outer, edge_gain, node_inner, node_outer, node_gain, *pieces)


def own_layer(layer, long_rows, tags, sends, table, edge_inner, edge_outer, edge_gain):
    count = long_rows.shape[0]
    slots, rows = sends.shape

    def body(long_ref, tags_ref, sends_ref, table_ref, ei_ref, eo_ref, eg_ref, next_ref, all_ref):
        mine = tags_ref[...].astype(jnp.float32)
        all_ref[:slots, :] = sends_ref[...]
        all_ref[slots : slots + count, :] = pick(decode(mine, 0), rows)
        all_ref[slots + count :, :] = pick(decode(mine, 2), rows)
        picked = dot(all_ref[slots:, :], table_ref[...]).astype(jnp.bfloat16)
        next_ref[...] = long_step(long_ref[...], picked[:count], picked[count:], ei_ref, eo_ref, eg_ref, layer)

    held = pl.BlockSpec(memory_space=pltpu.VMEM)
    return pl.pallas_call(
        body,
        name=f"own{layer}",
        out_shape=(
            jax.ShapeDtypeStruct(long_rows.shape, jnp.bfloat16),
            jax.ShapeDtypeStruct((slots + 2 * count, rows), jnp.bfloat16),
        ),
        in_specs=[held] * 7,
        out_specs=(held, held),
        compiler_params=pltpu.CompilerParams(vmem_limit_bytes=8 * MIB),
    )(long_rows, tags, sends, table, edge_inner, edge_outer, edge_gain)


def shards(
    node_latents,
    fine_edges,
    long_edges,
    neighbours,
    coarse_slots,
    long_senders,
    long_receivers,
    edge_inner,
    edge_outer,
    edge_gain,
    node_inner,
    node_outer,
    node_gain,
):
    rows, columns, features = node_latents.shape
    degree = fine_edges.shape[2]
    nodes = rows * columns
    coarse_count = coarse_slots.shape[0]
    layers = edge_inner.shape[0]
    devices = lax.axis_size("px") * lax.axis_size("py")

    latents = node_latents.transpose(1, 0, 2).reshape(nodes, features)
    fine = fine_edges.transpose(1, 2, 0, 3).reshape(nodes * degree, features)
    own, last_row, first_row, to_left, to_right, choose = coarse_start(coarse_slots[None, :], latents, rows, columns)
    long_edges, own = tie(long_edges, own)
    own_rows = long_edges
    me = lax.axis_index(AXES).reshape(1)
    payload, own_tags = pack_edges(long_edges, long_senders[None, :], long_receivers[None, :], me, coarse_count, devices)
    for layer in range(layers):
        last = layer == layers - 1
        fars = [along(own, "px", 4 * s) for s in (1, 2, 3)]
        left = along(to_right, "py", 1)
        right = along(to_left, "py", -1)
        if layer == 0:
            *fars, left, right, payload = tie(*fars, left, right, payload)
        joined, up, down = join_far(own, fars, left, right, last_row, first_row)
        if layer == 0:
            packed = payload.reshape(devices, 16, TAGS)
            arrived = lax.all_to_all(packed, AXES, split_axis=0, concat_axis=0, tiled=True).reshape(payload.shape)
        two = along(joined, "px", 2)
        up = along(up, "px", 1)
        down = along(down, "px", -1)
        joined, sides = join_near(layer, joined, up, two, down)
        joined, sides, own_rows = tie(joined, sides, own_rows)
        pieces = [joined] + [shift(joined, Z, s) for s in (1, 2, 3)]
        if layer == 0:
            table_rows = 2 * len(pieces) * joined.shape[0]
            long_rows, sends, recvs, adds = unpack_edges(arrived, choose, features, table_rows, coarse_count)
            left, long_rows, neighbours = tie(left, long_rows, neighbours)
            picks = selection(neighbours)
        else:
            own_rows, sends = own_layer(layer - 1, own_rows, own_tags, sends, table, edge_inner, edge_outer, edge_gain)
        fine, fine_sum = fine_layer(
            layer, fine, picks, latents, left, right, sides, edge_inner, edge_outer, edge_gain, rows
        )
        swapped = shift(joined, CORE, 1)
        *others, fine_sum, own_rows, long_rows = tie(*pieces[1:], fine_sum, own_rows, long_rows)
        pieces = [joined] + others + [swapped] + [shift(piece, CORE, 1) for piece in others]
        latents, *rest = coarse_layer(
            layer, long_rows, own_rows, sends, recvs, adds, choose, pieces, latents, fine_sum,
            edge_inner, edge_outer, edge_gain, node_inner, node_outer, node_gain, coarse_count, last,
        )
        if last:
            own_rows = rest[0]
        else:
            long_rows, own, last_row, first_row, table, to_left, to_right = rest
    return (
        latents.reshape(columns, rows, features).transpose(1, 0, 2),
        fine.reshape(columns, degree, rows, features).transpose(2, 0, 1, 3),
        own_rows,
    )


def solution(mesh):
    in_specs = (
        P("px", "py", None),
        P("px", "py", None, None),
        P(AXES, None),
        P("px", "py", None),
        P(AXES),
        P(AXES),
        P(AXES),
        P(),
        P(),
        P(),
        P(),
        P(),
        P(),
    )
    out_specs = (P("px", "py", None), P("px", "py", None, None), P(AXES, None))
    return jax.shard_map(shards, mesh=mesh, in_specs=in_specs, out_specs=out_specs, check_vma=False)
```

```python
import jax
import jax.numpy as jnp
from jax import lax
from jax.experimental import pallas as pl
from jax.experimental.pallas import tpu as pltpu
from jax.sharding import PartitionSpec as P

EPSILON = 1e-05
AXES = ("px", "py")
Z, CORE = (2, 4), (1, 2)
BAND = 4
TAGS = 128
LOW = 64
CAP = 3
ABOVE, BELOW = 160, 192
MIB = 1024 * 1024


def shift(values, digit, step):
    stride, size = digit
    pairs = []
    for i in range(8):
        here = i // stride % size
        pairs.append((i, i + ((here + step) % size - here) * stride))
    return lax.ppermute(values, "py", pairs)


def tie(*values):
    return lax.optimization_barrier(values)


def table_row(px, py, coarse, coarse_count):
    home = jnp.floor((coarse.astype(jnp.float32) + 0.5) * (1.0 / coarse_count)).astype(jnp.int32)
    row = coarse - home * coarse_count
    home_px = lax.shift_right_logical(home, 3)
    ky = (lax.shift_right_logical(px, 2) - lax.shift_right_logical(home_px, 2)) & 3
    kx = (px - home_px) & 3
    home_z, home_core = lax.shift_right_logical(home, 1) & 3, home & 1
    kz = (lax.shift_right_logical(py, 1) - home_z) & 3
    kc = (py - home_core) & 1
    return (((kc * 4 + kz) * 4 + kx) * 4 + ky) * coarse_count + row, home


def around_x(values, step):
    return lax.ppermute(values, "px", [(i, i // 4 * 4 + (i + step) % 4) for i in range(16)])


def along(values, axis, step):
    count = lax.axis_size(axis)
    return lax.ppermute(values, axis, [(i, (i + step) % count) for i in range(count)])


def selection(neighbours):
    rows, columns, degree = neighbours.shape

    def body(codes_ref, picks_ref):
        codes = codes_ref[...]
        q = codes + (codes >= 4).astype(jnp.int32)
        down = (q >= 3).astype(jnp.int32) + (q >= 6).astype(jnp.int32)
        step = q - 3 * down
        from_row = lax.broadcasted_iota(jnp.int32, codes.shape, 1) + down - 1
        column = lax.broadcasted_iota(jnp.int32, codes.shape, 2)
        near = ((column & (BAND - 1)) + step) * rows + from_row
        wide = column + step - 1
        wide = jnp.where(wide < 0, columns, jnp.where(wide >= columns, columns + 1, wide))
        sender = jnp.where(from_row < 0, ABOVE + wide, jnp.where(from_row >= rows, BELOW + wide, near))
        lanes = lax.broadcasted_iota(jnp.int32, (rows, 256), 1)
        row = lax.broadcasted_iota(jnp.int32, (rows, 256), 0)
        for c in range(columns):
            receiver = lanes == (BAND + 2 + c % BAND) * rows + row
            for k in range(degree):
                picks = (lanes == sender[k, :, c : c + 1]) | receiver
                picks_ref[(c * degree + k) * rows : (c * degree + k + 1) * rows, :] = picks.astype(jnp.bfloat16)

    held = pl.BlockSpec(memory_space=pltpu.VMEM)
    return pl.pallas_call(
        body,
        name="selection",
        out_shape=jax.ShapeDtypeStruct((rows * columns * degree, 256), jnp.bfloat16),
        in_specs=[held],
        out_specs=held,
        compiler_params=pltpu.CompilerParams(vmem_limit_bytes=4 * MIB),
    )(neighbours.transpose(2, 0, 1))


def dot(a, b):
    return jnp.dot(a, b, preferred_element_type=jnp.float32)


def finish(before, inner_sum, outer, gains):
    hidden = jax.nn.silu(inner_sum).astype(jnp.bfloat16)
    output = dot(hidden, outer)
    center = output - jnp.mean(output, axis=-1, keepdims=True)
    spread_of = jnp.mean(center * center, axis=-1, keepdims=True)
    scaled = center * lax.rsqrt(spread_of + EPSILON) * gains
    return (before.astype(jnp.float32) + scaled).astype(jnp.bfloat16)


def fine_layer(layer, fine, picks, latents, left, right, above, below, inner, outer, gain, rows):
    edges, features = fine.shape
    nodes = latents.shape[0]
    hidden = inner.shape[2]
    near = (BAND + 2) * rows
    own = BAND * rows
    columns = above.shape[0]
    steps = nodes // own
    block = edges // steps
    degree = edges // nodes

    halo = (left, right, above, below)

    def body(fine_ref, picks_ref, latents_ref, left_away, right_away, above_away, below_away, inner_ref, outer_ref, gain_ref,
             next_ref, sum_ref, send_ref, recv_ref, table_ref, left_ref, right_ref, above_ref, below_ref, sems):
        step = pl.program_id(0)

        @pl.when(step == 0)
        def _():
            fetch(
                [(left_away, left_ref), (right_away, right_ref), (above_away, above_ref), (below_away, below_ref)], sems
            )
            send = inner_ref[layer, features : 2 * features, :]
            project = lambda ref: dot(ref[...], send).astype(jnp.bfloat16)
            table_ref[ABOVE:, :] = jnp.zeros((256 - ABOVE, hidden), jnp.bfloat16)
            table_ref[ABOVE : ABOVE + columns, :] = project(above_ref)
            table_ref[BELOW : BELOW + columns, :] = project(below_ref)
            send_ref[rows : rows + nodes, :] = project(latents_ref)
            recv_ref[...] = dot(latents_ref[...], inner_ref[layer, 2 * features :, :]).astype(jnp.bfloat16)
            side = project(left_ref)
            send_ref[:rows, :] = side[:rows]
            table_ref[ABOVE + columns : ABOVE + columns + 1, :] = side[rows : rows + 1]
            table_ref[BELOW + columns : BELOW + columns + 1, :] = side[rows + 1 : rows + 2]
            side = project(right_ref)
            send_ref[rows + nodes :, :] = side[:rows]
            table_ref[ABOVE + columns + 1 : ABOVE + columns + 2, :] = side[rows : rows + 1]
            table_ref[BELOW + columns + 1 : BELOW + columns + 2, :] = side[rows + 1 : rows + 2]

        start = pl.multiple_of(step * own, own)
        table_ref[:near, :] = send_ref[pl.ds(start, near), :]
        table_ref[near : near + own, :] = recv_ref[pl.ds(start, own), :]
        before = fine_ref[...]
        total = dot(before, inner_ref[layer, :features, :]) + dot(picks_ref[...], table_ref[...])
        after = finish(before, total, outer_ref[layer], gain_ref[layer : layer + 1, :])
        next_ref[...] = after
        split = after.astype(jnp.float32).reshape(BAND, degree, rows, features)
        sum_ref[...] = jnp.sum(split, axis=1).reshape(own, features)

    held = pl.BlockSpec(memory_space=pltpu.VMEM)
    return pl.pallas_call(
        body,
        name=f"fine{layer}",
        out_shape=(
            jax.ShapeDtypeStruct(fine.shape, jnp.bfloat16),
            jax.ShapeDtypeStruct((nodes, features), jnp.float32),
        ),
        grid=(steps,),
        in_specs=[
            pl.BlockSpec((block, features), lambda i: (i, 0)),
            pl.BlockSpec((block, 256), lambda i: (i, 0)),
        ]
        + [held]
        + [pl.BlockSpec(memory_space=pl.ANY)] * 4
        + [held] * 3,
        out_specs=(
            pl.BlockSpec((block, features), lambda i: (i, 0)),
            pl.BlockSpec((own, features), lambda i: (i, 0)),
        ),
        scratch_shapes=[
            pltpu.VMEM((nodes + 2 * rows, hidden), jnp.bfloat16),
            pltpu.VMEM((nodes, hidden), jnp.bfloat16),
            pltpu.VMEM((256, hidden), jnp.bfloat16),
            *(pltpu.VMEM(part.shape, jnp.bfloat16) for part in halo),
            pltpu.SemaphoreType.DMA((4,)),
        ],
        compiler_params=pltpu.CompilerParams(dimension_semantics=("arbitrary",), vmem_limit_bytes=14 * MIB),
    )(fine, picks, latents, *(map(in_hbm, halo) if layer == 0 else halo), inner, outer, gain)


def pick(index, width):
    lanes = lax.broadcasted_iota(jnp.int32, (index.shape[0], width), 1)
    return (lanes == index).astype(jnp.bfloat16)


def rows_to_columns(left, right):
    return lax.dot_general(left, right, (((1,), (1,)), ((), ())), preferred_element_type=jnp.float32)


def decode(tags, at):
    numbers = tags.astype(jnp.int32)
    return jnp.where(numbers[:, 4:5] > 0, numbers[:, at : at + 1] * LOW + numbers[:, at + 1 : at + 2], -1)


def send_rows(both, own_ref, last_ref, first_ref):
    rows = both.astype(jnp.bfloat16)
    count, columns = own_ref.shape[0], last_ref.shape[0]
    own_ref[...] = rows[:count]
    last_ref[...] = rows[count : count + columns]
    first_ref[...] = rows[count + columns :]


def join_far(own, fars, above, below, last_column, first_column):
    count, features = own.shape
    rows = last_column.shape[0]

    def body(own_ref, far1_ref, far2_ref, far3_ref, above_ref, below_ref, last_ref, first_ref, four_ref, right_ref, left_ref):
        for at, ref in enumerate((own_ref, far1_ref, far2_ref, far3_ref)):
            four_ref[at * count : (at + 1) * count, :] = ref[...]
        end = above_ref.shape[0] - 1
        for out_ref, line_ref, at in ((right_ref, last_ref, end), (left_ref, first_ref, 0)):
            out_ref[:rows, :] = line_ref[...]
            out_ref[rows : rows + 1, :] = above_ref[at : at + 1, :]
            out_ref[rows + 1 :, :] = below_ref[at : at + 1, :]

    held = pl.BlockSpec(memory_space=pltpu.VMEM)
    return pl.pallas_call(
        body,
        name="join_far",
        out_shape=tuple(jax.ShapeDtypeStruct((n, features), jnp.bfloat16) for n in (4 * count, rows + 2, rows + 2)),
        in_specs=[held] * 8,
        out_specs=(held,) * 3,
        compiler_params=pltpu.CompilerParams(vmem_limit_bytes=2 * MIB),
    )(own, *fars, above, below, last_column, first_column)


def in_hbm(values):
    return pltpu.with_memory_space_constraint(values, pltpu.HBM)


def fetch(pairs, sems):
    copies = [pltpu.make_async_copy(here, there, sems.at[i]) for i, (here, there) in enumerate(pairs)]
    for copy in copies:
        copy.start()
    for copy in copies:
        copy.wait()


def join_near(layer, *parts):
    each, features = parts[0].shape
    count = len(parts)
    far = layer == 0
    shape = (count * each, features)

    def body(*refs):
        joined_ref, sems, *near = refs[count:]
        to = near[0] if far else joined_ref
        fetch([(ref, to.at[pl.ds(at * each, each), :]) for at, ref in enumerate(refs[:count])], sems)
        if far:
            fetch([(to, joined_ref)], sems)

    away = pl.BlockSpec(memory_space=pl.ANY)
    return pl.pallas_call(
        body,
        name="join_near",
        cost_estimate=pl.CostEstimate(flops=3_000_000_000, bytes_accessed=0, transcendentals=0),
        out_shape=pltpu.HBM(shape, jnp.bfloat16) if far else jax.ShapeDtypeStruct(shape, jnp.bfloat16),
        in_specs=[away] * count,
        out_specs=away,
        scratch_shapes=[pltpu.SemaphoreType.DMA((count,))] + ([pltpu.VMEM(shape, jnp.bfloat16)] if far else []),
        compiler_params=pltpu.CompilerParams(vmem_limit_bytes=2 * MIB),
    )(*(map(in_hbm, parts) if far else parts))


def coarse_start(coarse_slots, latents, rows, columns):
    count = coarse_slots.shape[1]
    nodes, features = latents.shape
    size = count + 2 * columns

    def body(slots_away, latents_away, own_ref, last_ref, first_ref, left_ref, right_ref, choose_ref, slots_ref, latents_ref, sems):
        fetch([(slots_away, slots_ref), (latents_away, latents_ref)], sems)
        slot = slots_ref[...]
        row = jnp.floor((slot.astype(jnp.float32) + 0.5) * (1.0 / columns)).astype(jnp.int32)
        at = (slot - row * columns) * rows + row
        place = (lax.broadcasted_iota(jnp.int32, (nodes, count), 0) == at).astype(jnp.bfloat16)
        out = lax.broadcasted_iota(jnp.int32, (size, count), 0)
        same = (out == lax.broadcasted_iota(jnp.int32, (size, count), 1)).astype(jnp.bfloat16)
        out = lax.broadcasted_iota(jnp.int32, (size, nodes), 0)
        node = lax.broadcasted_iota(jnp.int32, (size, nodes), 1)
        edge = ((out >= count) & (out < count + columns) & (node == (out - count) * rows + rows - 1)) | (
            (out >= count + columns) & (node == (out - count - columns) * rows)
        )
        choose = (rows_to_columns(same, place) + edge.astype(jnp.float32)).astype(jnp.bfloat16)
        choose_ref[...] = choose
        send_rows(dot(choose, latents_ref[...]), own_ref, last_ref, first_ref)
        left_ref[...] = latents_ref[:rows, :]
        right_ref[...] = latents_ref[-rows:, :]

    shapes = (
        *(jax.ShapeDtypeStruct((n, features), jnp.bfloat16) for n in (count, columns, columns, rows, rows)),
        jax.ShapeDtypeStruct((size, nodes), jnp.bfloat16),
    )
    away = pl.BlockSpec(memory_space=pltpu.HBM)
    held = pl.BlockSpec(memory_space=pltpu.VMEM)
    return pl.pallas_call(
        body,
        name="coarse_start",
        out_shape=shapes,
        in_specs=[away] * 2,
        out_specs=(held,) * len(shapes),
        scratch_shapes=[
            pltpu.VMEM(coarse_slots.shape, jnp.int32),
            pltpu.VMEM(latents.shape, jnp.bfloat16),
            pltpu.SemaphoreType.DMA((2,)),
        ],
        compiler_params=pltpu.CompilerParams(vmem_limit_bytes=4 * MIB),
    )(*map(in_hbm, (coarse_slots, latents)))


def pack_edges(long_edges, senders, receivers, me, coarse_count, devices):
    count, features = long_edges.shape
    blocks = features // TAGS
    slots = devices * CAP

    def body(me_ref, long_away, send_away, recv_away, sent_ref, mine_ref, wide, long_ref, send_ref, recv_ref, sems):
        fetch([(long_away, long_ref), (send_away, send_ref), (recv_away, recv_ref)], sems)
        send, recv = send_ref[...], recv_ref[...]
        _, owner = table_row(0, 0, recv, coarse_count)
        here = (lax.shift_right_logical(me_ref[0], 3), me_ref[0] & 7)
        there = (lax.shift_right_logical(owner, 3), owner & 7)
        field = lax.broadcasted_iota(jnp.int32, (TAGS, count), 0)

        def fields(digits):
            sender = table_row(*digits, send, coarse_count)[0]
            receiver = table_row(*digits, recv, coarse_count)[0]
            both = jnp.where(field < 2, sender, receiver)
            high = lax.shift_right_logical(both, LOW.bit_length() - 1)
            value = jnp.where(field % 2 == 0, high, both & (LOW - 1))
            value = jnp.where(field == 4, 1, jnp.where(field == 5, owner, value))
            return jnp.where(field < 6, value, 0).astype(jnp.float32).astype(jnp.bfloat16)

        down = lax.broadcasted_iota(jnp.int32, (count, count), 0)
        across = lax.broadcasted_iota(jnp.int32, (count, count), 1)
        mine = rows_to_columns((down == across).astype(jnp.bfloat16), fields(here))
        mine_ref[...] = mine.astype(jnp.bfloat16)
        same = (mine[:, 5:6].astype(jnp.int32) == owner) & (down < across)
        rank = jnp.sum(same.astype(jnp.float32), axis=0, keepdims=True).astype(jnp.int32)
        spot = rank * devices + owner
        place = (lax.broadcasted_iota(jnp.int32, (slots, count), 0) == spot).astype(jnp.bfloat16)
        edges = dot(place, long_ref[...])
        tags = rows_to_columns(place, fields(there))
        for j in range(CAP):
            part = slice(j * devices, (j + 1) * devices)
            for b in range(blocks):
                wide[pl.ds(j * blocks + b, devices, stride=16), :] = edges[part, b * TAGS : (b + 1) * TAGS]
            wide[pl.ds(CAP * blocks + j, devices, stride=16), :] = tags[part]
        wide[pl.ds(15, devices, stride=16), :] = jnp.zeros((devices, TAGS), jnp.float32)
        sent_ref[...] = wide[...].astype(jnp.bfloat16)

    shapes = (
        jax.ShapeDtypeStruct((devices * 16, TAGS), jnp.bfloat16),
        jax.ShapeDtypeStruct((count, TAGS), jnp.bfloat16),
    )
    return pl.pallas_call(
        body,
        name="pack_edges",
        out_shape=shapes,
        cost_estimate=pl.CostEstimate(flops=12_000_000_000, bytes_accessed=0, transcendentals=0),
        in_specs=[pl.BlockSpec(memory_space=pltpu.SMEM)] + [pl.BlockSpec(memory_space=pltpu.HBM)] * 3,
        out_specs=(pl.BlockSpec(memory_space=pltpu.VMEM),) * 2,
        scratch_shapes=[
            pltpu.VMEM((devices * 16, TAGS), jnp.float32),
            pltpu.VMEM(long_edges.shape, jnp.bfloat16),
            pltpu.VMEM(senders.shape, jnp.int32),
            pltpu.VMEM(receivers.shape, jnp.int32),
            pltpu.SemaphoreType.DMA((3,)),
        ],
        compiler_params=pltpu.CompilerParams(vmem_limit_bytes=8 * MIB),
    )(me, *map(in_hbm, (long_edges, senders, receivers)))


def unpack_edges(arrived, choose, features, table_rows, coarse_count):
    devices = arrived.shape[0] // 16
    blocks = features // TAGS
    slots = devices * CAP
    nodes = choose.shape[1]

    def body(arrived_ref, choose_ref, rows_ref, send_ref, recv_ref, adds_ref, wide):
        wide[...] = arrived_ref[...].astype(jnp.float32)
        for j in range(CAP):
            part = slice(j * devices, (j + 1) * devices)
            for b in range(blocks):
                lanes = slice(b * TAGS, (b + 1) * TAGS)
                rows_ref[part, lanes] = wide[pl.ds(j * blocks + b, devices, stride=16), :].astype(jnp.bfloat16)
            tags = wide[pl.ds(CAP * blocks + j, devices, stride=16), :]
            send_ref[part, :] = pick(decode(tags, 0), table_rows)
            recv_ref[part, :] = pick(decode(tags, 2), TAGS)
        here = recv_ref[:, :coarse_count]
        place = lax.dot_general(
            choose_ref[:coarse_count, :], here, (((0,), (1,)), ((), ())), preferred_element_type=jnp.float32
        )
        adds_ref[...] = place.astype(jnp.bfloat16)

    held = pl.BlockSpec(memory_space=pltpu.VMEM)
    return pl.pallas_call(
        body,
        name="unpack_edges",
        out_shape=(
            jax.ShapeDtypeStruct((slots, features), jnp.bfloat16),
            jax.ShapeDtypeStruct((slots, table_rows), jnp.bfloat16),
            jax.ShapeDtypeStruct((slots, TAGS), jnp.bfloat16),
            jax.ShapeDtypeStruct((nodes, slots), jnp.bfloat16),
        ),
        in_specs=[held] * 2,
        out_specs=(held,) * 4,
        scratch_shapes=[pltpu.VMEM(arrived.shape, jnp.float32)],
        compiler_params=pltpu.CompilerParams(vmem_limit_bytes=8 * MIB),
    )(arrived, choose)


def long_step(before, sent, got, inner_ref, outer_ref, gain_ref, layer):
    features = before.shape[1]
    total = dot(before, inner_ref[layer, :features, :])
    total += dot(sent, inner_ref[layer, features : 2 * features, :])
    total += dot(got, inner_ref[layer, 2 * features :, :])
    return finish(before, total, outer_ref[layer], gain_ref[layer : layer + 1, :])


def coarse_layer(layer, long_rows, own_rows, sends, recvs, adds, choose, pieces, latents, fine_sum,
                 edge_inner, edge_outer, edge_gain, node_inner, node_outer, node_gain, coarse_count, last):
    slots = long_rows.shape[0]
    nodes, features = latents.shape
    count = len(pieces)
    each = pieces[0].shape[0]
    table_rows = count * each
    both = slots + own_rows.shape[0]

    def body(long_ref, own_ref, sends_ref, recvs_ref, adds_ref, choose_ref, latents_ref, sum_ref,
             ei_ref, eo_ref, eg_ref, ni_ref, no_ref, ng_ref, *rest):
        piece_refs = rest[:count]
        next_ref, *outs, ni, no, sems = rest[count:]
        table = outs[1] if last else outs[4]
        weights = [
            pltpu.make_async_copy(ni_ref.at[layer], ni, sems.at[0]),
            pltpu.make_async_copy(no_ref.at[layer], no, sems.at[1]),
        ]
        for copy in weights:
            copy.start()
        for p in range(count):
            table[p * each : (p + 1) * each, :] = piece_refs[p][...]
        got = dot(recvs_ref[...], table[:TAGS, :]).astype(jnp.bfloat16)
        if last:
            picked = dot(sends_ref[...], table[...]).astype(jnp.bfloat16)
            before = jnp.concatenate([long_ref[...], own_ref[...]], axis=0)
            got = jnp.concatenate([got, picked[both:]], axis=0)
            after = long_step(before, picked[:both], got, ei_ref, eo_ref, eg_ref, layer)
            outs[0][...] = after[slots:]
            after = after[:slots]
        else:
            sent = dot(sends_ref[...], table[...]).astype(jnp.bfloat16)
            after = long_step(long_ref[...], sent, got, ei_ref, eo_ref, eg_ref, layer)
            outs[0][...] = after
        incoming = (sum_ref[...] + dot(adds_ref[...], after)).astype(jnp.bfloat16)
        old = latents_ref[...]
        for copy in weights:
            copy.wait()
        total = dot(old, ni[:features, :]) + dot(incoming, ni[features:, :])
        new = finish(old, total, no[...], ng_ref[layer : layer + 1, :])
        next_ref[...] = new
        if not last:
            send_rows(dot(choose_ref[...], new), *outs[1:4])
            outs[5][...] = new[:rows]
            outs[6][...] = new[-rows:]

    held = pl.BlockSpec(memory_space=pltpu.VMEM)
    away = pl.BlockSpec(memory_space=pltpu.HBM)
    table_shape = (table_rows, features)
    side = (choose.shape[0] - coarse_count) // 2
    rows = nodes // side
    kept = (both - slots,) if last else (slots, coarse_count, side, side, table_rows, rows, rows)
    shapes = [jax.ShapeDtypeStruct((n, features), jnp.bfloat16) for n in (nodes, *kept)]

    return pl.pallas_call(
        body,
        name=f"coarse{layer}",
        out_shape=tuple(shapes),
        in_specs=[held] * 11 + [away] * 2 + [held] * (1 + count),
        out_specs=(held,) * len(shapes),
        scratch_shapes=([pltpu.VMEM(table_shape, jnp.bfloat16)] if last else [])
        + [
            pltpu.VMEM(node_inner.shape[1:], jnp.bfloat16),
            pltpu.VMEM(node_outer.shape[1:], jnp.bfloat16),
            pltpu.SemaphoreType.DMA((2,)),
        ],
        compiler_params=pltpu.CompilerParams(vmem_limit_bytes=(18 if last else 14) * MIB),
    )(long_rows, own_rows, sends, recvs, adds, choose, latents, fine_sum,
      edge_inner, edge_outer, edge_gain, node_inner, node_outer, node_gain, *pieces)


def own_layer(layer, long_rows, tags, sends, table, edge_inner, edge_outer, edge_gain):
    count = long_rows.shape[0]
    slots, rows = sends.shape

    def body(long_ref, tags_ref, sends_ref, table_ref, ei_ref, eo_ref, eg_ref, next_ref, all_ref):
        mine = tags_ref[...].astype(jnp.float32)
        all_ref[:slots, :] = sends_ref[...]
        all_ref[slots : slots + count, :] = pick(decode(mine, 0), rows)
        all_ref[slots + count :, :] = pick(decode(mine, 2), rows)
        picked = dot(all_ref[slots:, :], table_ref[...]).astype(jnp.bfloat16)
        next_ref[...] = long_step(long_ref[...], picked[:count], picked[count:], ei_ref, eo_ref, eg_ref, layer)

    held = pl.BlockSpec(memory_space=pltpu.VMEM)
    return pl.pallas_call(
        body,
        name=f"own{layer}",
        out_shape=(
            jax.ShapeDtypeStruct(long_rows.shape, jnp.bfloat16),
            jax.ShapeDtypeStruct((slots + 2 * count, rows), jnp.bfloat16),
        ),
        in_specs=[held] * 7,
        out_specs=(held, held),
        compiler_params=pltpu.CompilerParams(vmem_limit_bytes=8 * MIB),
    )(long_rows, tags, sends, table, edge_inner, edge_outer, edge_gain)


def shards(
    node_latents,
    fine_edges,
    long_edges,
    neighbours,
    coarse_slots,
    long_senders,
    long_receivers,
    edge_inner,
    edge_outer,
    edge_gain,
    node_inner,
    node_outer,
    node_gain,
):
    rows, columns, features = node_latents.shape
    degree = fine_edges.shape[2]
    nodes = rows * columns
    coarse_count = coarse_slots.shape[0]
    layers = edge_inner.shape[0]
    devices = lax.axis_size("px") * lax.axis_size("py")

    latents = node_latents.transpose(1, 0, 2).reshape(nodes, features)
    fine = fine_edges.transpose(1, 2, 0, 3).reshape(nodes * degree, features)
    own, last_row, first_row, to_left, to_right, choose = coarse_start(coarse_slots[None, :], latents, rows, columns)
    long_edges, own = tie(long_edges, own)
    own_rows = long_edges
    me = lax.axis_index(AXES).reshape(1)
    payload, own_tags = pack_edges(long_edges, long_senders[None, :], long_receivers[None, :], me, coarse_count, devices)
    for layer in range(layers):
        last = layer == layers - 1
        fars = [along(own, "px", 4 * s) for s in (1, 2, 3)]
        above = along(last_row, "px", 1)
        below = along(first_row, "px", -1)
        if layer == 0:
            *fars, above, below, payload = tie(*fars, above, below, payload)
            packed = payload.reshape(devices, 16, TAGS)
            arrived = lax.all_to_all(packed, AXES, split_axis=0, concat_axis=0, tiled=True).reshape(payload.shape)
        four, to_right, to_left = join_far(own, fars, above, below, to_right, to_left)
        left = along(to_right, "py", 1)
        right = along(to_left, "py", -1)
        *nears, left, right = tie(*(around_x(four, s) for s in (1, 2, 3)), left, right)
        joined = join_near(layer, four, *nears)
        joined, left, right, own_rows = tie(joined, left, right, own_rows)
        pieces = [joined] + [shift(joined, Z, s) for s in (1, 2, 3)]
        if layer == 0:
            table_rows = 2 * len(pieces) * joined.shape[0]
            long_rows, sends, recvs, adds = unpack_edges(arrived, choose, features, table_rows, coarse_count)
            left, long_rows, neighbours = tie(left, long_rows, neighbours)
            picks = selection(neighbours)
        else:
            own_rows, sends = own_layer(layer - 1, own_rows, own_tags, sends, table, edge_inner, edge_outer, edge_gain)
        fine, fine_sum = fine_layer(
            layer, fine, picks, latents, left, right, above, below, edge_inner, edge_outer, edge_gain, rows
        )
        swapped = shift(joined, CORE, 1)
        *others, fine_sum, own_rows, long_rows = tie(*pieces[1:], fine_sum, own_rows, long_rows)
        pieces = [joined] + others + [swapped] + [shift(piece, CORE, 1) for piece in others]
        latents, *rest = coarse_layer(
            layer, long_rows, own_rows, sends, recvs, adds, choose, pieces, latents, fine_sum,
            edge_inner, edge_outer, edge_gain, node_inner, node_outer, node_gain, coarse_count, last,
        )
        if last:
            own_rows = rest[0]
        else:
            long_rows, own, last_row, first_row, table, to_left, to_right = rest
    return (
        latents.reshape(columns, rows, features).transpose(1, 0, 2),
        fine.reshape(columns, degree, rows, features).transpose(2, 0, 1, 3),
        own_rows,
    )


def solution(mesh):
    in_specs = (
        P("px", "py", None),
        P("px", "py", None, None),
        P(AXES, None),
        P("px", "py", None),
        P(AXES),
        P(AXES),
        P(AXES),
        P(),
        P(),
        P(),
        P(),
        P(),
        P(),
    )
    out_specs = (P("px", "py", None), P("px", "py", None, None), P(AXES, None))
    return jax.shard_map(shards, mesh=mesh, in_specs=in_specs, out_specs=out_specs, check_vma=False)
```

```python
import jax
import jax.numpy as jnp
from jax import lax
from jax.experimental import pallas as pl
from jax.experimental.pallas import tpu as pltpu
from jax.sharding import PartitionSpec as P

EPSILON = 1e-05
AXES = ("px", "py")
Z, CORE = (2, 4), (1, 2)
BAND = 4
TAGS = 128
LOW = 64
CAP = 3
ABOVE, BELOW = 160, 192
MIB = 1024 * 1024


def shift(values, digit, step):
    stride, size = digit
    pairs = []
    for i in range(8):
        here = i // stride % size
        pairs.append((i, i + ((here + step) % size - here) * stride))
    return lax.ppermute(values, "py", pairs)


def tie(*values):
    return lax.optimization_barrier(values)


def table_row(px, py, coarse, coarse_count):
    home = jnp.floor((coarse.astype(jnp.float32) + 0.5) * (1.0 / coarse_count)).astype(jnp.int32)
    row = coarse - home * coarse_count
    home_px = lax.shift_right_logical(home, 3)
    near = (px - home_px) & 3
    x = px & 3
    turn = jnp.where((near == 1) & (x == 0), -1, jnp.where((near == 3) & (x == 3), 1, 0))
    far = (lax.shift_right_logical(px, 2) + turn - lax.shift_right_logical(home_px, 2)) & 3
    home_z, home_core = lax.shift_right_logical(home, 1) & 3, home & 1
    kz = (lax.shift_right_logical(py, 1) - home_z) & 3
    kc = (py - home_core) & 1
    return (((kc * 4 + kz) * 4 + near) * 4 + far) * coarse_count + row, home


def around_x(values, step):
    return lax.ppermute(values, "px", [(i, i // 4 * 4 + (i + step) % 4) for i in range(16)])


def along(values, axis, step):
    count = lax.axis_size(axis)
    return lax.ppermute(values, axis, [(i, (i + step) % count) for i in range(count)])


def selection(neighbours):
    rows, columns, degree = neighbours.shape

    def body(codes_ref, picks_ref):
        codes = codes_ref[...]
        q = codes + (codes >= 4).astype(jnp.int32)
        down = (q >= 3).astype(jnp.int32) + (q >= 6).astype(jnp.int32)
        step = q - 3 * down
        from_row = lax.broadcasted_iota(jnp.int32, codes.shape, 1) + down - 1
        column = lax.broadcasted_iota(jnp.int32, codes.shape, 2)
        near = ((column & (BAND - 1)) + step) * rows + from_row
        sender = jnp.where(from_row < 0, ABOVE + column + step, jnp.where(from_row >= rows, BELOW + column + step, near))
        lanes = lax.broadcasted_iota(jnp.int32, (rows, 256), 1)
        row = lax.broadcasted_iota(jnp.int32, (rows, 256), 0)
        for c in range(columns):
            receiver = lanes == (BAND + 2 + c % BAND) * rows + row
            for k in range(degree):
                picks = (lanes == sender[k, :, c : c + 1]) | receiver
                picks_ref[(c * degree + k) * rows : (c * degree + k + 1) * rows, :] = picks.astype(jnp.bfloat16)

    held = pl.BlockSpec(memory_space=pltpu.VMEM)
    return pl.pallas_call(
        body,
        name="selection",
        out_shape=jax.ShapeDtypeStruct((rows * columns * degree, 256), jnp.bfloat16),
        in_specs=[held],
        out_specs=held,
        compiler_params=pltpu.CompilerParams(vmem_limit_bytes=4 * MIB),
    )(neighbours.transpose(2, 0, 1))


def dot(a, b):
    return jnp.dot(a, b, preferred_element_type=jnp.float32)


def finish(before, inner_sum, outer, gains):
    hidden = jax.nn.silu(inner_sum).astype(jnp.bfloat16)
    output = dot(hidden, outer)
    center = output - jnp.mean(output, axis=-1, keepdims=True)
    spread_of = jnp.mean(center * center, axis=-1, keepdims=True)
    scaled = center * lax.rsqrt(spread_of + EPSILON) * gains
    return (before.astype(jnp.float32) + scaled).astype(jnp.bfloat16)


def fine_layer(layer, fine, picks, latents, left, right, sides, inner, outer, gain, rows):
    edges, features = fine.shape
    nodes = latents.shape[0]
    hidden = inner.shape[2]
    near = (BAND + 2) * rows
    own = BAND * rows
    steps = nodes // own
    block = edges // steps
    degree = edges // nodes

    def body(fine_ref, picks_ref, latents_ref, left_ref, right_ref, sides_ref, inner_ref, outer_ref, gain_ref,
             next_ref, sum_ref, send_ref, recv_ref, table_ref):
        step = pl.program_id(0)

        @pl.when(step == 0)
        def _():
            send = inner_ref[layer, features : 2 * features, :]
            project = lambda ref: dot(ref[...], send).astype(jnp.bfloat16)
            table_ref[ABOVE : ABOVE + sides.shape[0], :] = project(sides_ref)
            table_ref[ABOVE + sides.shape[0] :, :] = jnp.zeros((256 - ABOVE - sides.shape[0], hidden), jnp.bfloat16)
            send_ref[rows : rows + nodes, :] = project(latents_ref)
            recv_ref[...] = dot(latents_ref[...], inner_ref[layer, 2 * features :, :]).astype(jnp.bfloat16)
            send_ref[:rows, :] = project(left_ref)
            send_ref[rows + nodes :, :] = project(right_ref)

        start = pl.multiple_of(step * own, own)
        table_ref[:near, :] = send_ref[pl.ds(start, near), :]
        table_ref[near : near + own, :] = recv_ref[pl.ds(start, own), :]
        before = fine_ref[...]
        total = dot(before, inner_ref[layer, :features, :]) + dot(picks_ref[...], table_ref[...])
        after = finish(before, total, outer_ref[layer], gain_ref[layer : layer + 1, :])
        next_ref[...] = after
        split = after.astype(jnp.float32).reshape(BAND, degree, rows, features)
        sum_ref[...] = jnp.sum(split, axis=1).reshape(own, features)

    held = pl.BlockSpec(memory_space=pltpu.VMEM)
    return pl.pallas_call(
        body,
        name=f"fine{layer}",
        out_shape=(
            jax.ShapeDtypeStruct(fine.shape, jnp.bfloat16),
            jax.ShapeDtypeStruct((nodes, features), jnp.float32),
        ),
        grid=(steps,),
        in_specs=[
            pl.BlockSpec((block, features), lambda i: (i, 0)),
            pl.BlockSpec((block, 256), lambda i: (i, 0)),
        ]
        + [held] * 7,
        out_specs=(
            pl.BlockSpec((block, features), lambda i: (i, 0)),
            pl.BlockSpec((own, features), lambda i: (i, 0)),
        ),
        scratch_shapes=[
            pltpu.VMEM((nodes + 2 * rows, hidden), jnp.bfloat16),
            pltpu.VMEM((nodes, hidden), jnp.bfloat16),
            pltpu.VMEM((256, hidden), jnp.bfloat16),
        ],
        compiler_params=pltpu.CompilerParams(dimension_semantics=("arbitrary",), vmem_limit_bytes=14 * MIB),
    )(fine, picks, latents, left, right, sides, inner, outer, gain)


def pick(index, width):
    lanes = lax.broadcasted_iota(jnp.int32, (index.shape[0], width), 1)
    return (lanes == index).astype(jnp.bfloat16)


def rows_to_columns(left, right):
    return lax.dot_general(left, right, (((1,), (1,)), ((), ())), preferred_element_type=jnp.float32)


def decode(tags, at):
    numbers = tags.astype(jnp.int32)
    return jnp.where(numbers[:, 4:5] > 0, numbers[:, at : at + 1] * LOW + numbers[:, at + 1 : at + 2], -1)


def send_rows(both, own_ref, last_ref, first_ref):
    rows = both.astype(jnp.bfloat16)
    count, columns = own_ref.shape[0], last_ref.shape[0]
    own_ref[...] = rows[:count]
    last_ref[...] = rows[count : count + columns]
    first_ref[...] = rows[count + columns :]


def join_far(own, fars, left, right, last, first):
    count, features = own.shape
    rows = left.shape[0]
    four = 4 * count
    columns = last.shape[0]

    def body(own_ref, far1_ref, far2_ref, far3_ref, left_ref, right_ref, last_ref, first_ref, two_ref, up_ref, down_ref):
        for at, ref in enumerate((own_ref, far1_ref, far2_ref, far3_ref)):
            two_ref[at * count : (at + 1) * count, :] = ref[...]
        for out_ref, line_ref, row in ((up_ref, last_ref, rows - 1), (down_ref, first_ref, 0)):
            out_ref[:four, :] = two_ref[...]
            out_ref[four:, :] = jnp.zeros((out_ref.shape[0] - four, features), jnp.bfloat16)
            out_ref[four : four + 1, :] = left_ref[row : row + 1, :]
            out_ref[four + 1 : four + 1 + columns, :] = line_ref[...]
            out_ref[four + 1 + columns : four + 2 + columns, :] = right_ref[row : row + 1, :]

    held = pl.BlockSpec(memory_space=pltpu.VMEM)
    return pl.pallas_call(
        body,
        name="join_far",
        out_shape=tuple(jax.ShapeDtypeStruct((n, features), jnp.bfloat16) for n in (four, four + 32, four + 32)),
        in_specs=[held] * 8,
        out_specs=(held,) * 3,
        compiler_params=pltpu.CompilerParams(vmem_limit_bytes=2 * MIB),
    )(own, *fars, left, right, last, first)


def in_hbm(values):
    return pltpu.with_memory_space_constraint(values, pltpu.HBM)


def fetch(pairs, sems):
    copies = [pltpu.make_async_copy(here, there, sems.at[i]) for i, (here, there) in enumerate(pairs)]
    for copy in copies:
        copy.start()
    for copy in copies:
        copy.wait()


def join_near(layer, own, up, two, down):
    each, features = own.shape
    side = BELOW - ABOVE

    far = layer == 0

    def body(own_ref, two_ref, up_ref, down_ref, joined_ref, sides_ref, sems, *near):
        to, beside = near or (joined_ref, sides_ref)
        part = lambda at: to.at[pl.ds(at * each, each), :]
        fetch(
            [
                (own_ref, part(0)),
                (up_ref.at[pl.ds(0, each), :], part(1)),
                (two_ref, part(2)),
                (down_ref.at[pl.ds(0, each), :], part(3)),
                (up_ref.at[pl.ds(each, side), :], beside.at[pl.ds(0, side), :]),
                (down_ref.at[pl.ds(each, side), :], beside.at[pl.ds(side, side), :]),
            ],
            sems,
        )
        if near:
            fetch([(to, joined_ref), (beside, sides_ref)], sems)

    away = pl.BlockSpec(memory_space=pl.ANY)
    place = pltpu.HBM if far else jax.ShapeDtypeStruct
    shapes = ((4 * each, features), (2 * side, features))
    operands = (own, two, up, down)
    return pl.pallas_call(
        body,
        name="join_near",
        cost_estimate=pl.CostEstimate(flops=3_000_000_000, bytes_accessed=0, transcendentals=0),
        out_shape=tuple(place(shape, jnp.bfloat16) for shape in shapes),
        in_specs=[away] * 4,
        out_specs=(away,) * 2,
        scratch_shapes=[pltpu.SemaphoreType.DMA((6,))]
        + [pltpu.VMEM(shape, jnp.bfloat16) for shape in shapes if far],
        compiler_params=pltpu.CompilerParams(vmem_limit_bytes=2 * MIB),
    )(*(map(in_hbm, operands) if far else operands))


def coarse_start(coarse_slots, latents, rows, columns):
    count = coarse_slots.shape[1]
    nodes, features = latents.shape
    size = count + 2 * columns

    def body(slots_away, latents_away, own_ref, last_ref, first_ref, left_ref, right_ref, choose_ref, slots_ref, latents_ref, sems):
        fetch([(slots_away, slots_ref), (latents_away, latents_ref)], sems)
        slot = slots_ref[...]
        row = jnp.floor((slot.astype(jnp.float32) + 0.5) * (1.0 / columns)).astype(jnp.int32)
        at = (slot - row * columns) * rows + row
        place = (lax.broadcasted_iota(jnp.int32, (nodes, count), 0) == at).astype(jnp.bfloat16)
        out = lax.broadcasted_iota(jnp.int32, (size, count), 0)
        same = (out == lax.broadcasted_iota(jnp.int32, (size, count), 1)).astype(jnp.bfloat16)
        out = lax.broadcasted_iota(jnp.int32, (size, nodes), 0)
        node = lax.broadcasted_iota(jnp.int32, (size, nodes), 1)
        edge = ((out >= count) & (out < count + columns) & (node == (out - count) * rows + rows - 1)) | (
            (out >= count + columns) & (node == (out - count - columns) * rows)
        )
        choose = (rows_to_columns(same, place) + edge.astype(jnp.float32)).astype(jnp.bfloat16)
        choose_ref[...] = choose
        send_rows(dot(choose, latents_ref[...]), own_ref, last_ref, first_ref)
        left_ref[...] = latents_ref[:rows, :]
        right_ref[...] = latents_ref[-rows:, :]

    shapes = (
        *(jax.ShapeDtypeStruct((n, features), jnp.bfloat16) for n in (count, columns, columns, rows, rows)),
        jax.ShapeDtypeStruct((size, nodes), jnp.bfloat16),
    )
    away = pl.BlockSpec(memory_space=pltpu.HBM)
    held = pl.BlockSpec(memory_space=pltpu.VMEM)
    return pl.pallas_call(
        body,
        name="coarse_start",
        out_shape=shapes,
        in_specs=[away] * 2,
        out_specs=(held,) * len(shapes),
        scratch_shapes=[
            pltpu.VMEM(coarse_slots.shape, jnp.int32),
            pltpu.VMEM(latents.shape, jnp.bfloat16),
            pltpu.SemaphoreType.DMA((2,)),
        ],
        compiler_params=pltpu.CompilerParams(vmem_limit_bytes=4 * MIB),
    )(*map(in_hbm, (coarse_slots, latents)))


def pack_edges(long_edges, senders, receivers, me, coarse_count, devices):
    count, features = long_edges.shape
    blocks = features // TAGS
    slots = devices * CAP

    def body(me_ref, long_away, send_away, recv_away, sent_ref, mine_ref, wide, long_ref, send_ref, recv_ref, sems):
        fetch([(long_away, long_ref), (send_away, send_ref), (recv_away, recv_ref)], sems)
        send, recv = send_ref[...], recv_ref[...]
        _, owner = table_row(0, 0, recv, coarse_count)
        here = (lax.shift_right_logical(me_ref[0], 3), me_ref[0] & 7)
        there = (lax.shift_right_logical(owner, 3), owner & 7)
        field = lax.broadcasted_iota(jnp.int32, (TAGS, count), 0)

        def fields(digits):
            sender = table_row(*digits, send, coarse_count)[0]
            receiver = table_row(*digits, recv, coarse_count)[0]
            both = jnp.where(field < 2, sender, receiver)
            high = lax.shift_right_logical(both, LOW.bit_length() - 1)
            value = jnp.where(field % 2 == 0, high, both & (LOW - 1))
            value = jnp.where(field == 4, 1, jnp.where(field == 5, owner, value))
            return jnp.where(field < 6, value, 0).astype(jnp.float32).astype(jnp.bfloat16)

        down = lax.broadcasted_iota(jnp.int32, (count, count), 0)
        across = lax.broadcasted_iota(jnp.int32, (count, count), 1)
        mine = rows_to_columns((down == across).astype(jnp.bfloat16), fields(here))
        mine_ref[...] = mine.astype(jnp.bfloat16)
        same = (mine[:, 5:6].astype(jnp.int32) == owner) & (down < across)
        rank = jnp.sum(same.astype(jnp.float32), axis=0, keepdims=True).astype(jnp.int32)
        spot = rank * devices + owner
        place = (lax.broadcasted_iota(jnp.int32, (slots, count), 0) == spot).astype(jnp.bfloat16)
        edges = dot(place, long_ref[...])
        tags = rows_to_columns(place, fields(there))
        for j in range(CAP):
            part = slice(j * devices, (j + 1) * devices)
            for b in range(blocks):
                wide[pl.ds(j * blocks + b, devices, stride=16), :] = edges[part, b * TAGS : (b + 1) * TAGS]
            wide[pl.ds(CAP * blocks + j, devices, stride=16), :] = tags[part]
        wide[pl.ds(15, devices, stride=16), :] = jnp.zeros((devices, TAGS), jnp.float32)
        sent_ref[...] = wide[...].astype(jnp.bfloat16)

    shapes = (
        jax.ShapeDtypeStruct((devices * 16, TAGS), jnp.bfloat16),
        jax.ShapeDtypeStruct((count, TAGS), jnp.bfloat16),
    )
    return pl.pallas_call(
        body,
        name="pack_edges",
        out_shape=shapes,
        cost_estimate=pl.CostEstimate(flops=12_000_000_000, bytes_accessed=0, transcendentals=0),
        in_specs=[pl.BlockSpec(memory_space=pltpu.SMEM)] + [pl.BlockSpec(memory_space=pltpu.HBM)] * 3,
        out_specs=(pl.BlockSpec(memory_space=pltpu.VMEM),) * 2,
        scratch_shapes=[
            pltpu.VMEM((devices * 16, TAGS), jnp.float32),
            pltpu.VMEM(long_edges.shape, jnp.bfloat16),
            pltpu.VMEM(senders.shape, jnp.int32),
            pltpu.VMEM(receivers.shape, jnp.int32),
            pltpu.SemaphoreType.DMA((3,)),
        ],
        compiler_params=pltpu.CompilerParams(vmem_limit_bytes=8 * MIB),
    )(me, *map(in_hbm, (long_edges, senders, receivers)))


def unpack_edges(arrived, choose, features, table_rows, coarse_count):
    devices = arrived.shape[0] // 16
    blocks = features // TAGS
    slots = devices * CAP
    nodes = choose.shape[1]

    def body(arrived_ref, choose_ref, rows_ref, send_ref, recv_ref, adds_ref, wide):
        wide[...] = arrived_ref[...].astype(jnp.float32)
        for j in range(CAP):
            part = slice(j * devices, (j + 1) * devices)
            for b in range(blocks):
                lanes = slice(b * TAGS, (b + 1) * TAGS)
                rows_ref[part, lanes] = wide[pl.ds(j * blocks + b, devices, stride=16), :].astype(jnp.bfloat16)
            tags = wide[pl.ds(CAP * blocks + j, devices, stride=16), :]
            send_ref[part, :] = pick(decode(tags, 0), table_rows)
            recv_ref[part, :] = pick(decode(tags, 2), TAGS)
        here = recv_ref[:, :coarse_count]
        place = lax.dot_general(
            choose_ref[:coarse_count, :], here, (((0,), (1,)), ((), ())), preferred_element_type=jnp.float32
        )
        adds_ref[...] = place.astype(jnp.bfloat16)

    held = pl.BlockSpec(memory_space=pltpu.VMEM)
    return pl.pallas_call(
        body,
        name="unpack_edges",
        out_shape=(
            jax.ShapeDtypeStruct((slots, features), jnp.bfloat16),
            jax.ShapeDtypeStruct((slots, table_rows), jnp.bfloat16),
            jax.ShapeDtypeStruct((slots, TAGS), jnp.bfloat16),
            jax.ShapeDtypeStruct((nodes, slots), jnp.bfloat16),
        ),
        in_specs=[held] * 2,
        out_specs=(held,) * 4,
        scratch_shapes=[pltpu.VMEM(arrived.shape, jnp.float32)],
        compiler_params=pltpu.CompilerParams(vmem_limit_bytes=8 * MIB),
    )(arrived, choose)


def long_step(before, sent, got, inner_ref, outer_ref, gain_ref, layer):
    features = before.shape[1]
    total = dot(before, inner_ref[layer, :features, :])
    total += dot(sent, inner_ref[layer, features : 2 * features, :])
    total += dot(got, inner_ref[layer, 2 * features :, :])
    return finish(before, total, outer_ref[layer], gain_ref[layer : layer + 1, :])


def coarse_layer(layer, long_rows, own_rows, sends, recvs, adds, choose, pieces, latents, fine_sum,
                 edge_inner, edge_outer, edge_gain, node_inner, node_outer, node_gain, coarse_count, last):
    slots = long_rows.shape[0]
    nodes, features = latents.shape
    count = len(pieces)
    each = pieces[0].shape[0]
    table_rows = count * each
    both = slots + own_rows.shape[0]

    def body(long_ref, own_ref, sends_ref, recvs_ref, adds_ref, choose_ref, latents_ref, sum_ref,
             ei_ref, eo_ref, eg_ref, ni_ref, no_ref, ng_ref, *rest):
        piece_refs = rest[:count]
        next_ref, *outs, ni, no, sems = rest[count:]
        table = outs[1] if last else outs[4]
        weights = [
            pltpu.make_async_copy(ni_ref.at[layer], ni, sems.at[0]),
            pltpu.make_async_copy(no_ref.at[layer], no, sems.at[1]),
        ]
        for copy in weights:
            copy.start()
        for p in range(count):
            table[p * each : (p + 1) * each, :] = piece_refs[p][...]
        got = dot(recvs_ref[...], table[:TAGS, :]).astype(jnp.bfloat16)
        if last:
            picked = dot(sends_ref[...], table[...]).astype(jnp.bfloat16)
            before = jnp.concatenate([long_ref[...], own_ref[...]], axis=0)
            got = jnp.concatenate([got, picked[both:]], axis=0)
            after = long_step(before, picked[:both], got, ei_ref, eo_ref, eg_ref, layer)
            outs[0][...] = after[slots:]
            after = after[:slots]
        else:
            sent = dot(sends_ref[...], table[...]).astype(jnp.bfloat16)
            after = long_step(long_ref[...], sent, got, ei_ref, eo_ref, eg_ref, layer)
            outs[0][...] = after
        incoming = (sum_ref[...] + dot(adds_ref[...], after)).astype(jnp.bfloat16)
        old = latents_ref[...]
        for copy in weights:
            copy.wait()
        total = dot(old, ni[:features, :]) + dot(incoming, ni[features:, :])
        new = finish(old, total, no[...], ng_ref[layer : layer + 1, :])
        next_ref[...] = new
        if not last:
            send_rows(dot(choose_ref[...], new), *outs[1:4])
            outs[5][...] = new[:rows]
            outs[6][...] = new[-rows:]

    held = pl.BlockSpec(memory_space=pltpu.VMEM)
    away = pl.BlockSpec(memory_space=pltpu.HBM)
    table_shape = (table_rows, features)
    side = (choose.shape[0] - coarse_count) // 2
    rows = nodes // side
    kept = (both - slots,) if last else (slots, coarse_count, side, side, table_rows, rows, rows)
    shapes = [jax.ShapeDtypeStruct((n, features), jnp.bfloat16) for n in (nodes, *kept)]

    return pl.pallas_call(
        body,
        name=f"coarse{layer}",
        out_shape=tuple(shapes),
        in_specs=[held] * 11 + [away] * 2 + [held] * (1 + count),
        out_specs=(held,) * len(shapes),
        scratch_shapes=([pltpu.VMEM(table_shape, jnp.bfloat16)] if last else [])
        + [
            pltpu.VMEM(node_inner.shape[1:], jnp.bfloat16),
            pltpu.VMEM(node_outer.shape[1:], jnp.bfloat16),
            pltpu.SemaphoreType.DMA((2,)),
        ],
        compiler_params=pltpu.CompilerParams(vmem_limit_bytes=(18 if last else 14) * MIB),
    )(long_rows, own_rows, sends, recvs, adds, choose, latents, fine_sum,
      edge_inner, edge_outer, edge_gain, node_inner, node_outer, node_gain, *pieces)


def own_layer(layer, long_rows, tags, sends, table, edge_inner, edge_outer, edge_gain):
    count = long_rows.shape[0]
    slots, rows = sends.shape

    def body(long_ref, tags_ref, sends_ref, table_ref, ei_ref, eo_ref, eg_ref, next_ref, all_ref):
        mine = tags_ref[...].astype(jnp.float32)
        all_ref[:slots, :] = sends_ref[...]
        all_ref[slots : slots + count, :] = pick(decode(mine, 0), rows)
        all_ref[slots + count :, :] = pick(decode(mine, 2), rows)
        picked = dot(all_ref[slots:, :], table_ref[...]).astype(jnp.bfloat16)
        next_ref[...] = long_step(long_ref[...], picked[:count], picked[count:], ei_ref, eo_ref, eg_ref, layer)

    held = pl.BlockSpec(memory_space=pltpu.VMEM)
    return pl.pallas_call(
        body,
        name=f"own{layer}",
        out_shape=(
            jax.ShapeDtypeStruct(long_rows.shape, jnp.bfloat16),
            jax.ShapeDtypeStruct((slots + 2 * count, rows), jnp.bfloat16),
        ),
        in_specs=[held] * 7,
        out_specs=(held, held),
        compiler_params=pltpu.CompilerParams(vmem_limit_bytes=8 * MIB),
    )(long_rows, tags, sends, table, edge_inner, edge_outer, edge_gain)


def shards(
    node_latents,
    fine_edges,
    long_edges,
    neighbours,
    coarse_slots,
    long_senders,
    long_receivers,
    edge_inner,
    edge_outer,
    edge_gain,
    node_inner,
    node_outer,
    node_gain,
):
    rows, columns, features = node_latents.shape
    degree = fine_edges.shape[2]
    nodes = rows * columns
    coarse_count = coarse_slots.shape[0]
    layers = edge_inner.shape[0]
    devices = lax.axis_size("px") * lax.axis_size("py")

    latents = node_latents.transpose(1, 0, 2).reshape(nodes, features)
    fine = fine_edges.transpose(1, 2, 0, 3).reshape(nodes * degree, features)
    own, last_row, first_row, to_left, to_right, choose = coarse_start(coarse_slots[None, :], latents, rows, columns)
    long_edges, own = tie(long_edges, own)
    own_rows = long_edges
    me = lax.axis_index(AXES).reshape(1)
    payload, own_tags = pack_edges(long_edges, long_senders[None, :], long_receivers[None, :], me, coarse_count, devices)
    for layer in range(layers):
        last = layer == layers - 1
        fars = [along(own, "px", 4 * s) for s in (1, 2, 3)]
        left = along(to_right, "py", 1)
        right = along(to_left, "py", -1)
        if layer == 0:
            *fars, left, right, payload = tie(*fars, left, right, payload)
        joined, up, down = join_far(own, fars, left, right, last_row, first_row)
        if layer == 0:
            packed = payload.reshape(devices, 16, TAGS)
            arrived = lax.all_to_all(packed, AXES, split_axis=0, concat_axis=0, tiled=True).reshape(payload.shape)
        two = around_x(joined, 2)
        up = along(up, "px", 1)
        down = along(down, "px", -1)
        joined, sides = join_near(layer, joined, up, two, down)
        joined, sides, own_rows = tie(joined, sides, own_rows)
        pieces = [joined] + [shift(joined, Z, s) for s in (1, 2, 3)]
        if layer == 0:
            table_rows = 2 * len(pieces) * joined.shape[0]
            long_rows, sends, recvs, adds = unpack_edges(arrived, choose, features, table_rows, coarse_count)
            left, long_rows, neighbours = tie(left, long_rows, neighbours)
            picks = selection(neighbours)
        else:
            own_rows, sends = own_layer(layer - 1, own_rows, own_tags, sends, table, edge_inner, edge_outer, edge_gain)
        fine, fine_sum = fine_layer(
            layer, fine, picks, latents, left, right, sides, edge_inner, edge_outer, edge_gain, rows
        )
        swapped = shift(joined, CORE, 1)
        *others, fine_sum, own_rows, long_rows = tie(*pieces[1:], fine_sum, own_rows, long_rows)
        pieces = [joined] + others + [swapped] + [shift(piece, CORE, 1) for piece in others]
        latents, *rest = coarse_layer(
            layer, long_rows, own_rows, sends, recvs, adds, choose, pieces, latents, fine_sum,
            edge_inner, edge_outer, edge_gain, node_inner, node_outer, node_gain, coarse_count, last,
        )
        if last:
            own_rows = rest[0]
        else:
            long_rows, own, last_row, first_row, table, to_left, to_right = rest
    return (
        latents.reshape(columns, rows, features).transpose(1, 0, 2),
        fine.reshape(columns, degree, rows, features).transpose(2, 0, 1, 3),
        own_rows,
    )


def solution(mesh):
    in_specs = (
        P("px", "py", None),
        P("px", "py", None, None),
        P(AXES, None),
        P("px", "py", None),
        P(AXES),
        P(AXES),
        P(AXES),
        P(),
        P(),
        P(),
        P(),
        P(),
        P(),
    )
    out_specs = (P("px", "py", None), P("px", "py", None, None), P(AXES, None))
    return jax.shard_map(shards, mesh=mesh, in_specs=in_specs, out_specs=out_specs, check_vma=False)
```

```python
import jax
import jax.numpy as jnp
from jax import lax
from jax.experimental import pallas as pl
from jax.experimental.pallas import tpu as pltpu
from jax.sharding import PartitionSpec as P

EPSILON = 1e-05
AXES = ("px", "py")
Z, CORE = (2, 4), (1, 2)
BAND = 4
TAGS = 128
LOW = 64
CAP = 3
ABOVE, BELOW = 160, 192
MIB = 1024 * 1024


def shift(values, digit, step):
    stride, size = digit
    pairs = []
    for i in range(8):
        here = i // stride % size
        pairs.append((i, i + ((here + step) % size - here) * stride))
    return lax.ppermute(values, "py", pairs)


def tie(*values):
    return lax.optimization_barrier(values)


def table_row(px, py, coarse, coarse_count):
    home = jnp.floor((coarse.astype(jnp.float32) + 0.5) * (1.0 / coarse_count)).astype(jnp.int32)
    row = coarse - home * coarse_count
    home_px = lax.shift_right_logical(home, 3)
    near = (px - home_px) & 3
    x = px & 3
    turn = jnp.where((near == 1) & (x == 0), -1, jnp.where((near == 3) & (x == 3), 1, 0))
    far = (lax.shift_right_logical(px, 2) + turn - lax.shift_right_logical(home_px, 2)) & 3
    home_z, home_core = lax.shift_right_logical(home, 1) & 3, home & 1
    kz = (lax.shift_right_logical(py, 1) - home_z) & 3
    kc = (py - home_core) & 1
    return (((kc * 4 + kz) * 4 + near) * 4 + far) * coarse_count + row, home


def around_x(values, step):
    return lax.ppermute(values, "px", [(i, i // 4 * 4 + (i + step) % 4) for i in range(16)])


def along(values, axis, step):
    count = lax.axis_size(axis)
    return lax.ppermute(values, axis, [(i, (i + step) % count) for i in range(count)])


def selection(neighbours):
    rows, columns, degree = neighbours.shape

    def body(codes_ref, picks_ref):
        codes = codes_ref[...]
        q = codes + (codes >= 4).astype(jnp.int32)
        down = (q >= 3).astype(jnp.int32) + (q >= 6).astype(jnp.int32)
        step = q - 3 * down
        from_row = lax.broadcasted_iota(jnp.int32, codes.shape, 1) + down - 1
        column = lax.broadcasted_iota(jnp.int32, codes.shape, 2)
        near = ((column & (BAND - 1)) + step) * rows + from_row
        sender = jnp.where(from_row < 0, ABOVE + column + step, jnp.where(from_row >= rows, BELOW + column + step, near))
        lanes = lax.broadcasted_iota(jnp.int32, (rows, 256), 1)
        row = lax.broadcasted_iota(jnp.int32, (rows, 256), 0)
        for c in range(columns):
            receiver = lanes == (BAND + 2 + c % BAND) * rows + row
            for k in range(degree):
                picks = (lanes == sender[k, :, c : c + 1]) | receiver
                picks_ref[(c * degree + k) * rows : (c * degree + k + 1) * rows, :] = picks.astype(jnp.bfloat16)

    held = pl.BlockSpec(memory_space=pltpu.VMEM)
    return pl.pallas_call(
        body,
        name="selection",
        out_shape=jax.ShapeDtypeStruct((rows * columns * degree, 256), jnp.bfloat16),
        in_specs=[held],
        out_specs=held,
        compiler_params=pltpu.CompilerParams(vmem_limit_bytes=4 * MIB),
    )(neighbours.transpose(2, 0, 1))


def dot(a, b):
    return jnp.dot(a, b, preferred_element_type=jnp.float32)


def finish(before, inner_sum, outer, gains):
    hidden = jax.nn.silu(inner_sum).astype(jnp.bfloat16)
    output = dot(hidden, outer)
    center = output - jnp.mean(output, axis=-1, keepdims=True)
    spread_of = jnp.mean(center * center, axis=-1, keepdims=True)
    scaled = center * lax.rsqrt(spread_of + EPSILON) * gains
    return (before.astype(jnp.float32) + scaled).astype(jnp.bfloat16)


def fine_layer(layer, fine, picks, latents, left, right, sides, inner, outer, gain, rows):
    edges, features = fine.shape
    nodes = latents.shape[0]
    hidden = inner.shape[2]
    near = (BAND + 2) * rows
    own = BAND * rows
    steps = nodes // own
    block = edges // steps
    degree = edges // nodes

    def body(fine_ref, picks_ref, latents_ref, left_ref, right_ref, sides_ref, inner_ref, outer_ref, gain_ref,
             next_ref, sum_ref, send_ref, recv_ref, table_ref):
        step = pl.program_id(0)

        @pl.when(step == 0)
        def _():
            send = inner_ref[layer, features : 2 * features, :]
            project = lambda ref: dot(ref[...], send).astype(jnp.bfloat16)
            table_ref[ABOVE : ABOVE + sides.shape[0], :] = project(sides_ref)
            table_ref[ABOVE + sides.shape[0] :, :] = jnp.zeros((256 - ABOVE - sides.shape[0], hidden), jnp.bfloat16)
            send_ref[rows : rows + nodes, :] = project(latents_ref)
            recv_ref[...] = dot(latents_ref[...], inner_ref[layer, 2 * features :, :]).astype(jnp.bfloat16)
            send_ref[:rows, :] = project(left_ref)
            send_ref[rows + nodes :, :] = project(right_ref)

        start = pl.multiple_of(step * own, own)
        table_ref[:near, :] = send_ref[pl.ds(start, near), :]
        table_ref[near : near + own, :] = recv_ref[pl.ds(start, own), :]
        before = fine_ref[...]
        total = dot(before, inner_ref[layer, :features, :]) + dot(picks_ref[...], table_ref[...])
        after = finish(before, total, outer_ref[layer], gain_ref[layer : layer + 1, :])
        next_ref[...] = after
        split = after.astype(jnp.float32).reshape(BAND, degree, rows, features)
        sum_ref[...] = jnp.sum(split, axis=1).reshape(own, features)

    held = pl.BlockSpec(memory_space=pltpu.VMEM)
    return pl.pallas_call(
        body,
        name=f"fine{layer}",
        out_shape=(
            jax.ShapeDtypeStruct(fine.shape, jnp.bfloat16),
            jax.ShapeDtypeStruct((nodes, features), jnp.float32),
        ),
        grid=(steps,),
        in_specs=[
            pl.BlockSpec((block, features), lambda i: (i, 0)),
            pl.BlockSpec((block, 256), lambda i: (i, 0)),
        ]
        + [held] * 7,
        out_specs=(
            pl.BlockSpec((block, features), lambda i: (i, 0)),
            pl.BlockSpec((own, features), lambda i: (i, 0)),
        ),
        scratch_shapes=[
            pltpu.VMEM((nodes + 2 * rows, hidden), jnp.bfloat16),
            pltpu.VMEM((nodes, hidden), jnp.bfloat16),
            pltpu.VMEM((256, hidden), jnp.bfloat16),
        ],
        compiler_params=pltpu.CompilerParams(dimension_semantics=("arbitrary",), vmem_limit_bytes=14 * MIB),
    )(fine, picks, latents, left, right, sides, inner, outer, gain)


def pick(index, width):
    lanes = lax.broadcasted_iota(jnp.int32, (index.shape[0], width), 1)
    return (lanes == index).astype(jnp.bfloat16)


def rows_to_columns(left, right):
    return lax.dot_general(left, right, (((1,), (1,)), ((), ())), preferred_element_type=jnp.float32)


def decode(tags, at):
    numbers = tags.astype(jnp.int32)
    return jnp.where(numbers[:, 4:5] > 0, numbers[:, at : at + 1] * LOW + numbers[:, at + 1 : at + 2], -1)


def send_rows(both, own_ref, last_ref, first_ref):
    rows = both.astype(jnp.bfloat16)
    count, columns = own_ref.shape[0], last_ref.shape[0]
    own_ref[...] = rows[:count]
    last_ref[...] = rows[count : count + columns]
    first_ref[...] = rows[count + columns :]


def join_far(own, fars, left, right, last, first):
    count, features = own.shape
    rows = left.shape[0]
    four = 4 * count
    columns = last.shape[0]

    def body(own_ref, far1_ref, far2_ref, far3_ref, left_ref, right_ref, last_ref, first_ref, two_ref, up_ref, down_ref):
        for at, ref in enumerate((own_ref, far1_ref, far2_ref, far3_ref)):
            two_ref[at * count : (at + 1) * count, :] = ref[...]
        for out_ref, line_ref, row in ((up_ref, last_ref, rows - 1), (down_ref, first_ref, 0)):
            out_ref[:four, :] = two_ref[...]
            out_ref[four:, :] = jnp.zeros((out_ref.shape[0] - four, features), jnp.bfloat16)
            out_ref[four : four + 1, :] = left_ref[row : row + 1, :]
            out_ref[four + 1 : four + 1 + columns, :] = line_ref[...]
            out_ref[four + 1 + columns : four + 2 + columns, :] = right_ref[row : row + 1, :]

    held = pl.BlockSpec(memory_space=pltpu.VMEM)
    return pl.pallas_call(
        body,
        name="join_far",
        out_shape=tuple(jax.ShapeDtypeStruct((n, features), jnp.bfloat16) for n in (four, four + 32, four + 32)),
        in_specs=[held] * 8,
        out_specs=(held,) * 3,
        compiler_params=pltpu.CompilerParams(vmem_limit_bytes=2 * MIB),
    )(own, *fars, left, right, last, first)


def in_hbm(values):
    return pltpu.with_memory_space_constraint(values, pltpu.HBM)


def fetch(pairs, sems):
    copies = [pltpu.make_async_copy(here, there, sems.at[i]) for i, (here, there) in enumerate(pairs)]
    for copy in copies:
        copy.start()
    for copy in copies:
        copy.wait()


def join_near(layer, own, up, two, down):
    each, features = own.shape
    side = BELOW - ABOVE

    far = layer == 0

    def body(own_ref, two_ref, up_ref, down_ref, joined_ref, sides_ref, sems, *near):
        to, beside = near or (joined_ref, sides_ref)
        part = lambda at: to.at[pl.ds(at * each, each), :]
        fetch(
            [
                (own_ref, part(0)),
                (up_ref.at[pl.ds(0, each), :], part(1)),
                (two_ref, part(2)),
                (down_ref.at[pl.ds(0, each), :], part(3)),
                (up_ref.at[pl.ds(each, side), :], beside.at[pl.ds(0, side), :]),
                (down_ref.at[pl.ds(each, side), :], beside.at[pl.ds(side, side), :]),
            ],
            sems,
        )
        if near:
            fetch([(to, joined_ref), (beside, sides_ref)], sems)

    away = pl.BlockSpec(memory_space=pl.ANY)
    place = pltpu.HBM if far else jax.ShapeDtypeStruct
    shapes = ((4 * each, features), (2 * side, features))
    operands = (own, two, up, down)
    return pl.pallas_call(
        body,
        name="join_near",
        cost_estimate=pl.CostEstimate(flops=3_000_000_000, bytes_accessed=0, transcendentals=0),
        out_shape=tuple(place(shape, jnp.bfloat16) for shape in shapes),
        in_specs=[away] * 4,
        out_specs=(away,) * 2,
        scratch_shapes=[pltpu.SemaphoreType.DMA((6,))]
        + [pltpu.VMEM(shape, jnp.bfloat16) for shape in shapes if far],
        compiler_params=pltpu.CompilerParams(vmem_limit_bytes=2 * MIB),
    )(*(map(in_hbm, operands) if far else operands))


def coarse_start(coarse_slots, latents, staged, rows, columns):
    count = coarse_slots.shape[1]
    nodes, features = latents.shape
    size = count + 2 * columns

    def body(slots_away, latents_away, *refs):
        away_refs, refs = refs[: len(staged)], refs[len(staged) :]
        own_ref, last_ref, first_ref, left_ref, right_ref, choose_ref, *refs = refs
        here_refs, (slots_ref, latents_ref, sems, later) = refs[: len(staged)], refs[len(staged) :]
        copies = [
            pltpu.make_async_copy(away, here, later.at[i])
            for i, (away, here) in enumerate(zip(away_refs, here_refs, strict=True))
        ]
        fetch([(slots_away, slots_ref), (latents_away, latents_ref)], sems)
        for copy in copies:
            copy.start()
        slot = slots_ref[...]
        row = jnp.floor((slot.astype(jnp.float32) + 0.5) * (1.0 / columns)).astype(jnp.int32)
        at = (slot - row * columns) * rows + row
        place = (lax.broadcasted_iota(jnp.int32, (nodes, count), 0) == at).astype(jnp.bfloat16)
        out = lax.broadcasted_iota(jnp.int32, (size, count), 0)
        same = (out == lax.broadcasted_iota(jnp.int32, (size, count), 1)).astype(jnp.bfloat16)
        out = lax.broadcasted_iota(jnp.int32, (size, nodes), 0)
        node = lax.broadcasted_iota(jnp.int32, (size, nodes), 1)
        edge = ((out >= count) & (out < count + columns) & (node == (out - count) * rows + rows - 1)) | (
            (out >= count + columns) & (node == (out - count - columns) * rows)
        )
        choose = (rows_to_columns(same, place) + edge.astype(jnp.float32)).astype(jnp.bfloat16)
        choose_ref[...] = choose
        send_rows(dot(choose, latents_ref[...]), own_ref, last_ref, first_ref)
        left_ref[...] = latents_ref[:rows, :]
        right_ref[...] = latents_ref[-rows:, :]
        for copy in copies:
            copy.wait()

    shapes = (
        *(jax.ShapeDtypeStruct((n, features), jnp.bfloat16) for n in (count, columns, columns, rows, rows)),
        jax.ShapeDtypeStruct((size, nodes), jnp.bfloat16),
        *(jax.ShapeDtypeStruct(a.shape, a.dtype) for a in staged),
    )
    away = pl.BlockSpec(memory_space=pltpu.HBM)
    held = pl.BlockSpec(memory_space=pltpu.VMEM)
    return pl.pallas_call(
        body,
        name="coarse_start",
        out_shape=shapes,
        in_specs=[away] * (2 + len(staged)),
        out_specs=(held,) * len(shapes),
        scratch_shapes=[
            pltpu.VMEM(coarse_slots.shape, jnp.int32),
            pltpu.VMEM(latents.shape, jnp.bfloat16),
            pltpu.SemaphoreType.DMA((2,)),
            pltpu.SemaphoreType.DMA((len(staged),)),
        ],
        compiler_params=pltpu.CompilerParams(vmem_limit_bytes=4 * MIB),
    )(*map(in_hbm, (coarse_slots, latents, *staged)))


def pack_edges(long_edges, senders, receivers, me, coarse_count, devices):
    count, features = long_edges.shape
    blocks = features // TAGS
    slots = devices * CAP

    def body(me_ref, long_ref, send_ref, recv_ref, sent_ref, mine_ref, wide):
        send, recv = send_ref[...], recv_ref[...]
        _, owner = table_row(0, 0, recv, coarse_count)
        here = (lax.shift_right_logical(me_ref[0], 3), me_ref[0] & 7)
        there = (lax.shift_right_logical(owner, 3), owner & 7)
        field = lax.broadcasted_iota(jnp.int32, (TAGS, count), 0)

        def fields(digits):
            sender = table_row(*digits, send, coarse_count)[0]
            receiver = table_row(*digits, recv, coarse_count)[0]
            both = jnp.where(field < 2, sender, receiver)
            high = lax.shift_right_logical(both, LOW.bit_length() - 1)
            value = jnp.where(field % 2 == 0, high, both & (LOW - 1))
            value = jnp.where(field == 4, 1, jnp.where(field == 5, owner, value))
            return jnp.where(field < 6, value, 0).astype(jnp.float32).astype(jnp.bfloat16)

        down = lax.broadcasted_iota(jnp.int32, (count, count), 0)
        across = lax.broadcasted_iota(jnp.int32, (count, count), 1)
        mine = rows_to_columns((down == across).astype(jnp.bfloat16), fields(here))
        mine_ref[...] = mine.astype(jnp.bfloat16)
        same = (mine[:, 5:6].astype(jnp.int32) == owner) & (down < across)
        rank = jnp.sum(same.astype(jnp.float32), axis=0, keepdims=True).astype(jnp.int32)
        spot = rank * devices + owner
        place = (lax.broadcasted_iota(jnp.int32, (slots, count), 0) == spot).astype(jnp.bfloat16)
        edges = dot(place, long_ref[...])
        tags = rows_to_columns(place, fields(there))
        for j in range(CAP):
            part = slice(j * devices, (j + 1) * devices)
            for b in range(blocks):
                wide[pl.ds(j * blocks + b, devices, stride=16), :] = edges[part, b * TAGS : (b + 1) * TAGS]
            wide[pl.ds(CAP * blocks + j, devices, stride=16), :] = tags[part]
        wide[pl.ds(15, devices, stride=16), :] = jnp.zeros((devices, TAGS), jnp.float32)
        sent_ref[...] = wide[...].astype(jnp.bfloat16)

    shapes = (
        jax.ShapeDtypeStruct((devices * 16, TAGS), jnp.bfloat16),
        jax.ShapeDtypeStruct((count, TAGS), jnp.bfloat16),
    )
    return pl.pallas_call(
        body,
        name="pack_edges",
        out_shape=shapes,
        cost_estimate=pl.CostEstimate(flops=12_000_000_000, bytes_accessed=0, transcendentals=0),
        in_specs=[pl.BlockSpec(memory_space=pltpu.SMEM)] + [pl.BlockSpec(memory_space=pltpu.VMEM)] * 3,
        out_specs=(pl.BlockSpec(memory_space=pltpu.VMEM),) * 2,
        scratch_shapes=[
            pltpu.VMEM((devices * 16, TAGS), jnp.float32),
        ],
        compiler_params=pltpu.CompilerParams(vmem_limit_bytes=8 * MIB),
    )(me, long_edges, senders, receivers)


def unpack_edges(arrived, choose, features, table_rows, coarse_count):
    devices = arrived.shape[0] // 16
    blocks = features // TAGS
    slots = devices * CAP
    nodes = choose.shape[1]

    def body(arrived_ref, choose_ref, rows_ref, send_ref, recv_ref, adds_ref, wide):
        wide[...] = arrived_ref[...].astype(jnp.float32)
        for j in range(CAP):
            part = slice(j * devices, (j + 1) * devices)
            for b in range(blocks):
                lanes = slice(b * TAGS, (b + 1) * TAGS)
                rows_ref[part, lanes] = wide[pl.ds(j * blocks + b, devices, stride=16), :].astype(jnp.bfloat16)
            tags = wide[pl.ds(CAP * blocks + j, devices, stride=16), :]
            send_ref[part, :] = pick(decode(tags, 0), table_rows)
            recv_ref[part, :] = pick(decode(tags, 2), TAGS)
        here = recv_ref[:, :coarse_count]
        place = lax.dot_general(
            choose_ref[:coarse_count, :], here, (((0,), (1,)), ((), ())), preferred_element_type=jnp.float32
        )
        adds_ref[...] = place.astype(jnp.bfloat16)

    held = pl.BlockSpec(memory_space=pltpu.VMEM)
    return pl.pallas_call(
        body,
        name="unpack_edges",
        out_shape=(
            jax.ShapeDtypeStruct((slots, features), jnp.bfloat16),
            jax.ShapeDtypeStruct((slots, table_rows), jnp.bfloat16),
            jax.ShapeDtypeStruct((slots, TAGS), jnp.bfloat16),
            jax.ShapeDtypeStruct((nodes, slots), jnp.bfloat16),
        ),
        in_specs=[held] * 2,
        out_specs=(held,) * 4,
        scratch_shapes=[pltpu.VMEM(arrived.shape, jnp.float32)],
        compiler_params=pltpu.CompilerParams(vmem_limit_bytes=8 * MIB),
    )(arrived, choose)


def long_step(before, sent, got, inner_ref, outer_ref, gain_ref, layer):
    features = before.shape[1]
    total = dot(before, inner_ref[layer, :features, :])
    total += dot(sent, inner_ref[layer, features : 2 * features, :])
    total += dot(got, inner_ref[layer, 2 * features :, :])
    return finish(before, total, outer_ref[layer], gain_ref[layer : layer + 1, :])


def coarse_layer(layer, long_rows, own_rows, sends, recvs, adds, choose, pieces, latents, fine_sum,
                 edge_inner, edge_outer, edge_gain, node_inner, node_outer, node_gain, coarse_count, last):
    slots = long_rows.shape[0]
    nodes, features = latents.shape
    count = len(pieces)
    each = pieces[0].shape[0]
    table_rows = count * each
    both = slots + own_rows.shape[0]

    def body(long_ref, own_ref, sends_ref, recvs_ref, adds_ref, choose_ref, latents_ref, sum_ref,
             ei_ref, eo_ref, eg_ref, ni_ref, no_ref, ng_ref, *rest):
        piece_refs = rest[:count]
        next_ref, *outs, ni, no, sems = rest[count:]
        table = outs[1] if last else outs[4]
        weights = [
            pltpu.make_async_copy(ni_ref.at[layer], ni, sems.at[0]),
            pltpu.make_async_copy(no_ref.at[layer], no, sems.at[1]),
        ]
        for copy in weights:
            copy.start()
        for p in range(count):
            table[p * each : (p + 1) * each, :] = piece_refs[p][...]
        got = dot(recvs_ref[...], table[:TAGS, :]).astype(jnp.bfloat16)
        if last:
            picked = dot(sends_ref[...], table[...]).astype(jnp.bfloat16)
            before = jnp.concatenate([long_ref[...], own_ref[...]], axis=0)
            got = jnp.concatenate([got, picked[both:]], axis=0)
            after = long_step(before, picked[:both], got, ei_ref, eo_ref, eg_ref, layer)
            outs[0][...] = after[slots:]
            after = after[:slots]
        else:
            sent = dot(sends_ref[...], table[...]).astype(jnp.bfloat16)
            after = long_step(long_ref[...], sent, got, ei_ref, eo_ref, eg_ref, layer)
            outs[0][...] = after
        incoming = (sum_ref[...] + dot(adds_ref[...], after)).astype(jnp.bfloat16)
        old = latents_ref[...]
        for copy in weights:
            copy.wait()
        total = dot(old, ni[:features, :]) + dot(incoming, ni[features:, :])
        new = finish(old, total, no[...], ng_ref[layer : layer + 1, :])
        next_ref[...] = new
        if not last:
            send_rows(dot(choose_ref[...], new), *outs[1:4])
            outs[5][...] = new[:rows]
            outs[6][...] = new[-rows:]

    held = pl.BlockSpec(memory_space=pltpu.VMEM)
    away = pl.BlockSpec(memory_space=pltpu.HBM)
    table_shape = (table_rows, features)
    side = (choose.shape[0] - coarse_count) // 2
    rows = nodes // side
    kept = (both - slots,) if last else (slots, coarse_count, side, side, table_rows, rows, rows)
    shapes = [jax.ShapeDtypeStruct((n, features), jnp.bfloat16) for n in (nodes, *kept)]

    return pl.pallas_call(
        body,
        name=f"coarse{layer}",
        out_shape=tuple(shapes),
        in_specs=[held] * 11 + [away] * 2 + [held] * (1 + count),
        out_specs=(held,) * len(shapes),
        scratch_shapes=([pltpu.VMEM(table_shape, jnp.bfloat16)] if last else [])
        + [
            pltpu.VMEM(node_inner.shape[1:], jnp.bfloat16),
            pltpu.VMEM(node_outer.shape[1:], jnp.bfloat16),
            pltpu.SemaphoreType.DMA((2,)),
        ],
        compiler_params=pltpu.CompilerParams(vmem_limit_bytes=(18 if last else 14) * MIB),
    )(long_rows, own_rows, sends, recvs, adds, choose, latents, fine_sum,
      edge_inner, edge_outer, edge_gain, node_inner, node_outer, node_gain, *pieces)


def own_layer(layer, long_rows, tags, sends, table, edge_inner, edge_outer, edge_gain):
    count = long_rows.shape[0]
    slots, rows = sends.shape

    def body(long_ref, tags_ref, sends_ref, table_ref, ei_ref, eo_ref, eg_ref, next_ref, all_ref):
        mine = tags_ref[...].astype(jnp.float32)
        all_ref[:slots, :] = sends_ref[...]
        all_ref[slots : slots + count, :] = pick(decode(mine, 0), rows)
        all_ref[slots + count :, :] = pick(decode(mine, 2), rows)
        picked = dot(all_ref[slots:, :], table_ref[...]).astype(jnp.bfloat16)
        next_ref[...] = long_step(long_ref[...], picked[:count], picked[count:], ei_ref, eo_ref, eg_ref, layer)

    held = pl.BlockSpec(memory_space=pltpu.VMEM)
    return pl.pallas_call(
        body,
        name=f"own{layer}",
        out_shape=(
            jax.ShapeDtypeStruct(long_rows.shape, jnp.bfloat16),
            jax.ShapeDtypeStruct((slots + 2 * count, rows), jnp.bfloat16),
        ),
        in_specs=[held] * 7,
        out_specs=(held, held),
        compiler_params=pltpu.CompilerParams(vmem_limit_bytes=8 * MIB),
    )(long_rows, tags, sends, table, edge_inner, edge_outer, edge_gain)


def shards(
    node_latents,
    fine_edges,
    long_edges,
    neighbours,
    coarse_slots,
    long_senders,
    long_receivers,
    edge_inner,
    edge_outer,
    edge_gain,
    node_inner,
    node_outer,
    node_gain,
):
    rows, columns, features = node_latents.shape
    degree = fine_edges.shape[2]
    nodes = rows * columns
    coarse_count = coarse_slots.shape[0]
    layers = edge_inner.shape[0]
    devices = lax.axis_size("px") * lax.axis_size("py")

    latents = node_latents.transpose(1, 0, 2).reshape(nodes, features)
    fine = fine_edges.transpose(1, 2, 0, 3).reshape(nodes * degree, features)
    staged = (long_edges, long_senders[None, :], long_receivers[None, :])
    own, last_row, first_row, to_left, to_right, choose, *staged = coarse_start(
        coarse_slots[None, :], latents, staged, rows, columns
    )
    own_rows = long_edges
    me = lax.axis_index(AXES).reshape(1)
    payload, own_tags = pack_edges(*staged, me, coarse_count, devices)
    for layer in range(layers):
        last = layer == layers - 1
        fars = [along(own, "px", 4 * s) for s in (1, 2, 3)]
        left = along(to_right, "py", 1)
        right = along(to_left, "py", -1)
        if layer == 0:
            *fars, left, right, payload = tie(*fars, left, right, payload)
        joined, up, down = join_far(own, fars, left, right, last_row, first_row)
        if layer == 0:
            packed = payload.reshape(devices, 16, TAGS)
            arrived = lax.all_to_all(packed, AXES, split_axis=0, concat_axis=0, tiled=True).reshape(payload.shape)
        two = around_x(joined, 2)
        up = along(up, "px", 1)
        down = along(down, "px", -1)
        joined, sides = join_near(layer, joined, up, two, down)
        joined, sides, own_rows = tie(joined, sides, own_rows)
        pieces = [joined] + [shift(joined, Z, s) for s in (1, 2, 3)]
        if layer == 0:
            table_rows = 2 * len(pieces) * joined.shape[0]
            long_rows, sends, recvs, adds = unpack_edges(arrived, choose, features, table_rows, coarse_count)
            left, long_rows, neighbours = tie(left, long_rows, neighbours)
            picks = selection(neighbours)
        else:
            own_rows, sends = own_layer(layer - 1, own_rows, own_tags, sends, table, edge_inner, edge_outer, edge_gain)
        fine, fine_sum = fine_layer(
            layer, fine, picks, latents, left, right, sides, edge_inner, edge_outer, edge_gain, rows
        )
        swapped = shift(joined, CORE, 1)
        *others, fine_sum, own_rows, long_rows = tie(*pieces[1:], fine_sum, own_rows, long_rows)
        pieces = [joined] + others + [swapped] + [shift(piece, CORE, 1) for piece in others]
        latents, *rest = coarse_layer(
            layer, long_rows, own_rows, sends, recvs, adds, choose, pieces, latents, fine_sum,
            edge_inner, edge_outer, edge_gain, node_inner, node_outer, node_gain, coarse_count, last,
        )
        if last:
            own_rows = rest[0]
        else:
            long_rows, own, last_row, first_row, table, to_left, to_right = rest
    return (
        latents.reshape(columns, rows, features).transpose(1, 0, 2),
        fine.reshape(columns, degree, rows, features).transpose(2, 0, 1, 3),
        own_rows,
    )


def solution(mesh):
    in_specs = (
        P("px", "py", None),
        P("px", "py", None, None),
        P(AXES, None),
        P("px", "py", None),
        P(AXES),
        P(AXES),
        P(AXES),
        P(),
        P(),
        P(),
        P(),
        P(),
        P(),
    )
    out_specs = (P("px", "py", None), P("px", "py", None, None), P(AXES, None))
    return jax.shard_map(shards, mesh=mesh, in_specs=in_specs, out_specs=out_specs, check_vma=False)
```
